256 devices in a mesh: space: 32 (over z, x), sample: 8 (over y, core).
Axes of the slice: x: 4, y: 4, z: 8, core: 2. Of those that a mesh axis runs over, the one named last changes fastest.
Arguments:
- crops: bfloat16 [256, 16, 64, 1024], P('sample', None, 'space'), may hold values from -6 to 6
- first_kernel: bfloat16 [32, 16, 3, 3, 3], replicated, may hold values from -0.3125 to 0.3125
- second_kernel: bfloat16 [64, 32, 3, 3, 3], replicated, may hold values from -0.21875 to 0.21875
- out_grad: bfloat16 [256, 64, 16, 64], P(('sample', 'space')), may hold values from -0.03125 to 0.03125
Outputs:
- features_out: bfloat16 [256, 64, 16, 64], P(('sample', 'space'))
- first_grad: float32 [32, 16, 3, 3, 3], replicated
- second_grad: float32 [64, 32, 3, 3, 3], replicated
The draws below stay inside these ranges and needn't reach their ends.
All inputs are finite; a program needn't handle non-finite values.
Results may differ from the reference program's by a relative error of at most 0.012.
Values may be sent and summed in bfloat16 or wider, within the bound.
A program may use at most 128 MiB of HBM per device.

```python
import jax
import jax.numpy as jnp
from jax import lax

C0 = 16
C1 = 32
C2 = 64
HEIGHT = 8
WIDTH = 128
SAMPLES = 256
DEPTH = 64


def level_of(stream_key, extent, shards, smallest, largest):
    def one(dim, blocks):
        steps = jax.random.uniform(jax.random.fold_in(jax.random.fold_in(stream_key, 6), dim), (blocks,), jnp.float32, smallest / len(shards), largest / len(shards))
        return jnp.repeat(jnp.exp(steps), extent[dim] // blocks).reshape((-1,) + (1,) * (len(extent) - dim - 1))

    level = one(*shards[0])
    for cut in shards[1:]:
        level = level * one(*cut)
    return level


def scatter_about(key, shape, deviation, reach, pieces=(), kind=jnp.bfloat16):
    drawn = jax.random.normal(key, shape, jnp.float32) * deviation
    if len(pieces) > 0:
        drawn = level_of(key, shape, pieces, -0.22, 0.18) * drawn
    return jnp.clip(drawn, min=-reach, max=reach).astype(kind)


def setup_inputs(seed: int = 0) -> dict:
    splits = jax.random.split(jax.random.key(seed), 5)
    return {
        "crops": scatter_about(splits[0], (SAMPLES, C0, DEPTH, HEIGHT * WIDTH), 1.0, 6.0, ((0, 8), (2, 32))),
        "first_kernel": scatter_about(splits[1], (C1, C0, 3, 3, 3), (C0 * 27) ** -0.5, 0.3125),
        "second_kernel": scatter_about(splits[2], (C2, C1, 3, 3, 3), (C1 * 27) ** -0.5, 0.21875),
        "out_grad": scatter_about(splits[3], (SAMPLES, C2, DEPTH // 4, HEIGHT * WIDTH // 16), ((SAMPLES * (DEPTH // 4) * (HEIGHT * WIDTH // 16)) ** -0.5), 0.03125, ((0, 256),)),
    }


def strided_conv(field, kernel):
    return lax.conv_general_dilated(field, kernel, (2, 2, 2), ((1, 0), (1, 0), (1, 0)), dimension_numbers=('NCDHW', 'OIDHW', 'NCDHW'), precision=lax.Precision.HIGHEST)

def silu_slope(value):
    sigma = jax.nn.sigmoid(value)
    return sigma * (1.0 + value * (1.0 - sigma))

def reference(crops, first_kernel, second_kernel, out_grad):
    kernel_one = first_kernel.astype(jnp.float32)
    kernel_two = second_kernel.astype(jnp.float32)

    def one_sample(carry, pair):
        sample, cotangent = pair
        field = sample.astype(jnp.float32).reshape(1, C0, DEPTH, HEIGHT, WIDTH)
        first_pre = strided_conv(field, kernel_one)
        first_act = lax.optimization_barrier(jax.nn.silu(first_pre).astype(jnp.bfloat16)).astype(jnp.float32)
        output, pullback = jax.vjp(strided_conv, first_act, kernel_two)
        grad_field = cotangent.astype(jnp.float32).reshape(1, C2, DEPTH // 4, HEIGHT // 4, WIDTH // 4)
        act_grad, kernel_two_grad = pullback(grad_field)
        act_grad = lax.optimization_barrier(act_grad.astype(jnp.bfloat16)).astype(jnp.float32)
        pre_grad = lax.optimization_barrier((act_grad * silu_slope(first_pre)).astype(jnp.bfloat16)).astype(jnp.float32)
        unused, pull_first = jax.vjp(lambda kernel: strided_conv(field, kernel), kernel_one)
        kernel_one_grad = pull_first(pre_grad)[0]
        result = output.astype(jnp.bfloat16).reshape(C2, DEPTH // 4, HEIGHT * WIDTH // 16)
        return ((carry[0] + kernel_one_grad, carry[1] + kernel_two_grad), result)
    start = (jnp.zeros((C1, C0, 3, 3, 3), jnp.float32), jnp.zeros((C2, C1, 3, 3, 3), jnp.float32))
    totals, features_out = lax.scan(one_sample, start, (crops, out_grad))
    return (features_out, totals[0], totals[1])
```

```python
import jax
import jax.numpy as jnp
from jax import lax
from jax.sharding import PartitionSpec as P

HEIGHT = 8
WIDTH = 128


def forward_conv(field, kernel, depth_pad):
    return lax.conv_general_dilated(
        field,
        kernel,
        (2, 2, 2),
        (depth_pad, (1, 0), (1, 0)),
        dimension_numbers=("NCDHW", "OIDHW", "NCDHW"),
        preferred_element_type=jnp.float32,
    )


def kernel_grad(field, cotangent, depth_pad):
    return lax.conv_general_dilated(
        field,
        cotangent,
        (1, 1, 1),
        (depth_pad, (1, 0), (1, 0)),
        rhs_dilation=(2, 2, 2),
        dimension_numbers=("CNDHW", "IODHW", "CNDHW"),
        preferred_element_type=jnp.float32,
    )


def input_grad(cotangent, kernel):
    flipped = kernel[:, :, ::-1, ::-1, ::-1]
    return lax.conv_general_dilated(
        cotangent,
        flipped,
        (1, 1, 1),
        ((1, 2), (1, 2), (1, 2)),
        lhs_dilation=(2, 2, 2),
        dimension_numbers=("NCDHW", "IODHW", "NCDHW"),
        preferred_element_type=jnp.float32,
    )


def silu_slope(value):
    sigma = jax.nn.sigmoid(value)
    return sigma * (1.0 + value * (1.0 - sigma))


def body(crops, first_kernel, second_kernel, out_grad):
    local_samples, channels_in, planes, flat_cells = crops.shape
    whole_input = lax.all_to_all(crops, "space", split_axis=0, concat_axis=2, tiled=True)
    whole_input = whole_input.reshape(
        whole_input.shape[0], channels_in, whole_input.shape[2], HEIGHT, WIDTH
    )
    first_pre = forward_conv(whole_input, first_kernel, (1, 0))
    act_whole = jax.nn.silu(first_pre).astype(jnp.bfloat16)
    sample_count = act_whole.shape[0]
    second_pre = forward_conv(act_whole, second_kernel, (1, 0))
    features_out = second_pre.astype(jnp.bfloat16).reshape(out_grad.shape)
    cotangent = out_grad.reshape(
        sample_count, out_grad.shape[1], out_grad.shape[2], HEIGHT // 4, WIDTH // 4
    )
    second_grad = kernel_grad(act_whole, cotangent, (1, 0))
    act_grad = input_grad(cotangent, second_kernel).astype(jnp.bfloat16)
    pre_grad = (act_grad.astype(jnp.float32) * silu_slope(first_pre)).astype(jnp.bfloat16)
    first_grad = kernel_grad(whole_input, pre_grad, (1, 0))
    flat = jnp.concatenate([first_grad.reshape(-1), second_grad.reshape(-1)])
    flat = lax.psum(flat, ("space", "sample"))
    first_grad = flat[: first_grad.size].reshape(first_grad.shape)
    second_grad = flat[first_grad.size :].reshape(second_grad.shape)
    return (features_out, first_grad, second_grad)


def solution(mesh):
    placed = (P("sample", None, "space", None), P(), P(), P(("sample", "space"), None, None, None))
    return jax.shard_map(
        body,
        mesh=mesh,
        in_specs=placed,
        out_specs=(P(("sample", "space"), None, None, None), P(), P()),
        check_vma=False,
    )
```

```python
import numpy as np

import jax
import jax.numpy as jnp
from jax import lax
from jax.experimental import pallas as pl
from jax.experimental.pallas import tpu as pltpu
from jax.sharding import PartitionSpec as P

HEIGHT = 8
WIDTH = 128

NT = (((1,), (1,)), ((), ()))


def selection_tables(c0_w, c1_h, c1_w):
    t1 = np.zeros((c0_w, 3 * 128), np.float32)
    for c in range(3):
        for pw in range(c0_w // 2):
            w = 2 * pw + c - 1
            if 0 <= w < c0_w:
                t1[w, c * 128 + pw] = 1.0
    q_h, q_w = c1_h // 2, c1_w // 2
    sel2 = np.zeros((c1_h * c1_w, 9 * 128), np.float32)
    up = np.zeros((q_h * q_w, 9 * c1_h * c1_w), np.float32)
    for b in range(3):
        for c in range(3):
            bc = b * 3 + c
            for qh in range(q_h):
                for qw in range(q_w):
                    h2, w2 = 2 * qh + b - 1, 2 * qw + c - 1
                    if 0 <= h2 < c1_h and 0 <= w2 < c1_w:
                        sel2[h2 * c1_w + w2, bc * 128 + qh * q_w + qw] = 1.0
                        up[qh * q_w + qw, bc * c1_h * c1_w + h2 * c1_w + w2] = 1.0
    return t1, sel2, up


def conv_kernel(x_ref, ogn_ref, ogq_ref, w1_ref, w2_ref, w2t_ref, t1_ref, sel2_ref, up_ref,
                feat_ref, fg_ref, sg_ref,
                q1_ref, s_ref, fp_ref, a2_ref, q2_ref, s2_ref, v_ref):
    depth, c0, cells = x_ref.shape
    n_h = cells // 128
    c1 = w1_ref.shape[0]
    c2 = w2_ref.shape[0]
    planes1 = depth // 2
    plane1 = s_ref.shape[2]
    planes2 = planes1 // 2
    plane2 = ogq_ref.shape[1]

    q1_ref[0] = jnp.zeros(q1_ref.shape[1:], q1_ref.dtype)
    for h in range(n_h):
        xh = x_ref[:, :, h * 128:(h + 1) * 128].reshape(depth * c0, 128)
        qh = jnp.dot(xh, t1_ref[...], preferred_element_type=jnp.float32)
        q1_ref[pl.ds(1, depth), :, h * 384:(h + 1) * 384] = qh.astype(q1_ref.dtype).reshape(depth, c0, 384)

    a2_ref[0] = jnp.zeros(a2_ref.shape[1:], a2_ref.dtype)

    def build_plane(pd, carry):
        for a in range(3):
            for b in range(3):
                for c in range(3):
                    r0 = ((a * 3 + b) * 3 + c) * c0
                    for m in range(plane1 // 128):
                        h_lo, h_hi = 4 * m + b - 1, 4 * m + b + 1
                        hi = q1_ref[2 * pd + a, :, pl.ds((h_hi * 3 + c) * 128, 128)].astype(jnp.float32)
                        val = pltpu.roll(hi, 64, 1)
                        if h_lo >= 0:
                            val = val + q1_ref[2 * pd + a, :, pl.ds((h_lo * 3 + c) * 128, 128)].astype(jnp.float32)
                        s_ref[pd, pl.ds(r0, c0), pl.ds(m * 128, 128)] = val.astype(s_ref.dtype)
        pre = jnp.dot(w1_ref[...], s_ref[pd], preferred_element_type=jnp.float32)
        fp_ref[pd] = pre
        sig = 1.0 / (1.0 + jnp.exp(-pre))
        a2_ref[pd + 1] = (pre * sig).astype(a2_ref.dtype)
        return carry

    lax.fori_loop(0, planes1, build_plane, 0)

    a2 = a2_ref[...].reshape((planes1 + 1) * c1, plane1)
    for bc in range(9):
        q2 = jnp.dot(a2, sel2_ref[:, bc * 128:(bc + 1) * 128], preferred_element_type=jnp.float32)
        q2_ref[:, :, bc * 128:(bc + 1) * 128] = q2.reshape(planes1 + 1, c1, 128)

    sg_ref[...] = jnp.zeros(sg_ref.shape, sg_ref.dtype)
    for n in range(planes2 // 2):
        for a in range(3):
            for bc in range(9):
                r0 = (a * 9 + bc) * c1
                lo = q2_ref[4 * n + a, :, bc * 128:(bc + 1) * 128]
                hi = q2_ref[4 * n + a + 2, :, bc * 128:(bc + 1) * 128]
                s2_ref[n, r0:r0 + c1, :] = (lo + pltpu.roll(hi, 64, 1)).astype(s2_ref.dtype)
        feat = jnp.dot(w2_ref[...], s2_ref[n], preferred_element_type=jnp.float32)
        feat_ref[:, n * 128:(n + 1) * 128] = feat.astype(feat_ref.dtype)
        sg_ref[...] += lax.dot_general(ogn_ref[:, n * 128:(n + 1) * 128], s2_ref[n], NT,
                                       preferred_element_type=jnp.float32)

    v_ref[planes2] = jnp.zeros(v_ref.shape[1:], v_ref.dtype)
    span = up_ref.shape[1] // 9
    for bc in range(9):
        u = jnp.dot(ogq_ref[...], up_ref[:, bc * span:(bc + 1) * span], preferred_element_type=jnp.float32)
        v_ref[pl.ds(0, planes2), bc] = u.astype(v_ref.dtype).reshape(planes2, c2, span)

    fg_ref[...] = jnp.zeros(fg_ref.shape, fg_ref.dtype)

    def back_plane(q, carry):
        vq = v_ref[q].reshape(9 * c2, span)
        vq1 = v_ref[q + 1].reshape(9 * c2, span)
        even = jnp.dot(w2t_ref[1], vq, preferred_element_type=jnp.float32)
        odd = (jnp.dot(w2t_ref[2], vq, preferred_element_type=jnp.float32)
               + jnp.dot(w2t_ref[0], vq1, preferred_element_type=jnp.float32))
        for k, act in ((0, even), (1, odd)):
            d2 = 2 * q + k
            pre = fp_ref[d2]
            sig = 1.0 / (1.0 + jnp.exp(-pre))
            slope = sig * (1.0 + pre * (1.0 - sig))
            pg = (act.astype(jnp.bfloat16).astype(jnp.float32) * slope).astype(jnp.bfloat16)
            fg_ref[...] += lax.dot_general(pg, s_ref[d2], NT, preferred_element_type=jnp.float32)
        return carry

    lax.fori_loop(0, planes2, back_plane, 0)


def per_sample(x, ogn, ogq, w1, w2, w2t, t1, sel2, up):
    depth, c0, cells = x.shape
    c1, c2 = w1.shape[0], w2.shape[0]
    planes1, planes2 = depth // 2, depth // 4
    plane1 = (HEIGHT // 2) * (WIDTH // 2)
    plane2 = ogq.shape[1]
    vmem = pltpu.VMEM
    return pl.pallas_call(
        conv_kernel,
        out_shape=(
            jax.ShapeDtypeStruct((c2, planes2 * plane2), jnp.bfloat16),
            jax.ShapeDtypeStruct((c1, 27 * c0), jnp.float32),
            jax.ShapeDtypeStruct((c2, 27 * c1), jnp.float32),
        ),
        in_specs=[pl.BlockSpec(memory_space=vmem)] * 9,
        out_specs=[pl.BlockSpec(memory_space=vmem)] * 3,
        scratch_shapes=[
            vmem((depth + 1, c0, (cells // 128) * 384), jnp.bfloat16),
            vmem((planes1, 27 * c0, plane1), jnp.bfloat16),
            vmem((planes1, c1, plane1), jnp.float32),
            vmem((planes1 + 1, c1, plane1), jnp.bfloat16),
            vmem((planes1 + 1, c1, 9 * 128), jnp.float32),
            vmem((planes2 // 2, 27 * c1, 128), jnp.bfloat16),
            vmem((planes2 + 1, 9, c2, plane1), jnp.bfloat16),
        ],
        compiler_params=pltpu.CompilerParams(vmem_limit_bytes=60 * 1024 * 1024),
    )(x, ogn, ogq, w1, w2, w2t, t1, sel2, up)


def body(crops, first_kernel, second_kernel, out_grad):
    local_samples, channels_in, planes, flat_cells = crops.shape
    whole_input = lax.all_to_all(crops, "space", split_axis=0, concat_axis=2, tiled=True)
    x = whole_input[0].transpose(1, 0, 2)
    c1, c2 = first_kernel.shape[0], second_kernel.shape[0]
    og = out_grad[0]
    ogn = og.reshape(c2, -1)
    ogq = og.transpose(1, 0, 2).reshape(-1, og.shape[2])
    w1 = first_kernel.transpose(0, 2, 3, 4, 1).reshape(c1, -1)
    w2 = second_kernel.transpose(0, 2, 3, 4, 1).reshape(c2, -1)
    w2t = second_kernel.transpose(2, 1, 3, 4, 0).reshape(3, c1, -1)
    t1, sel2, up = selection_tables(WIDTH, HEIGHT // 2, WIDTH // 2)
    feat, fg, sg = per_sample(
        x, ogn, ogq, w1, w2, w2t,
        jnp.asarray(t1, jnp.bfloat16), jnp.asarray(sel2, jnp.bfloat16), jnp.asarray(up, jnp.bfloat16),
    )
    features_out = feat.reshape(out_grad.shape)
    first_grad = fg.reshape(c1, 3, 3, 3, channels_in).transpose(0, 4, 1, 2, 3)
    second_grad = sg.reshape(c2, 3, 3, 3, c1).transpose(0, 4, 1, 2, 3)
    first_grad, second_grad = lax.psum((first_grad, second_grad), ("space", "sample"))
    return (features_out, first_grad, second_grad)


def solution(mesh):
    placed = (P("sample", None, "space", None), P(), P(), P(("sample", "space"), None, None, None))
    return jax.shard_map(
        body,
        mesh=mesh,
        in_specs=placed,
        out_specs=(P(("sample", "space"), None, None, None), P(), P()),
        check_vma=False,
    )
```

```python
import functools

import numpy as np

import jax
import jax.numpy as jnp
from jax import lax
from jax.experimental import pallas as pl
from jax.experimental.pallas import tpu as pltpu
from jax.sharding import PartitionSpec as P

HEIGHT = 8
WIDTH = 128

NT = (((1,), (1,)), ((), ()))


def selection_tables(c0_w, c1_h, c1_w):
    t1 = np.zeros((c0_w, 3 * 128), np.float32)
    for c in range(3):
        for pw in range(c0_w // 2):
            w = 2 * pw + c - 1
            if 0 <= w < c0_w:
                t1[w, c * 128 + pw] = 1.0
    q_h, q_w = c1_h // 2, c1_w // 2
    sel2 = np.zeros((c1_h * c1_w, 9 * 128), np.float32)
    up = np.zeros((q_h * q_w, 9 * c1_h * c1_w), np.float32)
    for b in range(3):
        for c in range(3):
            bc = b * 3 + c
            for qh in range(q_h):
                for qw in range(q_w):
                    h2, w2 = 2 * qh + b - 1, 2 * qw + c - 1
                    if 0 <= h2 < c1_h and 0 <= w2 < c1_w:
                        sel2[h2 * c1_w + w2, bc * 128 + qh * q_w + qw] = 1.0
                        up[qh * q_w + qw, bc * c1_h * c1_w + h2 * c1_w + w2] = 1.0
    return t1, sel2, up


def conv_kernel(x_ref, ogn_ref, ogq_ref, w1_ref, w2_ref, w2t_ref, t1_ref, sel2_ref, up_ref,
                feat_ref, fg_ref, sg_ref,
                q1_ref, s_ref, fp_ref, a2_ref, q2_ref, s2_ref, v_ref):
    depth, c0, cells = x_ref.shape
    n_h = cells // 128
    c1 = w1_ref.shape[0]
    c2 = w2_ref.shape[0]
    planes1 = depth // 2
    plane1 = s_ref.shape[2]
    planes2 = planes1 // 2
    plane2 = ogq_ref.shape[1]

    q1_ref[0] = jnp.zeros(q1_ref.shape[1:], q1_ref.dtype)
    for h in range(n_h):
        xh = x_ref[:, :, h * 128:(h + 1) * 128].reshape(depth * c0, 128)
        qh = jnp.dot(xh, t1_ref[...], preferred_element_type=jnp.float32)
        q1_ref[pl.ds(1, depth), :, h * 384:(h + 1) * 384] = qh.astype(q1_ref.dtype).reshape(depth, c0, 384)

    a2_ref[0] = jnp.zeros(a2_ref.shape[1:], a2_ref.dtype)

    def build_plane(pd, carry):
        for a in range(3):
            for b in range(3):
                for c in range(3):
                    r0 = ((a * 3 + b) * 3 + c) * c0
                    for m in range(plane1 // 128):
                        h_lo, h_hi = 4 * m + b - 1, 4 * m + b + 1
                        hi = q1_ref[2 * pd + a, :, pl.ds((h_hi * 3 + c) * 128, 128)].astype(jnp.float32)
                        val = pltpu.roll(hi, 64, 1)
                        if h_lo >= 0:
                            val = val + q1_ref[2 * pd + a, :, pl.ds((h_lo * 3 + c) * 128, 128)].astype(jnp.float32)
                        s_ref[pd, pl.ds(r0, c0), pl.ds(m * 128, 128)] = val.astype(s_ref.dtype)
        pre = jnp.dot(w1_ref[...], s_ref[pd], preferred_element_type=jnp.float32)
        fp_ref[pd] = pre
        sig = 1.0 / (1.0 + jnp.exp(-pre))
        a2_ref[pd + 1] = (pre * sig).astype(a2_ref.dtype)
        return carry

    lax.fori_loop(0, planes1, build_plane, 0)

    a2 = a2_ref[...].reshape((planes1 + 1) * c1, plane1)
    for bc in range(9):
        q2 = jnp.dot(a2, sel2_ref[:, bc * 128:(bc + 1) * 128], preferred_element_type=jnp.float32)
        q2_ref[:, :, bc * 128:(bc + 1) * 128] = q2.reshape(planes1 + 1, c1, 128)

    sg_ref[...] = jnp.zeros(sg_ref.shape, sg_ref.dtype)
    for n in range(planes2 // 2):
        for a in range(3):
            for bc in range(9):
                r0 = (a * 9 + bc) * c1
                lo = q2_ref[4 * n + a, :, bc * 128:(bc + 1) * 128]
                hi = q2_ref[4 * n + a + 2, :, bc * 128:(bc + 1) * 128]
                s2_ref[n, r0:r0 + c1, :] = (lo + pltpu.roll(hi, 64, 1)).astype(s2_ref.dtype)
        feat = jnp.dot(w2_ref[...], s2_ref[n], preferred_element_type=jnp.float32)
        feat_ref[:, n * 128:(n + 1) * 128] = feat.astype(feat_ref.dtype)
        sg_ref[...] += lax.dot_general(ogn_ref[:, n * 128:(n + 1) * 128], s2_ref[n], NT,
                                       preferred_element_type=jnp.float32)

    v_ref[planes2] = jnp.zeros(v_ref.shape[1:], v_ref.dtype)
    span = up_ref.shape[1] // 9
    for bc in range(9):
        u = jnp.dot(ogq_ref[...], up_ref[:, bc * span:(bc + 1) * span], preferred_element_type=jnp.float32)
        v_ref[pl.ds(0, planes2), bc] = u.astype(v_ref.dtype).reshape(planes2, c2, span)

    fg_ref[...] = jnp.zeros(fg_ref.shape, fg_ref.dtype)

    def back_plane(q, carry):
        vq = v_ref[q].reshape(9 * c2, span)
        vq1 = v_ref[q + 1].reshape(9 * c2, span)
        even = jnp.dot(w2t_ref[1], vq, preferred_element_type=jnp.float32)
        odd = (jnp.dot(w2t_ref[2], vq, preferred_element_type=jnp.float32)
               + jnp.dot(w2t_ref[0], vq1, preferred_element_type=jnp.float32))
        for k, act in ((0, even), (1, odd)):
            d2 = 2 * q + k
            pre = fp_ref[d2]
            sig = 1.0 / (1.0 + jnp.exp(-pre))
            slope = sig * (1.0 + pre * (1.0 - sig))
            pg = (act.astype(jnp.bfloat16).astype(jnp.float32) * slope).astype(jnp.bfloat16)
            fg_ref[...] += lax.dot_general(pg, s_ref[d2], NT, preferred_element_type=jnp.float32)
        return carry

    lax.fori_loop(0, planes2, back_plane, 0)


def per_sample(x, ogn, ogq, w1, w2, w2t, t1, sel2, up):
    depth, c0, cells = x.shape
    c1, c2 = w1.shape[0], w2.shape[0]
    planes1, planes2 = depth // 2, depth // 4
    plane1 = (HEIGHT // 2) * (WIDTH // 2)
    plane2 = ogq.shape[1]
    vmem = pltpu.VMEM
    return pl.pallas_call(
        conv_kernel,
        out_shape=(
            jax.ShapeDtypeStruct((c2, planes2 * plane2), jnp.bfloat16),
            jax.ShapeDtypeStruct((c1, 27 * c0), jnp.float32),
            jax.ShapeDtypeStruct((c2, 27 * c1), jnp.float32),
        ),
        in_specs=[pl.BlockSpec(memory_space=vmem)] * 9,
        out_specs=[pl.BlockSpec(memory_space=vmem)] * 3,
        scratch_shapes=[
            vmem((depth + 1, c0, (cells // 128) * 384), jnp.bfloat16),
            vmem((planes1, 27 * c0, plane1), jnp.bfloat16),
            vmem((planes1, c1, plane1), jnp.float32),
            vmem((planes1 + 1, c1, plane1), jnp.bfloat16),
            vmem((planes1 + 1, c1, 9 * 128), jnp.float32),
            vmem((planes2 // 2, 27 * c1, 128), jnp.bfloat16),
            vmem((planes2 + 1, 9, c2, plane1), jnp.bfloat16),
        ],
        compiler_params=pltpu.CompilerParams(vmem_limit_bytes=60 * 1024 * 1024),
    )(x, ogn, ogq, w1, w2, w2t, t1, sel2, up)


def partner_steps(axis_sizes):
    steps = []
    for axis, size in axis_sizes:
        bit = 1
        while bit < size:
            steps.append((axis, bit))
            bit *= 2
    return steps


def allreduce_kernel(axis_order, steps, g1_ref, g2_ref, o1_ref, o2_ref, r1_ref, r2_ref, send_sem, recv_sem):
    me = {axis: lax.axis_index(axis) for axis in axis_order}
    partners = []
    for axis, bit in steps:
        there = dict(me)
        there[axis] = me[axis] + bit - 2 * bit * ((me[axis] // bit) % 2)
        partners.append(tuple(there[a] for a in axis_order))

    barrier = pltpu.get_barrier_semaphore()
    for partner in partners:
        pl.semaphore_signal(barrier, 1, device_id=partner, device_id_type=pl.DeviceIdType.MESH)
    pl.semaphore_wait(barrier, len(partners))

    o1_ref[...] = g1_ref[...]
    o2_ref[...] = g2_ref[...]
    for s, partner in enumerate(partners):
        copies = [
            pltpu.make_async_remote_copy(
                src_ref=src, dst_ref=dst.at[s], send_sem=send_sem.at[s, k], recv_sem=recv_sem.at[s, k],
                device_id=partner, device_id_type=pl.DeviceIdType.MESH)
            for k, (src, dst) in enumerate(((o1_ref, r1_ref), (o2_ref, r2_ref)))
        ]
        for copy in copies:
            copy.start()
        for copy in copies:
            copy.wait()
        o1_ref[...] = o1_ref[...] + r1_ref[s]
        o2_ref[...] = o2_ref[...] + r2_ref[s]


def allreduce(g1, g2, axis_order, axis_sizes):
    steps = partner_steps(axis_sizes)
    vmem = pltpu.VMEM
    return pl.pallas_call(
        functools.partial(allreduce_kernel, axis_order, steps),
        out_shape=(jax.ShapeDtypeStruct(g1.shape, g1.dtype), jax.ShapeDtypeStruct(g2.shape, g2.dtype)),
        in_specs=[pl.BlockSpec(memory_space=vmem)] * 2,
        out_specs=[pl.BlockSpec(memory_space=vmem)] * 2,
        scratch_shapes=[
            vmem((len(steps),) + g1.shape, g1.dtype),
            vmem((len(steps),) + g2.shape, g2.dtype),
            pltpu.SemaphoreType.DMA((len(steps), 2)),
            pltpu.SemaphoreType.DMA((len(steps), 2)),
        ],
        compiler_params=pltpu.CompilerParams(collective_id=0, has_side_effects=True),
    )(g1, g2)


def body(axis_order, axis_sizes, crops, first_kernel, second_kernel, out_grad):
    local_samples, channels_in, planes, flat_cells = crops.shape
    whole_input = lax.all_to_all(crops, "space", split_axis=0, concat_axis=2, tiled=True)
    x = whole_input[0].transpose(1, 0, 2)
    c1, c2 = first_kernel.shape[0], second_kernel.shape[0]
    og = out_grad[0]
    ogn = og.reshape(c2, -1)
    ogq = og.transpose(1, 0, 2).reshape(-1, og.shape[2])
    w1 = first_kernel.transpose(0, 2, 3, 4, 1).reshape(c1, -1)
    w2 = second_kernel.transpose(0, 2, 3, 4, 1).reshape(c2, -1)
    w2t = second_kernel.transpose(2, 1, 3, 4, 0).reshape(3, c1, -1)
    t1, sel2, up = selection_tables(WIDTH, HEIGHT // 2, WIDTH // 2)
    feat, fg, sg = per_sample(
        x, ogn, ogq, w1, w2, w2t,
        jnp.asarray(t1, jnp.bfloat16), jnp.asarray(sel2, jnp.bfloat16), jnp.asarray(up, jnp.bfloat16),
    )
    features_out = feat.reshape(out_grad.shape)
    fg, sg = allreduce(fg, sg, axis_order, axis_sizes)
    first_grad = fg.reshape(c1, 3, 3, 3, channels_in).transpose(0, 4, 1, 2, 3)
    second_grad = sg.reshape(c2, 3, 3, 3, c1).transpose(0, 4, 1, 2, 3)
    return (features_out, first_grad, second_grad)


def solution(mesh):
    placed = (P("sample", None, "space", None), P(), P(), P(("sample", "space"), None, None, None))
    axis_order = tuple(mesh.axis_names)
    axis_sizes = [(a, mesh.shape[a]) for a in ("sample", "space")]
    return jax.shard_map(
        functools.partial(body, axis_order, axis_sizes),
        mesh=mesh,
        in_specs=placed,
        out_specs=(P(("sample", "space"), None, None, None), P(), P()),
        check_vma=False,
    )
```

```python
import functools

import numpy as np

import jax
import jax.numpy as jnp
from jax import lax
from jax.experimental import pallas as pl
from jax.experimental.pallas import tpu as pltpu
from jax.sharding import PartitionSpec as P

HEIGHT = 8
WIDTH = 128

NT = (((1,), (1,)), ((), ()))


def selection_tables(c0_w, c1_h, c1_w):
    t1 = np.zeros((c0_w, 3 * 128), np.float32)
    for c in range(3):
        for pw in range(c0_w // 2):
            w = 2 * pw + c - 1
            if 0 <= w < c0_w:
                t1[w, c * 128 + pw] = 1.0
    q_h, q_w = c1_h // 2, c1_w // 2
    sel2 = np.zeros((c1_h * c1_w, 9 * 128), np.float32)
    up = np.zeros((q_h * q_w, 9 * c1_h * c1_w), np.float32)
    for b in range(3):
        for c in range(3):
            bc = b * 3 + c
            for qh in range(q_h):
                for qw in range(q_w):
                    h2, w2 = 2 * qh + b - 1, 2 * qw + c - 1
                    if 0 <= h2 < c1_h and 0 <= w2 < c1_w:
                        sel2[h2 * c1_w + w2, bc * 128 + qh * q_w + qw] = 1.0
                        up[qh * q_w + qw, bc * c1_h * c1_w + h2 * c1_w + w2] = 1.0
    return t1, sel2, up


def conv_kernel(x_ref, ogn_ref, ogq_ref, w1_ref, w2_ref, w2t_ref, t1_ref, sel2_ref, up_ref,
                feat_ref, fg_ref, sg_ref,
                q1_ref, s_ref, fp_ref, a2_ref, q2_ref, s2_ref, v_ref):
    depth, c0, cells = x_ref.shape
    n_h = cells // 128
    c1 = w1_ref.shape[0]
    c2 = w2_ref.shape[0]
    planes1 = depth // 2
    plane1 = s_ref.shape[2]
    planes2 = planes1 // 2
    plane2 = ogq_ref.shape[1]

    q1_ref[0] = jnp.zeros(q1_ref.shape[1:], q1_ref.dtype)
    for h in range(n_h):
        xh = x_ref[:, :, h * 128:(h + 1) * 128].reshape(depth * c0, 128)
        qh = jnp.dot(xh, t1_ref[...], preferred_element_type=jnp.float32)
        q1_ref[pl.ds(1, depth), :, h * 384:(h + 1) * 384] = qh.astype(q1_ref.dtype).reshape(depth, c0, 384)

    a2_ref[0] = jnp.zeros(a2_ref.shape[1:], a2_ref.dtype)

    def build_plane(pd, carry):
        for a in range(3):
            for b in range(3):
                for c in range(3):
                    r0 = ((a * 3 + b) * 3 + c) * c0
                    for m in range(plane1 // 128):
                        h_lo, h_hi = 4 * m + b - 1, 4 * m + b + 1
                        hi = q1_ref[2 * pd + a, :, pl.ds((h_hi * 3 + c) * 128, 128)].astype(jnp.float32)
                        val = pltpu.roll(hi, 64, 1)
                        if h_lo >= 0:
                            val = val + q1_ref[2 * pd + a, :, pl.ds((h_lo * 3 + c) * 128, 128)].astype(jnp.float32)
                        s_ref[pd, pl.ds(r0, c0), pl.ds(m * 128, 128)] = val.astype(s_ref.dtype)
        pre = jnp.dot(w1_ref[...], s_ref[pd], preferred_element_type=jnp.float32)
        fp_ref[pd] = pre
        sig = 1.0 / (1.0 + jnp.exp(-pre))
        a2_ref[pd + 1] = (pre * sig).astype(a2_ref.dtype)
        return carry

    lax.fori_loop(0, planes1, build_plane, 0)

    a2 = a2_ref[...].reshape((planes1 + 1) * c1, plane1)
    for bc in range(9):
        q2 = jnp.dot(a2, sel2_ref[:, bc * 128:(bc + 1) * 128], preferred_element_type=jnp.float32)
        q2_ref[:, :, bc * 128:(bc + 1) * 128] = q2.reshape(planes1 + 1, c1, 128)

    sg_ref[...] = jnp.zeros(sg_ref.shape, sg_ref.dtype)
    for n in range(planes2 // 2):
        for a in range(3):
            for bc in range(9):
                r0 = (a * 9 + bc) * c1
                lo = q2_ref[4 * n + a, :, bc * 128:(bc + 1) * 128]
                hi = q2_ref[4 * n + a + 2, :, bc * 128:(bc + 1) * 128]
                s2_ref[n, r0:r0 + c1, :] = (lo + pltpu.roll(hi, 64, 1)).astype(s2_ref.dtype)
        feat = jnp.dot(w2_ref[...], s2_ref[n], preferred_element_type=jnp.float32)
        feat_ref[:, n * 128:(n + 1) * 128] = feat.astype(feat_ref.dtype)
        sg_ref[...] += lax.dot_general(ogn_ref[:, n * 128:(n + 1) * 128], s2_ref[n], NT,
                                       preferred_element_type=jnp.float32)

    v_ref[planes2] = jnp.zeros(v_ref.shape[1:], v_ref.dtype)
    span = up_ref.shape[1] // 9
    for bc in range(9):
        u = jnp.dot(ogq_ref[...], up_ref[:, bc * span:(bc + 1) * span], preferred_element_type=jnp.float32)
        v_ref[pl.ds(0, planes2), bc] = u.astype(v_ref.dtype).reshape(planes2, c2, span)

    fg_ref[...] = jnp.zeros(fg_ref.shape, fg_ref.dtype)

    def back_plane(q, carry):
        vq = v_ref[q].reshape(9 * c2, span)
        vq1 = v_ref[q + 1].reshape(9 * c2, span)
        even = jnp.dot(w2t_ref[1], vq, preferred_element_type=jnp.float32)
        odd = (jnp.dot(w2t_ref[2], vq, preferred_element_type=jnp.float32)
               + jnp.dot(w2t_ref[0], vq1, preferred_element_type=jnp.float32))
        for k, act in ((0, even), (1, odd)):
            d2 = 2 * q + k
            pre = fp_ref[d2]
            sig = 1.0 / (1.0 + jnp.exp(-pre))
            slope = sig * (1.0 + pre * (1.0 - sig))
            pg = (act.astype(jnp.bfloat16).astype(jnp.float32) * slope).astype(jnp.bfloat16)
            fg_ref[...] += lax.dot_general(pg, s_ref[d2], NT, preferred_element_type=jnp.float32)
        return carry

    lax.fori_loop(0, planes2, back_plane, 0)


def per_sample(x, ogn, ogq, w1, w2, w2t, t1, sel2, up):
    depth, c0, cells = x.shape
    c1, c2 = w1.shape[0], w2.shape[0]
    planes1, planes2 = depth // 2, depth // 4
    plane1 = (HEIGHT // 2) * (WIDTH // 2)
    plane2 = ogq.shape[1]
    vmem = pltpu.VMEM
    return pl.pallas_call(
        conv_kernel,
        out_shape=(
            jax.ShapeDtypeStruct((c2, planes2 * plane2), jnp.bfloat16),
            jax.ShapeDtypeStruct((c1, 27 * c0), jnp.float32),
            jax.ShapeDtypeStruct((c2, 27 * c1), jnp.float32),
        ),
        in_specs=[pl.BlockSpec(memory_space=vmem)] * 9,
        out_specs=[pl.BlockSpec(memory_space=vmem)] * 3,
        scratch_shapes=[
            vmem((depth + 1, c0, (cells // 128) * 384), jnp.bfloat16),
            vmem((planes1, 27 * c0, plane1), jnp.bfloat16),
            vmem((planes1, c1, plane1), jnp.float32),
            vmem((planes1 + 1, c1, plane1), jnp.bfloat16),
            vmem((planes1 + 1, c1, 9 * 128), jnp.float32),
            vmem((planes2 // 2, 27 * c1, 128), jnp.bfloat16),
            vmem((planes2 + 1, 9, c2, plane1), jnp.bfloat16),
        ],
        compiler_params=pltpu.CompilerParams(vmem_limit_bytes=60 * 1024 * 1024),
    )(x, ogn, ogq, w1, w2, w2t, t1, sel2, up)


STEP_ORDER = (("sample", 1), ("space", 4), ("sample", 2), ("space", 1),
              ("space", 2), ("sample", 4), ("space", 8), ("space", 16))


def partner_steps(axis_sizes):
    sizes = dict(axis_sizes)
    steps = [(axis, bit) for axis, bit in STEP_ORDER if bit < sizes[axis]]
    for axis, size in axis_sizes:
        bit = 1
        while bit < size:
            if (axis, bit) not in steps:
                steps.append((axis, bit))
            bit *= 2
    return steps


def halvings(rows, steps):
    count = 0
    while count < len(steps) and rows % (2 ** (count + 1) * 8) == 0:
        count += 1
    return count


def allreduce_kernel(axis_order, steps, g1_ref, g2_ref, o1_ref, o2_ref, r1_ref, r2_ref, a1_ref, a2_ref,
                     send_sem, recv_sem):
    me = {axis: lax.axis_index(axis) for axis in axis_order}
    partners, bits = [], []
    for axis, bit in steps:
        mine = (me[axis] // bit) % 2
        there = dict(me)
        there[axis] = me[axis] + bit - 2 * bit * mine
        partners.append(tuple(there[a] for a in axis_order))
        bits.append(mine)

    barrier = pltpu.get_barrier_semaphore()
    for partner in partners:
        pl.semaphore_signal(barrier, 1, device_id=partner, device_id_type=pl.DeviceIdType.MESH)
    pl.semaphore_wait(barrier, len(partners))

    accs = (o1_ref, o2_ref)
    recvs = (r1_ref, r2_ref)
    gathers = (a1_ref, a2_ref)
    o1_ref[...] = g1_ref[...]
    o2_ref[...] = g2_ref[...]
    n_steps = len(steps)
    plans = []
    for acc in accs:
        plans.append({"rows": acc.shape[0], "h": halvings(acc.shape[0], steps), "off": 0, "kept": []})

    def remote(src, dst, slot, k, partner):
        return pltpu.make_async_remote_copy(
            src_ref=src, dst_ref=dst, send_sem=send_sem.at[slot, k], recv_sem=recv_sem.at[slot, k],
            device_id=partner, device_id_type=pl.DeviceIdType.MESH)

    for s in range(n_steps):
        copies, adds = [], []
        for k, (acc, recv, plan) in enumerate(zip(accs, recvs, plans)):
            if s < plan["h"]:
                half = plan["rows"] // 2
                keep = pl.multiple_of(plan["off"] + bits[s] * half, 8)
                give = pl.multiple_of(plan["off"] + (1 - bits[s]) * half, 8)
                copies.append(remote(acc.at[pl.ds(give, half)], recv.at[s, pl.ds(0, half)], s, k, partners[s]))
                adds.append((acc, recv, s, keep, half))
                plan["kept"].append((s, keep, give, half))
                plan["off"], plan["rows"] = keep, half
            else:
                rows = plan["rows"]
                off = plan["off"]
                copies.append(remote(acc.at[pl.ds(off, rows)], recv.at[s, pl.ds(0, rows)], s, k, partners[s]))
                adds.append((acc, recv, s, off, rows))
        for copy in copies:
            copy.start()
        for copy in copies:
            copy.wait()
        for acc, recv, slot, off, rows in adds:
            acc[pl.ds(off, rows)] = acc[pl.ds(off, rows)] + recv[slot, pl.ds(0, rows)]

    for s in reversed(range(n_steps)):
        copies, places = [], []
        for k, (acc, gather, plan) in enumerate(zip(accs, gathers, plans)):
            for step, keep, give, half in plan["kept"]:
                if step == s:
                    copies.append(remote(acc.at[pl.ds(keep, half)], gather.at[s, pl.ds(0, half)],
                                         n_steps + s, k, partners[s]))
                    places.append((acc, gather, give, half))
        for copy in copies:
            copy.start()
        for copy in copies:
            copy.wait()
        for acc, gather, give, half in places:
            acc[pl.ds(give, half)] = gather[s, pl.ds(0, half)]


def allreduce(g1, g2, axis_order, axis_sizes):
    steps = partner_steps(axis_sizes)
    vmem = pltpu.VMEM
    return pl.pallas_call(
        functools.partial(allreduce_kernel, axis_order, steps),
        out_shape=(jax.ShapeDtypeStruct(g1.shape, g1.dtype), jax.ShapeDtypeStruct(g2.shape, g2.dtype)),
        in_specs=[pl.BlockSpec(memory_space=vmem)] * 2,
        out_specs=[pl.BlockSpec(memory_space=vmem)] * 2,
        scratch_shapes=[
            vmem((len(steps), g1.shape[0] // 2) + g1.shape[1:], g1.dtype),
            vmem((len(steps), g2.shape[0] // 2) + g2.shape[1:], g2.dtype),
            vmem((len(steps), g1.shape[0] // 2) + g1.shape[1:], g1.dtype),
            vmem((len(steps), g2.shape[0] // 2) + g2.shape[1:], g2.dtype),
            pltpu.SemaphoreType.DMA((2 * len(steps), 2)),
            pltpu.SemaphoreType.DMA((2 * len(steps), 2)),
        ],
        compiler_params=pltpu.CompilerParams(collective_id=0, has_side_effects=True),
    )(g1, g2)


def body(axis_order, axis_sizes, crops, first_kernel, second_kernel, out_grad):
    local_samples, channels_in, planes, flat_cells = crops.shape
    whole_input = lax.all_to_all(crops, "space", split_axis=0, concat_axis=2, tiled=True)
    x = whole_input[0].transpose(1, 0, 2)
    c1, c2 = first_kernel.shape[0], second_kernel.shape[0]
    og = out_grad[0]
    ogn = og.reshape(c2, -1)
    ogq = og.transpose(1, 0, 2).reshape(-1, og.shape[2])
    w1 = first_kernel.transpose(0, 2, 3, 4, 1).reshape(c1, -1)
    w2 = second_kernel.transpose(0, 2, 3, 4, 1).reshape(c2, -1)
    w2t = second_kernel.transpose(2, 1, 3, 4, 0).reshape(3, c1, -1)
    t1, sel2, up = selection_tables(WIDTH, HEIGHT // 2, WIDTH // 2)
    feat, fg, sg = per_sample(
        x, ogn, ogq, w1, w2, w2t,
        jnp.asarray(t1, jnp.bfloat16), jnp.asarray(sel2, jnp.bfloat16), jnp.asarray(up, jnp.bfloat16),
    )
    features_out = feat.reshape(out_grad.shape)
    fg, sg = allreduce(fg, sg, axis_order, axis_sizes)
    first_grad = fg.reshape(c1, 3, 3, 3, channels_in).transpose(0, 4, 1, 2, 3)
    second_grad = sg.reshape(c2, 3, 3, 3, c1).transpose(0, 4, 1, 2, 3)
    return (features_out, first_grad, second_grad)


def solution(mesh):
    placed = (P("sample", None, "space", None), P(), P(), P(("sample", "space"), None, None, None))
    axis_order = tuple(mesh.axis_names)
    axis_sizes = [(a, mesh.shape[a]) for a in ("sample", "space")]
    return jax.shard_map(
        functools.partial(body, axis_order, axis_sizes),
        mesh=mesh,
        in_specs=placed,
        out_specs=(P(("sample", "space"), None, None, None), P(), P()),
        check_vma=False,
    )
```

```python
import functools

import numpy as np

import jax
import jax.numpy as jnp
from jax import lax
from jax.experimental import pallas as pl
from jax.experimental.pallas import tpu as pltpu
from jax.sharding import PartitionSpec as P

HEIGHT = 8
WIDTH = 128

NT = (((1,), (1,)), ((), ()))


def selection_tables(c0_w, c1_h, c1_w):
    t1 = np.zeros((c0_w, 3 * 128), np.float32)
    for c in range(3):
        for pw in range(c0_w // 2):
            w = 2 * pw + c - 1
            if 0 <= w < c0_w:
                t1[w, c * 128 + pw] = 1.0
    q_h, q_w = c1_h // 2, c1_w // 2
    sel2 = np.zeros((c1_h * c1_w, 9 * 128), np.float32)
    up = np.zeros((q_h * q_w, 9 * c1_h * c1_w), np.float32)
    for b in range(3):
        for c in range(3):
            bc = b * 3 + c
            for qh in range(q_h):
                for qw in range(q_w):
                    h2, w2 = 2 * qh + b - 1, 2 * qw + c - 1
                    if 0 <= h2 < c1_h and 0 <= w2 < c1_w:
                        sel2[h2 * c1_w + w2, bc * 128 + qh * q_w + qw] = 1.0
                        up[qh * q_w + qw, bc * c1_h * c1_w + h2 * c1_w + w2] = 1.0
    return t1, sel2, up


def conv_kernel(x_ref, ogn_ref, ogq_ref, w1_ref, w2_ref, w2t_ref, t1_ref, sel2_ref, up_ref,
                feat_ref, fg_ref, sg_ref,
                q1_ref, s_ref, fp_ref, a2_ref, q2_ref, s2_ref, v_ref):
    depth, c0, cells = x_ref.shape
    n_h = cells // 128
    c1 = w1_ref.shape[0]
    c2 = w2_ref.shape[0]
    planes1 = depth // 2
    plane1 = s_ref.shape[2]
    planes2 = planes1 // 2
    plane2 = ogq_ref.shape[1]

    q1_ref[0] = jnp.zeros(q1_ref.shape[1:], q1_ref.dtype)
    for h in range(n_h):
        xh = x_ref[:, :, h * 128:(h + 1) * 128].reshape(depth * c0, 128)
        qh = jnp.dot(xh, t1_ref[...], preferred_element_type=jnp.float32)
        q1_ref[pl.ds(1, depth), :, h * 384:(h + 1) * 384] = qh.astype(q1_ref.dtype).reshape(depth, c0, 384)

    a2_ref[0] = jnp.zeros(a2_ref.shape[1:], a2_ref.dtype)

    def build_plane(pd, carry):
        for a in range(3):
            for b in range(3):
                for c in range(3):
                    r0 = ((a * 3 + b) * 3 + c) * c0
                    for m in range(plane1 // 128):
                        h_lo, h_hi = 4 * m + b - 1, 4 * m + b + 1
                        hi = q1_ref[2 * pd + a, :, pl.ds((h_hi * 3 + c) * 128, 128)].astype(jnp.float32)
                        val = pltpu.roll(hi, 64, 1)
                        if h_lo >= 0:
                            val = val + q1_ref[2 * pd + a, :, pl.ds((h_lo * 3 + c) * 128, 128)].astype(jnp.float32)
                        s_ref[pd, pl.ds(r0, c0), pl.ds(m * 128, 128)] = val.astype(s_ref.dtype)
        pre = jnp.dot(w1_ref[...], s_ref[pd], preferred_element_type=jnp.float32)
        fp_ref[pd] = pre
        sig = 1.0 / (1.0 + jnp.exp(-pre))
        a2_ref[pd + 1] = (pre * sig).astype(a2_ref.dtype)
        return carry

    lax.fori_loop(0, planes1, build_plane, 0)

    a2 = a2_ref[...].reshape((planes1 + 1) * c1, plane1)
    for bc in range(9):
        q2 = jnp.dot(a2, sel2_ref[:, bc * 128:(bc + 1) * 128], preferred_element_type=jnp.float32)
        q2_ref[:, :, bc * 128:(bc + 1) * 128] = q2.reshape(planes1 + 1, c1, 128)

    sg_ref[...] = jnp.zeros(sg_ref.shape, sg_ref.dtype)
    for n in range(planes2 // 2):
        for a in range(3):
            for bc in range(9):
                r0 = (a * 9 + bc) * c1
                lo = q2_ref[4 * n + a, :, bc * 128:(bc + 1) * 128]
                hi = q2_ref[4 * n + a + 2, :, bc * 128:(bc + 1) * 128]
                s2_ref[n, r0:r0 + c1, :] = (lo + pltpu.roll(hi, 64, 1)).astype(s2_ref.dtype)
        feat = jnp.dot(w2_ref[...], s2_ref[n], preferred_element_type=jnp.float32)
        feat_ref[:, n * 128:(n + 1) * 128] = feat.astype(feat_ref.dtype)
        sg_ref[...] += lax.dot_general(ogn_ref[:, n * 128:(n + 1) * 128], s2_ref[n], NT,
                                       preferred_element_type=jnp.float32)

    v_ref[planes2] = jnp.zeros(v_ref.shape[1:], v_ref.dtype)
    span = up_ref.shape[1] // 9
    for bc in range(9):
        u = jnp.dot(ogq_ref[...], up_ref[:, bc * span:(bc + 1) * span], preferred_element_type=jnp.float32)
        v_ref[pl.ds(0, planes2), bc] = u.astype(v_ref.dtype).reshape(planes2, c2, span)

    fg_ref[...] = jnp.zeros(fg_ref.shape, fg_ref.dtype)

    def back_plane(q, carry):
        vq = v_ref[q].reshape(9 * c2, span)
        vq1 = v_ref[q + 1].reshape(9 * c2, span)
        even = jnp.dot(w2t_ref[1], vq, preferred_element_type=jnp.float32)
        odd = (jnp.dot(w2t_ref[2], vq, preferred_element_type=jnp.float32)
               + jnp.dot(w2t_ref[0], vq1, preferred_element_type=jnp.float32))
        for k, act in ((0, even), (1, odd)):
            d2 = 2 * q + k
            pre = fp_ref[d2]
            sig = 1.0 / (1.0 + jnp.exp(-pre))
            slope = sig * (1.0 + pre * (1.0 - sig))
            pg = (act.astype(jnp.bfloat16).astype(jnp.float32) * slope).astype(jnp.bfloat16)
            fg_ref[...] += lax.dot_general(pg, s_ref[d2], NT, preferred_element_type=jnp.float32)
        return carry

    lax.fori_loop(0, planes2, back_plane, 0)


def per_sample(x, ogn, ogq, w1, w2, w2t, t1, sel2, up):
    depth, c0, cells = x.shape
    c1, c2 = w1.shape[0], w2.shape[0]
    planes1, planes2 = depth // 2, depth // 4
    plane1 = (HEIGHT // 2) * (WIDTH // 2)
    plane2 = ogq.shape[1]
    vmem = pltpu.VMEM
    return pl.pallas_call(
        conv_kernel,
        out_shape=(
            jax.ShapeDtypeStruct((c2, planes2 * plane2), jnp.bfloat16),
            jax.ShapeDtypeStruct((c1, 27 * c0), jnp.float32),
            jax.ShapeDtypeStruct((c2, 27 * c1), jnp.float32),
        ),
        in_specs=[pl.BlockSpec(memory_space=vmem)] * 9,
        out_specs=[pl.BlockSpec(memory_space=vmem)] * 3,
        scratch_shapes=[
            vmem((depth + 1, c0, (cells // 128) * 384), jnp.bfloat16),
            vmem((planes1, 27 * c0, plane1), jnp.bfloat16),
            vmem((planes1, c1, plane1), jnp.float32),
            vmem((planes1 + 1, c1, plane1), jnp.bfloat16),
            vmem((planes1 + 1, c1, 9 * 128), jnp.float32),
            vmem((planes2 // 2, 27 * c1, 128), jnp.bfloat16),
            vmem((planes2 + 1, 9, c2, plane1), jnp.bfloat16),
        ],
        compiler_params=pltpu.CompilerParams(vmem_limit_bytes=60 * 1024 * 1024),
    )(x, ogn, ogq, w1, w2, w2t, t1, sel2, up)


STEP_ORDER = (("sample", 1), ("space", 4), ("sample", 2), ("space", 1),
              ("space", 2), ("sample", 4), ("space", 8), ("space", 16))


def partner_steps(axis_sizes):
    sizes = dict(axis_sizes)
    steps = [(axis, bit) for axis, bit in STEP_ORDER if bit < sizes[axis]]
    for axis, size in axis_sizes:
        bit = 1
        while bit < size:
            if (axis, bit) not in steps:
                steps.append((axis, bit))
            bit *= 2
    return steps


def halvings(rows, steps):
    count = 0
    while count < len(steps) and rows % (2 ** (count + 1) * 8) == 0:
        count += 1
    return count


def allreduce_kernel(axis_order, steps, g1_ref, g2_ref, o1_ref, o2_ref, r1_ref, r2_ref, a1_ref, a2_ref,
                     send_sem, recv_sem):
    me = {axis: lax.axis_index(axis) for axis in axis_order}
    partners, bits = [], []
    for axis, bit in steps:
        mine = (me[axis] // bit) % 2
        there = dict(me)
        there[axis] = me[axis] + bit - 2 * bit * mine
        partners.append(tuple(there[a] for a in axis_order))
        bits.append(mine)

    barrier = pltpu.get_barrier_semaphore()
    for partner in partners:
        pl.semaphore_signal(barrier, 1, device_id=partner, device_id_type=pl.DeviceIdType.MESH)
    pl.semaphore_wait(barrier, len(partners))

    accs = (o1_ref, o2_ref)
    recvs = (r1_ref, r2_ref)
    gathers = (a1_ref, a2_ref)
    o1_ref[...] = g1_ref[...]
    o2_ref[...] = g2_ref[...]
    n_steps = len(steps)
    plans = []
    for acc in accs:
        plans.append({"rows": acc.shape[0], "h": halvings(acc.shape[0], steps), "off": 0, "kept": []})

    def remote(src, dst, slot, k, partner):
        return pltpu.make_async_remote_copy(
            src_ref=src, dst_ref=dst, send_sem=send_sem.at[slot, k], recv_sem=recv_sem.at[slot, k],
            device_id=partner, device_id_type=pl.DeviceIdType.MESH)

    for s in range(n_steps):
        copies, adds = [], []
        for k, (acc, recv, plan) in enumerate(zip(accs, recvs, plans)):
            if s < plan["h"]:
                half = plan["rows"] // 2
                keep = pl.multiple_of(plan["off"] + bits[s] * half, 8)
                give = pl.multiple_of(plan["off"] + (1 - bits[s]) * half, 8)
                copies.append(remote(acc.at[pl.ds(give, half)], recv.at[s, pl.ds(0, half)], s, k, partners[s]))
                adds.append((acc, recv, s, keep, half))
                plan["kept"].append((s, keep, give, half))
                plan["off"], plan["rows"] = keep, half
            else:
                rows = plan["rows"]
                off = plan["off"]
                copies.append(remote(acc.at[pl.ds(off, rows)], recv.at[s, pl.ds(0, rows)], s, k, partners[s]))
                adds.append((acc, recv, s, off, rows))
        for copy in copies:
            copy.start()
        for copy in copies:
            copy.wait()
        for acc, recv, slot, off, rows in adds:
            acc[pl.ds(off, rows)] = acc[pl.ds(off, rows)] + recv[slot, pl.ds(0, rows)]

    for s in reversed(range(n_steps)):
        copies, places = [], []
        for k, (acc, gather, plan) in enumerate(zip(accs, gathers, plans)):
            for step, keep, give, half in plan["kept"]:
                if step == s:
                    copies.append(remote(acc.at[pl.ds(keep, half)], gather.at[s, pl.ds(0, half)],
                                         n_steps + s, k, partners[s]))
                    places.append((acc, gather, give, half))
        for copy in copies:
            copy.start()
        for copy in copies:
            copy.wait()
        for acc, gather, give, half in places:
            acc[pl.ds(give, half)] = gather[s, pl.ds(0, half)]


def allreduce(g1, g2, axis_order, axis_sizes):
    steps = partner_steps(axis_sizes)
    vmem = pltpu.VMEM
    return pl.pallas_call(
        functools.partial(allreduce_kernel, axis_order, steps),
        out_shape=(jax.ShapeDtypeStruct(g1.shape, g1.dtype), jax.ShapeDtypeStruct(g2.shape, g2.dtype)),
        in_specs=[pl.BlockSpec(memory_space=vmem)] * 2,
        out_specs=[pl.BlockSpec(memory_space=vmem)] * 2,
        scratch_shapes=[
            vmem((len(steps), g1.shape[0] // 2) + g1.shape[1:], g1.dtype),
            vmem((len(steps), g2.shape[0] // 2) + g2.shape[1:], g2.dtype),
            vmem((len(steps), g1.shape[0] // 2) + g1.shape[1:], g1.dtype),
            vmem((len(steps), g2.shape[0] // 2) + g2.shape[1:], g2.dtype),
            pltpu.SemaphoreType.DMA((2 * len(steps), 2)),
            pltpu.SemaphoreType.DMA((2 * len(steps), 2)),
        ],
        compiler_params=pltpu.CompilerParams(collective_id=0, has_side_effects=True),
    )(g1, g2)


def gather_kernel(axis_order, src_ref, out_ref, send_sem, recv_sem, local_sem):
    me = {axis: lax.axis_index(axis) for axis in axis_order}
    n = src_ref.shape[0]
    planes = src_ref.shape[2]
    j = me["space"]
    targets = []
    for t in range(1, n):
        there = dict(me)
        there["space"] = (j + t) % n
        targets.append((t, there["space"], tuple(there[a] for a in axis_order)))

    barrier = pltpu.get_barrier_semaphore()
    for t, dest, device in targets:
        pl.semaphore_signal(barrier, 1, device_id=device, device_id_type=pl.DeviceIdType.MESH)
    pl.semaphore_wait(barrier, n - 1)

    mine = pl.ds(pl.multiple_of(j * planes, planes), planes)
    local = pltpu.make_async_copy(src_ref.at[j], out_ref.at[:, mine, :], local_sem)
    local.start()
    copies = []
    for t, dest, device in targets:
        copy = pltpu.make_async_remote_copy(
            src_ref=src_ref.at[dest], dst_ref=out_ref.at[:, mine, :],
            send_sem=send_sem.at[t], recv_sem=recv_sem.at[t],
            device_id=device, device_id_type=pl.DeviceIdType.MESH)
        copy.start()
        copies.append(copy)
    local.wait()
    for copy in copies:
        copy.wait()


def gather_crops(crops, axis_order):
    n, c0, planes, cells = crops.shape
    return pl.pallas_call(
        functools.partial(gather_kernel, axis_order),
        out_shape=jax.ShapeDtypeStruct((c0, n * planes, cells), crops.dtype),
        in_specs=[pl.BlockSpec(memory_space=pl.ANY)],
        out_specs=pl.BlockSpec(memory_space=pl.ANY),
        scratch_shapes=[
            pltpu.SemaphoreType.DMA((n,)),
            pltpu.SemaphoreType.DMA((n,)),
            pltpu.SemaphoreType.DMA(()),
        ],
        compiler_params=pltpu.CompilerParams(collective_id=1, has_side_effects=True),
    )(crops)


def body(axis_order, axis_sizes, crops, first_kernel, second_kernel, out_grad):
    local_samples, channels_in, planes, flat_cells = crops.shape
    x = gather_crops(crops, axis_order).transpose(1, 0, 2)
    c1, c2 = first_kernel.shape[0], second_kernel.shape[0]
    og = out_grad[0]
    ogn = og.reshape(c2, -1)
    ogq = og.transpose(1, 0, 2).reshape(-1, og.shape[2])
    w1 = first_kernel.transpose(0, 2, 3, 4, 1).reshape(c1, -1)
    w2 = second_kernel.transpose(0, 2, 3, 4, 1).reshape(c2, -1)
    w2t = second_kernel.transpose(2, 1, 3, 4, 0).reshape(3, c1, -1)
    t1, sel2, up = selection_tables(WIDTH, HEIGHT // 2, WIDTH // 2)
    feat, fg, sg = per_sample(
        x, ogn, ogq, w1, w2, w2t,
        jnp.asarray(t1, jnp.bfloat16), jnp.asarray(sel2, jnp.bfloat16), jnp.asarray(up, jnp.bfloat16),
    )
    features_out = feat.reshape(out_grad.shape)
    fg, sg = allreduce(fg, sg, axis_order, axis_sizes)
    first_grad = fg.reshape(c1, 3, 3, 3, channels_in).transpose(0, 4, 1, 2, 3)
    second_grad = sg.reshape(c2, 3, 3, 3, c1).transpose(0, 4, 1, 2, 3)
    return (features_out, first_grad, second_grad)


def solution(mesh):
    placed = (P("sample", None, "space", None), P(), P(), P(("sample", "space"), None, None, None))
    axis_order = tuple(mesh.axis_names)
    axis_sizes = [(a, mesh.shape[a]) for a in ("sample", "space")]
    return jax.shard_map(
        functools.partial(body, axis_order, axis_sizes),
        mesh=mesh,
        in_specs=placed,
        out_specs=(P(("sample", "space"), None, None, None), P(), P()),
        check_vma=False,
    )
```

```python
import functools

import numpy as np

import jax
import jax.numpy as jnp
from jax import lax
from jax.experimental import pallas as pl
from jax.experimental.pallas import tpu as pltpu
from jax.sharding import PartitionSpec as P

HEIGHT = 8
WIDTH = 128

NT = (((1,), (1,)), ((), ()))


def selection_tables(c0_w, c1_h, c1_w):
    t1 = np.zeros((c0_w, 3 * 128), np.float32)
    for c in range(3):
        for pw in range(c0_w // 2):
            w = 2 * pw + c - 1
            if 0 <= w < c0_w:
                t1[w, c * 128 + pw] = 1.0
    q_h, q_w = c1_h // 2, c1_w // 2
    sel2 = np.zeros((c1_h * c1_w, 9 * 128), np.float32)
    up = np.zeros((q_h * q_w, 9 * c1_h * c1_w), np.float32)
    for b in range(3):
        for c in range(3):
            bc = b * 3 + c
            for qh in range(q_h):
                for qw in range(q_w):
                    h2, w2 = 2 * qh + b - 1, 2 * qw + c - 1
                    if 0 <= h2 < c1_h and 0 <= w2 < c1_w:
                        sel2[h2 * c1_w + w2, bc * 128 + qh * q_w + qw] = 1.0
                        up[qh * q_w + qw, bc * c1_h * c1_w + h2 * c1_w + w2] = 1.0
    return t1, sel2, up


def conv_kernel(x_ref, ogn_ref, ogq_ref, w1_ref, w2_ref, w2t_ref, t1_ref, sel2_ref, up_ref,
                feat_ref, fg_ref, sg_ref,
                q1_ref, s_ref, fp_ref, a2_ref, q2_ref, s2_ref, v_ref):
    depth, c0, cells = x_ref.shape
    n_h = cells // 128
    c1 = w1_ref.shape[0]
    c2 = w2_ref.shape[0]
    planes1 = depth // 2
    plane1 = s_ref.shape[2]
    planes2 = planes1 // 2
    plane2 = ogq_ref.shape[1]

    q1_ref[0] = jnp.zeros(q1_ref.shape[1:], q1_ref.dtype)
    for h in range(n_h):
        xh = x_ref[:, :, h * 128:(h + 1) * 128].reshape(depth * c0, 128)
        qh = jnp.dot(xh, t1_ref[...], preferred_element_type=jnp.float32)
        q1_ref[pl.ds(1, depth), :, h * 384:(h + 1) * 384] = qh.astype(q1_ref.dtype).reshape(depth, c0, 384)

    a2_ref[0] = jnp.zeros(a2_ref.shape[1:], a2_ref.dtype)

    def build_plane(pd, carry):
        for a in range(3):
            for b in range(3):
                for c in range(3):
                    r0 = ((a * 3 + b) * 3 + c) * c0
                    for m in range(plane1 // 128):
                        h_lo, h_hi = 4 * m + b - 1, 4 * m + b + 1
                        hi = q1_ref[2 * pd + a, :, pl.ds((h_hi * 3 + c) * 128, 128)].astype(jnp.float32)
                        val = pltpu.roll(hi, 64, 1)
                        if h_lo >= 0:
                            val = val + q1_ref[2 * pd + a, :, pl.ds((h_lo * 3 + c) * 128, 128)].astype(jnp.float32)
                        s_ref[pd, pl.ds(r0, c0), pl.ds(m * 128, 128)] = val.astype(s_ref.dtype)
        pre = jnp.dot(w1_ref[...], s_ref[pd], preferred_element_type=jnp.float32)
        sig = 1.0 / (1.0 + jnp.exp(-pre))
        fp_ref[pd] = sig * (1.0 + pre * (1.0 - sig))
        a2_ref[pd + 1] = (pre * sig).astype(a2_ref.dtype)
        return carry

    lax.fori_loop(0, planes1, build_plane, 0)

    a2 = a2_ref[...].reshape((planes1 + 1) * c1, plane1)
    for bc in range(9):
        q2 = jnp.dot(a2, sel2_ref[:, bc * 128:(bc + 1) * 128], preferred_element_type=jnp.float32)
        q2_ref[:, :, bc * 128:(bc + 1) * 128] = q2.reshape(planes1 + 1, c1, 128)

    sg_ref[...] = jnp.zeros(sg_ref.shape, sg_ref.dtype)
    for n in range(planes2 // 2):
        for a in range(3):
            for bc in range(9):
                r0 = (a * 9 + bc) * c1
                lo = q2_ref[4 * n + a, :, bc * 128:(bc + 1) * 128]
                hi = q2_ref[4 * n + a + 2, :, bc * 128:(bc + 1) * 128]
                s2_ref[n, r0:r0 + c1, :] = (lo + pltpu.roll(hi, 64, 1)).astype(s2_ref.dtype)
        feat = jnp.dot(w2_ref[...], s2_ref[n], preferred_element_type=jnp.float32)
        feat_ref[:, n * 128:(n + 1) * 128] = feat.astype(feat_ref.dtype)
        sg_ref[...] += lax.dot_general(ogn_ref[:, n * 128:(n + 1) * 128], s2_ref[n], NT,
                                       preferred_element_type=jnp.float32)

    v_ref[planes2] = jnp.zeros(v_ref.shape[1:], v_ref.dtype)
    span = up_ref.shape[1] // 9
    for bc in range(9):
        u = jnp.dot(ogq_ref[...], up_ref[:, bc * span:(bc + 1) * span], preferred_element_type=jnp.float32)
        v_ref[pl.ds(0, planes2), bc] = u.astype(v_ref.dtype).reshape(planes2, c2, span)

    fg_ref[...] = jnp.zeros(fg_ref.shape, fg_ref.dtype)

    def back_plane(q, carry):
        vq = v_ref[q].reshape(9 * c2, span)
        vq1 = v_ref[q + 1].reshape(9 * c2, span)
        even = jnp.dot(w2t_ref[1], vq, preferred_element_type=jnp.float32)
        odd = (jnp.dot(w2t_ref[2], vq, preferred_element_type=jnp.float32)
               + jnp.dot(w2t_ref[0], vq1, preferred_element_type=jnp.float32))
        for k, act in ((0, even), (1, odd)):
            d2 = 2 * q + k
            slope = fp_ref[d2]
            pg = (act.astype(jnp.bfloat16).astype(jnp.float32) * slope).astype(jnp.bfloat16)
            fg_ref[...] += lax.dot_general(pg, s_ref[d2], NT, preferred_element_type=jnp.float32)
        return carry

    lax.fori_loop(0, planes2, back_plane, 0)


def per_sample(x, ogn, ogq, w1, w2, w2t, t1, sel2, up):
    depth, c0, cells = x.shape
    c1, c2 = w1.shape[0], w2.shape[0]
    planes1, planes2 = depth // 2, depth // 4
    plane1 = (HEIGHT // 2) * (WIDTH // 2)
    plane2 = ogq.shape[1]
    vmem = pltpu.VMEM
    return pl.pallas_call(
        conv_kernel,
        out_shape=(
            jax.ShapeDtypeStruct((c2, planes2 * plane2), jnp.bfloat16),
            jax.ShapeDtypeStruct((c1, 27 * c0), jnp.float32),
            jax.ShapeDtypeStruct((c2, 27 * c1), jnp.float32),
        ),
        in_specs=[pl.BlockSpec(memory_space=vmem)] * 9,
        out_specs=[pl.BlockSpec(memory_space=vmem)] * 3,
        scratch_shapes=[
            vmem((depth + 1, c0, (cells // 128) * 384), jnp.bfloat16),
            vmem((planes1, 27 * c0, plane1), jnp.bfloat16),
            vmem((planes1, c1, plane1), jnp.float32),
            vmem((planes1 + 1, c1, plane1), jnp.bfloat16),
            vmem((planes1 + 1, c1, 9 * 128), jnp.float32),
            vmem((planes2 // 2, 27 * c1, 128), jnp.bfloat16),
            vmem((planes2 + 1, 9, c2, plane1), jnp.bfloat16),
        ],
        compiler_params=pltpu.CompilerParams(vmem_limit_bytes=60 * 1024 * 1024),
    )(x, ogn, ogq, w1, w2, w2t, t1, sel2, up)


STEP_ORDER = (("sample", 1), ("space", 4), ("sample", 2), ("space", 1),
              ("space", 2), ("sample", 4), ("space", 8), ("space", 16))


def partner_steps(axis_sizes):
    sizes = dict(axis_sizes)
    steps = [(axis, bit) for axis, bit in STEP_ORDER if bit < sizes[axis]]
    for axis, size in axis_sizes:
        bit = 1
        while bit < size:
            if (axis, bit) not in steps:
                steps.append((axis, bit))
            bit *= 2
    return steps


def halvings(rows, steps):
    count = 0
    while count < len(steps) and rows % (2 ** (count + 1) * 8) == 0:
        count += 1
    return count


def allreduce_kernel(axis_order, steps, g1_ref, g2_ref, t1_ref, t2_ref, o1_ref, o2_ref, r1_ref, r2_ref,
                     a1_ref, a2_ref, send_sem, recv_sem):
    me = {axis: lax.axis_index(axis) for axis in axis_order}
    partners, bits = [], []
    for axis, bit in steps:
        mine = (me[axis] // bit) % 2
        there = dict(me)
        there[axis] = me[axis] + bit - 2 * bit * mine
        partners.append(tuple(there[a] for a in axis_order))
        bits.append(mine)

    barrier = pltpu.get_barrier_semaphore()
    for partner in partners:
        pl.semaphore_signal(barrier, 1, device_id=partner, device_id_type=pl.DeviceIdType.MESH)
    pl.semaphore_wait(barrier, len(partners))

    accs = (o1_ref, o2_ref)
    recvs = (r1_ref, r2_ref)
    gathers = (a1_ref, a2_ref)
    o1_ref[...] = g1_ref[...]
    o2_ref[...] = g2_ref[...]
    n_steps = len(steps)
    plans = []
    for acc in accs:
        plans.append({"rows": acc.shape[0], "h": halvings(acc.shape[0], steps), "off": 0, "kept": []})

    def remote(src, dst, slot, k, partner):
        return pltpu.make_async_remote_copy(
            src_ref=src, dst_ref=dst, send_sem=send_sem.at[slot, k], recv_sem=recv_sem.at[slot, k],
            device_id=partner, device_id_type=pl.DeviceIdType.MESH)

    for s in range(n_steps):
        copies, adds = [], []
        for k, (acc, recv, plan) in enumerate(zip(accs, recvs, plans)):
            if s < plan["h"]:
                half = plan["rows"] // 2
                keep = pl.multiple_of(plan["off"] + bits[s] * half, 8)
                give = pl.multiple_of(plan["off"] + (1 - bits[s]) * half, 8)
                copies.append(remote(acc.at[pl.ds(give, half)], recv.at[s, pl.ds(0, half)], s, k, partners[s]))
                adds.append((acc, recv, s, keep, half))
                plan["kept"].append((s, keep, give, half))
                plan["off"], plan["rows"] = keep, half
            else:
                rows = plan["rows"]
                off = plan["off"]
                copies.append(remote(acc.at[pl.ds(off, rows)], recv.at[s, pl.ds(0, rows)], s, k, partners[s]))
                adds.append((acc, recv, s, off, rows))
        for copy in copies:
            copy.start()
        for copy in copies:
            copy.wait()
        for acc, recv, slot, off, rows in adds:
            acc[pl.ds(off, rows)] = acc[pl.ds(off, rows)] + recv[slot, pl.ds(0, rows)]

    for s in reversed(range(n_steps)):
        copies, places = [], []
        for k, (acc, gather, plan) in enumerate(zip(accs, gathers, plans)):
            for step, keep, give, half in plan["kept"]:
                if step == s:
                    copies.append(remote(acc.at[pl.ds(keep, half)], gather.at[s, pl.ds(0, half)],
                                         n_steps + s, k, partners[s]))
                    places.append((acc, gather, give, half))
        for copy in copies:
            copy.start()
        for copy in copies:
            copy.wait()
        for acc, gather, give, half in places:
            acc[pl.ds(give, half)] = gather[s, pl.ds(0, half)]
    t1_ref[...] = o1_ref[...].T
    t2_ref[...] = o2_ref[...].T


def allreduce(g1, g2, axis_order, axis_sizes):
    steps = partner_steps(axis_sizes)
    vmem = pltpu.VMEM
    return pl.pallas_call(
        functools.partial(allreduce_kernel, axis_order, steps),
        out_shape=(jax.ShapeDtypeStruct(g1.shape[::-1], g1.dtype), jax.ShapeDtypeStruct(g2.shape[::-1], g2.dtype)),
        in_specs=[pl.BlockSpec(memory_space=vmem)] * 2,
        out_specs=[pl.BlockSpec(memory_space=vmem)] * 2,
        scratch_shapes=[
            vmem(g1.shape, g1.dtype),
            vmem(g2.shape, g2.dtype),
            vmem((len(steps), g1.shape[0] // 2) + g1.shape[1:], g1.dtype),
            vmem((len(steps), g2.shape[0] // 2) + g2.shape[1:], g2.dtype),
            vmem((len(steps), g1.shape[0] // 2) + g1.shape[1:], g1.dtype),
            vmem((len(steps), g2.shape[0] // 2) + g2.shape[1:], g2.dtype),
            pltpu.SemaphoreType.DMA((2 * len(steps), 2)),
            pltpu.SemaphoreType.DMA((2 * len(steps), 2)),
        ],
        compiler_params=pltpu.CompilerParams(collective_id=0, has_side_effects=True),
    )(g1, g2)


def body(axis_order, axis_sizes, crops, first_kernel, second_kernel, out_grad):
    local_samples, channels_in, planes, flat_cells = crops.shape
    whole_input = lax.all_to_all(crops, "space", split_axis=0, concat_axis=2, tiled=True)
    x = whole_input[0].transpose(1, 0, 2)
    c1, c2 = first_kernel.shape[0], second_kernel.shape[0]
    og = out_grad[0]
    ogn = og.reshape(c2, -1)
    ogq = og.transpose(1, 0, 2).reshape(-1, og.shape[2])
    w1 = first_kernel.transpose(0, 2, 3, 4, 1).reshape(c1, -1)
    w2 = second_kernel.transpose(0, 2, 3, 4, 1).reshape(c2, -1)
    w2t = second_kernel.transpose(2, 1, 3, 4, 0).reshape(3, c1, -1)
    t1, sel2, up = selection_tables(WIDTH, HEIGHT // 2, WIDTH // 2)
    feat, fg, sg = per_sample(
        x, ogn, ogq, w1, w2, w2t,
        jnp.asarray(t1, jnp.bfloat16), jnp.asarray(sel2, jnp.bfloat16), jnp.asarray(up, jnp.bfloat16),
    )
    features_out = feat.reshape(out_grad.shape)
    fg, sg = allreduce(fg, sg, axis_order, axis_sizes)
    first_grad = fg.reshape(3, 3, 3, channels_in, c1).transpose(4, 3, 0, 1, 2)
    second_grad = sg.reshape(3, 3, 3, c1, c2).transpose(4, 3, 0, 1, 2)
    return (features_out, first_grad, second_grad)


def solution(mesh):
    placed = (P("sample", None, "space", None), P(), P(), P(("sample", "space"), None, None, None))
    axis_order = tuple(mesh.axis_names)
    axis_sizes = [(a, mesh.shape[a]) for a in ("sample", "space")]
    return jax.shard_map(
        functools.partial(body, axis_order, axis_sizes),
        mesh=mesh,
        in_specs=placed,
        out_specs=(P(("sample", "space"), None, None, None), P(), P()),
        check_vma=False,
    )
```

```python
import functools

import numpy as np

import jax
import jax.numpy as jnp
from jax import lax
from jax.experimental import pallas as pl
from jax.experimental.pallas import tpu as pltpu
from jax.sharding import PartitionSpec as P

HEIGHT = 8
WIDTH = 128

NT = (((1,), (1,)), ((), ()))


def selection_tables(c0_w, c1_h, c1_w):
    t1 = np.zeros((c0_w, 3 * 128), np.float32)
    for c in range(3):
        for pw in range(c0_w // 2):
            w = 2 * pw + c - 1
            if 0 <= w < c0_w:
                t1[w, c * 128 + pw] = 1.0
    q_h, q_w = c1_h // 2, c1_w // 2
    sel2 = np.zeros((c1_h * c1_w, 9 * 128), np.float32)
    up = np.zeros((q_h * q_w, 9 * c1_h * c1_w), np.float32)
    for b in range(3):
        for c in range(3):
            bc = b * 3 + c
            for qh in range(q_h):
                for qw in range(q_w):
                    h2, w2 = 2 * qh + b - 1, 2 * qw + c - 1
                    if 0 <= h2 < c1_h and 0 <= w2 < c1_w:
                        sel2[h2 * c1_w + w2, bc * 128 + qh * q_w + qw] = 1.0
                        up[qh * q_w + qw, bc * c1_h * c1_w + h2 * c1_w + w2] = 1.0
    return t1, sel2, up


def conv_kernel(x_ref, ogn_ref, ogq_ref, w1_ref, w2_ref, w2t_ref, t1_ref, sel2_ref, up_ref,
                feat_ref, fg_ref, sg_ref,
                q1_ref, s_ref, fp_ref, a2_ref, q2_ref, s2_ref, v_ref):
    depth, c0, cells = x_ref.shape
    n_h = cells // 128
    c1 = w1_ref.shape[0]
    c2 = w2_ref.shape[0]
    planes1 = depth // 2
    plane1 = s_ref.shape[2]
    planes2 = planes1 // 2
    plane2 = ogq_ref.shape[1]

    q1_ref[0] = jnp.zeros(q1_ref.shape[1:], q1_ref.dtype)
    for h in range(n_h):
        xh = x_ref[:, :, h * 128:(h + 1) * 128].reshape(depth * c0, 128)
        qh = jnp.dot(xh, t1_ref[...], preferred_element_type=jnp.float32)
        q1_ref[pl.ds(1, depth), :, h * 384:(h + 1) * 384] = qh.astype(q1_ref.dtype).reshape(depth, c0, 384)

    a2_ref[0] = jnp.zeros(a2_ref.shape[1:], a2_ref.dtype)

    def build_plane(pd, carry):
        for a in range(3):
            for b in range(3):
                for c in range(3):
                    r0 = ((a * 3 + b) * 3 + c) * c0
                    for m in range(plane1 // 128):
                        h_lo, h_hi = 4 * m + b - 1, 4 * m + b + 1
                        hi = q1_ref[2 * pd + a, :, pl.ds((h_hi * 3 + c) * 128, 128)].astype(jnp.float32)
                        val = pltpu.roll(hi, 64, 1)
                        if h_lo >= 0:
                            val = val + q1_ref[2 * pd + a, :, pl.ds((h_lo * 3 + c) * 128, 128)].astype(jnp.float32)
                        s_ref[pd, pl.ds(r0, c0), pl.ds(m * 128, 128)] = val.astype(s_ref.dtype)
        pre = jnp.dot(w1_ref[...], s_ref[pd], preferred_element_type=jnp.float32)
        sig = 1.0 / (1.0 + jnp.exp(-pre))
        fp_ref[pd] = sig * (1.0 + pre * (1.0 - sig))
        a2_ref[pd + 1] = (pre * sig).astype(a2_ref.dtype)
        return carry

    lax.fori_loop(0, planes1, build_plane, 0)

    a2 = a2_ref[...].reshape((planes1 + 1) * c1, plane1)
    for bc in range(9):
        q2 = jnp.dot(a2, sel2_ref[:, bc * 128:(bc + 1) * 128], preferred_element_type=jnp.float32)
        q2_ref[:, :, bc * 128:(bc + 1) * 128] = q2.reshape(planes1 + 1, c1, 128)

    sg_ref[...] = jnp.zeros(sg_ref.shape, sg_ref.dtype)
    for n in range(planes2 // 2):
        for a in range(3):
            for bc in range(9):
                r0 = (a * 9 + bc) * c1
                lo = q2_ref[4 * n + a, :, bc * 128:(bc + 1) * 128]
                hi = q2_ref[4 * n + a + 2, :, bc * 128:(bc + 1) * 128]
                s2_ref[n, r0:r0 + c1, :] = (lo + pltpu.roll(hi, 64, 1)).astype(s2_ref.dtype)
        feat = jnp.dot(w2_ref[...], s2_ref[n], preferred_element_type=jnp.float32)
        feat_ref[:, n * 128:(n + 1) * 128] = feat.astype(feat_ref.dtype)
        sg_ref[...] += lax.dot_general(ogn_ref[:, n * 128:(n + 1) * 128], s2_ref[n], NT,
                                       preferred_element_type=jnp.float32)

    v_ref[planes2] = jnp.zeros(v_ref.shape[1:], v_ref.dtype)
    span = up_ref.shape[1] // 9
    for bc in range(9):
        u = jnp.dot(ogq_ref[...], up_ref[:, bc * span:(bc + 1) * span], preferred_element_type=jnp.float32)
        v_ref[pl.ds(0, planes2), bc] = u.astype(v_ref.dtype).reshape(planes2, c2, span)

    fg_ref[...] = jnp.zeros(fg_ref.shape, fg_ref.dtype)

    def back_plane(q, carry):
        vq = v_ref[q].reshape(9 * c2, span)
        vq1 = v_ref[q + 1].reshape(9 * c2, span)
        even = jnp.dot(w2t_ref[1], vq, preferred_element_type=jnp.float32)
        odd = (jnp.dot(w2t_ref[2], vq, preferred_element_type=jnp.float32)
               + jnp.dot(w2t_ref[0], vq1, preferred_element_type=jnp.float32))
        for k, act in ((0, even), (1, odd)):
            d2 = 2 * q + k
            slope = fp_ref[d2]
            pg = (act.astype(jnp.bfloat16).astype(jnp.float32) * slope).astype(jnp.bfloat16)
            fg_ref[...] += lax.dot_general(pg, s_ref[d2], NT, preferred_element_type=jnp.float32)
        return carry

    lax.fori_loop(0, planes2, back_plane, 0)


def per_sample(x, ogn, ogq, w1, w2, w2t, t1, sel2, up):
    depth, c0, cells = x.shape
    c1, c2 = w1.shape[0], w2.shape[0]
    planes1, planes2 = depth // 2, depth // 4
    plane1 = (HEIGHT // 2) * (WIDTH // 2)
    plane2 = ogq.shape[1]
    vmem = pltpu.VMEM
    return pl.pallas_call(
        conv_kernel,
        out_shape=(
            jax.ShapeDtypeStruct((c2, planes2 * plane2), jnp.bfloat16),
            jax.ShapeDtypeStruct((c1, 27 * c0), jnp.float32),
            jax.ShapeDtypeStruct((c2, 27 * c1), jnp.float32),
        ),
        in_specs=[pl.BlockSpec(memory_space=vmem)] * 9,
        out_specs=[pl.BlockSpec(memory_space=vmem)] * 3,
        scratch_shapes=[
            vmem((depth + 1, c0, (cells // 128) * 384), jnp.bfloat16),
            vmem((planes1, 27 * c0, plane1), jnp.bfloat16),
            vmem((planes1, c1, plane1), jnp.float32),
            vmem((planes1 + 1, c1, plane1), jnp.bfloat16),
            vmem((planes1 + 1, c1, 9 * 128), jnp.float32),
            vmem((planes2 // 2, 27 * c1, 128), jnp.bfloat16),
            vmem((planes2 + 1, 9, c2, plane1), jnp.bfloat16),
        ],
        compiler_params=pltpu.CompilerParams(vmem_limit_bytes=60 * 1024 * 1024),
    )(x, ogn, ogq, w1, w2, w2t, t1, sel2, up)


ROUND_ORDER = ((("sample", 1),), (("space", 4),), (("sample", 2),),
               (("space", 1), ("space", 2), ("sample", 4)), (("space", 8), ("space", 16)))


def exchange_rounds(axis_sizes):
    sizes = dict(axis_sizes)
    rounds = []
    for group in ROUND_ORDER:
        kept = tuple((axis, bit) for axis, bit in group if bit < sizes[axis])
        if kept:
            rounds.append(kept)
    used = {pair for group in rounds for pair in group}
    for axis, size in axis_sizes:
        bit = 1
        while bit < size:
            if (axis, bit) not in used:
                rounds.append(((axis, bit),))
            bit *= 2
    return rounds


def halvings(rows, rounds):
    count = 0
    while (count < len(rounds) and len(rounds[count]) == 1
           and rows % (2 ** (count + 1) * 8) == 0):
        count += 1
    return count


def allreduce_kernel(axis_order, rounds, g1_ref, g2_ref, t1_ref, t2_ref, o1_ref, o2_ref, r1_ref, r2_ref,
                     a1_ref, a2_ref, x1_ref, x2_ref, send_sem, recv_sem, gather_sem):
    me = {axis: lax.axis_index(axis) for axis in axis_order}

    def bit_of(axis, bit):
        return (me[axis] // bit) % 2

    plan_rounds = []
    for group in rounds:
        own = sum(bit_of(axis, bit) * 2 ** idx for idx, (axis, bit) in enumerate(group))
        members = []
        for t in range(1, 2 ** len(group)):
            there = dict(me)
            slot = 0
            for idx, (axis, bit) in enumerate(group):
                flip = (t // 2 ** idx) % 2
                if flip:
                    there[axis] = there[axis] + bit - 2 * bit * bit_of(axis, bit)
                slot = slot + ((bit_of(axis, bit) + flip) % 2) * 2 ** idx
            members.append((t, slot, tuple(there[a] for a in axis_order)))
        plan_rounds.append((group, own, members))

    barrier = pltpu.get_barrier_semaphore()
    count = 0
    for group, own, members in plan_rounds:
        for t, slot, device in members:
            pl.semaphore_signal(barrier, 1, device_id=device, device_id_type=pl.DeviceIdType.MESH)
            count += 1
    pl.semaphore_wait(barrier, count)

    accs = (o1_ref, o2_ref)
    recvs = (r1_ref, r2_ref)
    gathers = (a1_ref, a2_ref)
    groups = (x1_ref, x2_ref)
    o1_ref[...] = g1_ref[...]
    o2_ref[...] = g2_ref[...]
    plans = [{"rows": acc.shape[0], "h": halvings(acc.shape[0], rounds), "off": 0, "kept": []} for acc in accs]

    def remote(src, dst, send, recv, device):
        return pltpu.make_async_remote_copy(
            src_ref=src, dst_ref=dst, send_sem=send, recv_sem=recv,
            device_id=device, device_id_type=pl.DeviceIdType.MESH)

    for r, (group, own, members) in enumerate(plan_rounds):
        sends, recvs_wait, after = [], [], []
        for k, (acc, recv, xbuf, plan) in enumerate(zip(accs, recvs, groups, plans)):
            if r < plan["h"]:
                (axis, bit), = group
                t, slot, device = members[0]
                mine = bit_of(axis, bit)
                half = plan["rows"] // 2
                keep = pl.multiple_of(plan["off"] + mine * half, 8)
                give = pl.multiple_of(plan["off"] + (1 - mine) * half, 8)
                copy = remote(acc.at[pl.ds(give, half)], recv.at[r, pl.ds(0, half)],
                              send_sem.at[r, 0, k], recv_sem.at[r, 0, k], device)
                sends.append(copy)
                recvs_wait.append(copy)
                after.append(("add", acc, recv, r, keep, half))
                plan["kept"].append((r, keep, give, half))
                plan["off"], plan["rows"] = keep, half
            else:
                rows, off = plan["rows"], plan["off"]
                xbuf[r, own] = acc[pl.ds(off, rows)]
                for t, slot, device in members:
                    sends.append(remote(acc.at[pl.ds(off, rows)], xbuf.at[r, own],
                                        send_sem.at[r, t, k], recv_sem.at[r, own, k], device))
                    recvs_wait.append(remote(acc.at[pl.ds(off, rows)], xbuf.at[r, slot],
                                             send_sem.at[r, t, k], recv_sem.at[r, slot, k], device))
                after.append(("sum", acc, xbuf, r, off, rows, 2 ** len(group)))
        for copy in sends:
            copy.start()
        for copy in sends:
            copy.wait_send()
        for copy in recvs_wait:
            copy.wait_recv()
        for item in after:
            if item[0] == "add":
                _, acc, recv, slot_r, off, rows = item
                acc[pl.ds(off, rows)] = acc[pl.ds(off, rows)] + recv[slot_r, pl.ds(0, rows)]
            else:
                _, acc, xbuf, slot_r, off, rows, n_members = item
                total = xbuf[slot_r, 0]
                for q in range(1, n_members):
                    total = total + xbuf[slot_r, q]
                acc[pl.ds(off, rows)] = total

    for r in reversed(range(len(plan_rounds))):
        copies, places = [], []
        group, own, members = plan_rounds[r]
        for k, (acc, gather, plan) in enumerate(zip(accs, gathers, plans)):
            for step, keep, give, half in plan["kept"]:
                if step == r:
                    t, slot, device = members[0]
                    copies.append(remote(acc.at[pl.ds(keep, half)], gather.at[r, pl.ds(0, half)],
                                         gather_sem.at[r, 0, k], gather_sem.at[r, 1, k], device))
                    places.append((acc, gather, give, half))
        for copy in copies:
            copy.start()
        for copy in copies:
            copy.wait()
        for acc, gather, give, half in places:
            acc[pl.ds(give, half)] = gather[r, pl.ds(0, half)]
    t1_ref[...] = o1_ref[...].T
    t2_ref[...] = o2_ref[...].T


def allreduce(g1, g2, axis_order, axis_sizes):
    rounds = exchange_rounds(axis_sizes)
    n = len(rounds)
    width = max(2 ** len(group) for group in rounds)
    vmem = pltpu.VMEM
    chunk = [g.shape[0] // 2 ** halvings(g.shape[0], rounds) for g in (g1, g2)]
    return pl.pallas_call(
        functools.partial(allreduce_kernel, axis_order, rounds),
        out_shape=(jax.ShapeDtypeStruct(g1.shape[::-1], g1.dtype), jax.ShapeDtypeStruct(g2.shape[::-1], g2.dtype)),
        in_specs=[pl.BlockSpec(memory_space=vmem)] * 2,
        out_specs=[pl.BlockSpec(memory_space=vmem)] * 2,
        scratch_shapes=[
            vmem(g1.shape, g1.dtype),
            vmem(g2.shape, g2.dtype),
            vmem((n, g1.shape[0] // 2) + g1.shape[1:], g1.dtype),
            vmem((n, g2.shape[0] // 2) + g2.shape[1:], g2.dtype),
            vmem((n, g1.shape[0] // 2) + g1.shape[1:], g1.dtype),
            vmem((n, g2.shape[0] // 2) + g2.shape[1:], g2.dtype),
            vmem((n, width, chunk[0]) + g1.shape[1:], g1.dtype),
            vmem((n, width, chunk[1]) + g2.shape[1:], g2.dtype),
            pltpu.SemaphoreType.DMA((n, width, 2)),
            pltpu.SemaphoreType.DMA((n, width, 2)),
            pltpu.SemaphoreType.DMA((n, 2, 2)),
        ],
        compiler_params=pltpu.CompilerParams(collective_id=0, has_side_effects=True),
    )(g1, g2)


def body(axis_order, axis_sizes, crops, first_kernel, second_kernel, out_grad):
    local_samples, channels_in, planes, flat_cells = crops.shape
    whole_input = lax.all_to_all(crops, "space", split_axis=0, concat_axis=2, tiled=True)
    x = whole_input[0].transpose(1, 0, 2)
    c1, c2 = first_kernel.shape[0], second_kernel.shape[0]
    og = out_grad[0]
    ogn = og.reshape(c2, -1)
    ogq = og.transpose(1, 0, 2).reshape(-1, og.shape[2])
    w1 = first_kernel.transpose(0, 2, 3, 4, 1).reshape(c1, -1)
    w2 = second_kernel.transpose(0, 2, 3, 4, 1).reshape(c2, -1)
    w2t = second_kernel.transpose(2, 1, 3, 4, 0).reshape(3, c1, -1)
    t1, sel2, up = selection_tables(WIDTH, HEIGHT // 2, WIDTH // 2)
    feat, fg, sg = per_sample(
        x, ogn, ogq, w1, w2, w2t,
        jnp.asarray(t1, jnp.bfloat16), jnp.asarray(sel2, jnp.bfloat16), jnp.asarray(up, jnp.bfloat16),
    )
    features_out = feat.reshape(out_grad.shape)
    fg, sg = allreduce(fg, sg, axis_order, axis_sizes)
    first_grad = fg.reshape(3, 3, 3, channels_in, c1).transpose(4, 3, 0, 1, 2)
    second_grad = sg.reshape(3, 3, 3, c1, c2).transpose(4, 3, 0, 1, 2)
    return (features_out, first_grad, second_grad)


def solution(mesh):
    placed = (P("sample", None, "space", None), P(), P(), P(("sample", "space"), None, None, None))
    axis_order = tuple(mesh.axis_names)
    axis_sizes = [(a, mesh.shape[a]) for a in ("sample", "space")]
    return jax.shard_map(
        functools.partial(body, axis_order, axis_sizes),
        mesh=mesh,
        in_specs=placed,
        out_specs=(P(("sample", "space"), None, None, None), P(), P()),
        check_vma=False,
    )
```

```python
import functools

import numpy as np

import jax
import jax.numpy as jnp
from jax import lax
from jax.experimental import pallas as pl
from jax.experimental.pallas import tpu as pltpu
from jax.sharding import PartitionSpec as P

HEIGHT = 8
WIDTH = 128

NT = (((1,), (1,)), ((), ()))


def selection_tables(c0_w, c1_h, c1_w):
    t1 = np.zeros((c0_w, 3 * 128), np.float32)
    for c in range(3):
        for pw in range(c0_w // 2):
            w = 2 * pw + c - 1
            if 0 <= w < c0_w:
                t1[w, c * 128 + pw] = 1.0
    q_h, q_w = c1_h // 2, c1_w // 2
    sel2 = np.zeros((c1_h * c1_w, 9 * 128), np.float32)
    up = np.zeros((q_h * q_w, 9 * c1_h * c1_w), np.float32)
    for b in range(3):
        for c in range(3):
            bc = b * 3 + c
            for qh in range(q_h):
                for qw in range(q_w):
                    h2, w2 = 2 * qh + b - 1, 2 * qw + c - 1
                    if 0 <= h2 < c1_h and 0 <= w2 < c1_w:
                        sel2[h2 * c1_w + w2, bc * 128 + qh * q_w + qw] = 1.0
                        up[qh * q_w + qw, bc * c1_h * c1_w + h2 * c1_w + w2] = 1.0
    return t1, sel2, up


def conv_kernel(x_ref, ogn_ref, ogq_ref, w1_ref, w2_ref, w2t_ref, t1_ref, sel2_ref, up_ref,
                feat_ref, fg_ref, sg_ref,
                q1_ref, s_ref, fp_ref, a2_ref, q2_ref, s2_ref, v_ref):
    depth, c0, cells = x_ref.shape
    n_h = cells // 128
    c1 = w1_ref.shape[0]
    c2 = w2_ref.shape[0]
    planes1 = depth // 2
    plane1 = s_ref.shape[2]
    planes2 = planes1 // 2
    plane2 = ogq_ref.shape[1]

    q1_ref[0] = jnp.zeros(q1_ref.shape[1:], q1_ref.dtype)
    for h in range(n_h):
        xh = x_ref[:, :, h * 128:(h + 1) * 128].reshape(depth * c0, 128)
        qh = jnp.dot(xh, t1_ref[...], preferred_element_type=jnp.float32)
        q1_ref[pl.ds(1, depth), :, h * 384:(h + 1) * 384] = qh.astype(q1_ref.dtype).reshape(depth, c0, 384)

    a2_ref[0] = jnp.zeros(a2_ref.shape[1:], a2_ref.dtype)

    def build_plane(pd, carry):
        for a in range(3):
            for b in range(3):
                for c in range(3):
                    r0 = ((a * 3 + b) * 3 + c) * c0
                    for m in range(plane1 // 128):
                        h_lo, h_hi = 4 * m + b - 1, 4 * m + b + 1
                        hi = q1_ref[2 * pd + a, :, pl.ds((h_hi * 3 + c) * 128, 128)].astype(jnp.float32)
                        val = pltpu.roll(hi, 64, 1)
                        if h_lo >= 0:
                            val = val + q1_ref[2 * pd + a, :, pl.ds((h_lo * 3 + c) * 128, 128)].astype(jnp.float32)
                        s_ref[pd, pl.ds(r0, c0), pl.ds(m * 128, 128)] = val.astype(s_ref.dtype)
        pre = jnp.dot(w1_ref[...], s_ref[pd], preferred_element_type=jnp.float32)
        sig = 1.0 / (1.0 + jnp.exp(-pre))
        fp_ref[pd] = sig * (1.0 + pre * (1.0 - sig))
        a2_ref[pd + 1] = (pre * sig).astype(a2_ref.dtype)
        return carry

    lax.fori_loop(0, planes1, build_plane, 0)

    a2 = a2_ref[...].reshape((planes1 + 1) * c1, plane1)
    for bc in range(9):
        q2 = jnp.dot(a2, sel2_ref[:, bc * 128:(bc + 1) * 128], preferred_element_type=jnp.float32)
        q2_ref[:, :, bc * 128:(bc + 1) * 128] = q2.reshape(planes1 + 1, c1, 128)

    sg_ref[...] = jnp.zeros(sg_ref.shape, sg_ref.dtype)
    for n in range(planes2 // 2):
        for a in range(3):
            for bc in range(9):
                r0 = (a * 9 + bc) * c1
                lo = q2_ref[4 * n + a, :, bc * 128:(bc + 1) * 128]
                hi = q2_ref[4 * n + a + 2, :, bc * 128:(bc + 1) * 128]
                s2_ref[n, r0:r0 + c1, :] = (lo + pltpu.roll(hi, 64, 1)).astype(s2_ref.dtype)
        feat = jnp.dot(w2_ref[...], s2_ref[n], preferred_element_type=jnp.float32)
        feat_ref[:, n * 128:(n + 1) * 128] = feat.astype(feat_ref.dtype)
        sg_ref[...] += lax.dot_general(ogn_ref[:, n * 128:(n + 1) * 128], s2_ref[n], NT,
                                       preferred_element_type=jnp.float32)

    v_ref[planes2] = jnp.zeros(v_ref.shape[1:], v_ref.dtype)
    span = up_ref.shape[1] // 9
    for bc in range(9):
        u = jnp.dot(ogq_ref[...], up_ref[:, bc * span:(bc + 1) * span], preferred_element_type=jnp.float32)
        v_ref[pl.ds(0, planes2), bc] = u.astype(v_ref.dtype).reshape(planes2, c2, span)

    fg_ref[...] = jnp.zeros(fg_ref.shape, fg_ref.dtype)

    def back_plane(q, carry):
        vq = v_ref[q].reshape(9 * c2, span)
        vq1 = v_ref[q + 1].reshape(9 * c2, span)
        even = jnp.dot(w2t_ref[1], vq, preferred_element_type=jnp.float32)
        odd = (jnp.dot(w2t_ref[2], vq, preferred_element_type=jnp.float32)
               + jnp.dot(w2t_ref[0], vq1, preferred_element_type=jnp.float32))
        for k, act in ((0, even), (1, odd)):
            d2 = 2 * q + k
            slope = fp_ref[d2]
            pg = (act.astype(jnp.bfloat16).astype(jnp.float32) * slope).astype(jnp.bfloat16)
            fg_ref[...] += lax.dot_general(pg, s_ref[d2], NT, preferred_element_type=jnp.float32)
        return carry

    lax.fori_loop(0, planes2, back_plane, 0)


def per_sample(x, ogn, ogq, w1, w2, w2t, t1, sel2, up):
    depth, c0, cells = x.shape
    c1, c2 = w1.shape[0], w2.shape[0]
    planes1, planes2 = depth // 2, depth // 4
    plane1 = (HEIGHT // 2) * (WIDTH // 2)
    plane2 = ogq.shape[1]
    vmem = pltpu.VMEM
    return pl.pallas_call(
        conv_kernel,
        out_shape=(
            jax.ShapeDtypeStruct((c2, planes2 * plane2), jnp.bfloat16),
            jax.ShapeDtypeStruct((c1, 27 * c0), jnp.float32),
            jax.ShapeDtypeStruct((c2, 27 * c1), jnp.float32),
        ),
        in_specs=[pl.BlockSpec(memory_space=vmem)] * 9,
        out_specs=[pl.BlockSpec(memory_space=vmem)] * 3,
        scratch_shapes=[
            vmem((depth + 1, c0, (cells // 128) * 384), jnp.bfloat16),
            vmem((planes1, 27 * c0, plane1), jnp.bfloat16),
            vmem((planes1, c1, plane1), jnp.float32),
            vmem((planes1 + 1, c1, plane1), jnp.bfloat16),
            vmem((planes1 + 1, c1, 9 * 128), jnp.float32),
            vmem((planes2 // 2, 27 * c1, 128), jnp.bfloat16),
            vmem((planes2 + 1, 9, c2, plane1), jnp.bfloat16),
        ],
        compiler_params=pltpu.CompilerParams(vmem_limit_bytes=60 * 1024 * 1024),
    )(x, ogn, ogq, w1, w2, w2t, t1, sel2, up)


ROUND_ORDER = ((("sample", 1),), (("space", 4),),
               (("sample", 2), ("sample", 4), ("space", 1)), (("space", 2), ("space", 8), ("space", 16)))


def exchange_rounds(axis_sizes):
    sizes = dict(axis_sizes)
    rounds = []
    for group in ROUND_ORDER:
        kept = tuple((axis, bit) for axis, bit in group if bit < sizes[axis])
        if kept:
            rounds.append(kept)
    used = {pair for group in rounds for pair in group}
    for axis, size in axis_sizes:
        bit = 1
        while bit < size:
            if (axis, bit) not in used:
                rounds.append(((axis, bit),))
            bit *= 2
    return rounds


def halvings(rows, rounds):
    count = 0
    while (count < len(rounds) and len(rounds[count]) == 1
           and rows % (2 ** (count + 1) * 8) == 0):
        count += 1
    return count


def allreduce_kernel(axis_order, rounds, g1_ref, g2_ref, t1_ref, t2_ref, o1_ref, o2_ref, r1_ref, r2_ref,
                     a1_ref, a2_ref, x1_ref, x2_ref, send_sem, recv_sem, gather_sem):
    me = {axis: lax.axis_index(axis) for axis in axis_order}

    def bit_of(axis, bit):
        return (me[axis] // bit) % 2

    plan_rounds = []
    for group in rounds:
        own = sum(bit_of(axis, bit) * 2 ** idx for idx, (axis, bit) in enumerate(group))
        members = []
        for t in range(1, 2 ** len(group)):
            there = dict(me)
            slot = 0
            for idx, (axis, bit) in enumerate(group):
                flip = (t // 2 ** idx) % 2
                if flip:
                    there[axis] = there[axis] + bit - 2 * bit * bit_of(axis, bit)
                slot = slot + ((bit_of(axis, bit) + flip) % 2) * 2 ** idx
            members.append((t, slot, tuple(there[a] for a in axis_order)))
        plan_rounds.append((group, own, members))

    barrier = pltpu.get_barrier_semaphore()
    count = 0
    for group, own, members in plan_rounds:
        for t, slot, device in members:
            pl.semaphore_signal(barrier, 1, device_id=device, device_id_type=pl.DeviceIdType.MESH)
            count += 1
    pl.semaphore_wait(barrier, count)

    accs = (o1_ref, o2_ref)
    recvs = (r1_ref, r2_ref)
    gathers = (a1_ref, a2_ref)
    groups = (x1_ref, x2_ref)
    o1_ref[...] = g1_ref[...]
    o2_ref[...] = g2_ref[...]
    plans = [{"rows": acc.shape[0], "h": halvings(acc.shape[0], rounds), "off": 0, "kept": []} for acc in accs]

    def remote(src, dst, send, recv, device):
        return pltpu.make_async_remote_copy(
            src_ref=src, dst_ref=dst, send_sem=send, recv_sem=recv,
            device_id=device, device_id_type=pl.DeviceIdType.MESH)

    for r, (group, own, members) in enumerate(plan_rounds):
        sends, recvs_wait, after = [], [], []
        for k, (acc, recv, xbuf, plan) in enumerate(zip(accs, recvs, groups, plans)):
            if r < plan["h"]:
                (axis, bit), = group
                t, slot, device = members[0]
                mine = bit_of(axis, bit)
                half = plan["rows"] // 2
                keep = pl.multiple_of(plan["off"] + mine * half, 8)
                give = pl.multiple_of(plan["off"] + (1 - mine) * half, 8)
                copy = remote(acc.at[pl.ds(give, half)], recv.at[r, pl.ds(0, half)],
                              send_sem.at[r, 0, k], recv_sem.at[r, 0, k], device)
                sends.append(copy)
                recvs_wait.append(copy)
                after.append(("add", acc, recv, r, keep, half))
                plan["kept"].append((r, keep, give, half))
                plan["off"], plan["rows"] = keep, half
            else:
                rows, off = plan["rows"], plan["off"]
                xbuf[r, own] = acc[pl.ds(off, rows)]
                for t, slot, device in members:
                    sends.append(remote(acc.at[pl.ds(off, rows)], xbuf.at[r, own],
                                        send_sem.at[r, t, k], recv_sem.at[r, own, k], device))
                    recvs_wait.append(remote(acc.at[pl.ds(off, rows)], xbuf.at[r, slot],
                                             send_sem.at[r, t, k], recv_sem.at[r, slot, k], device))
                after.append(("sum", acc, xbuf, r, off, rows, 2 ** len(group)))
        for copy in sends:
            copy.start()
        for copy in sends:
            copy.wait_send()
        for copy in recvs_wait:
            copy.wait_recv()
        for item in after:
            if item[0] == "add":
                _, acc, recv, slot_r, off, rows = item
                acc[pl.ds(off, rows)] = acc[pl.ds(off, rows)] + recv[slot_r, pl.ds(0, rows)]
            else:
                _, acc, xbuf, slot_r, off, rows, n_members = item
                total = xbuf[slot_r, 0]
                for q in range(1, n_members):
                    total = total + xbuf[slot_r, q]
                acc[pl.ds(off, rows)] = total

    for r in reversed(range(len(plan_rounds))):
        copies, places = [], []
        group, own, members = plan_rounds[r]
        for k, (acc, gather, plan) in enumerate(zip(accs, gathers, plans)):
            for step, keep, give, half in plan["kept"]:
                if step == r:
                    t, slot, device = members[0]
                    copies.append(remote(acc.at[pl.ds(keep, half)], gather.at[r, pl.ds(0, half)],
                                         gather_sem.at[r, 0, k], gather_sem.at[r, 1, k], device))
                    places.append((acc, gather, give, half))
        for copy in copies:
            copy.start()
        for copy in copies:
            copy.wait()
        for acc, gather, give, half in places:
            acc[pl.ds(give, half)] = gather[r, pl.ds(0, half)]
    t1_ref[...] = o1_ref[...].T
    t2_ref[...] = o2_ref[...].T


def allreduce(g1, g2, axis_order, axis_sizes):
    rounds = exchange_rounds(axis_sizes)
    n = len(rounds)
    width = max(2 ** len(group) for group in rounds)
    vmem = pltpu.VMEM
    chunk = [g.shape[0] // 2 ** halvings(g.shape[0], rounds) for g in (g1, g2)]
    return pl.pallas_call(
        functools.partial(allreduce_kernel, axis_order, rounds),
        out_shape=(jax.ShapeDtypeStruct(g1.shape[::-1], g1.dtype), jax.ShapeDtypeStruct(g2.shape[::-1], g2.dtype)),
        in_specs=[pl.BlockSpec(memory_space=vmem)] * 2,
        out_specs=[pl.BlockSpec(memory_space=vmem)] * 2,
        scratch_shapes=[
            vmem(g1.shape, g1.dtype),
            vmem(g2.shape, g2.dtype),
            vmem((n, g1.shape[0] // 2) + g1.shape[1:], g1.dtype),
            vmem((n, g2.shape[0] // 2) + g2.shape[1:], g2.dtype),
            vmem((n, g1.shape[0] // 2) + g1.shape[1:], g1.dtype),
            vmem((n, g2.shape[0] // 2) + g2.shape[1:], g2.dtype),
            vmem((n, width, chunk[0]) + g1.shape[1:], g1.dtype),
            vmem((n, width, chunk[1]) + g2.shape[1:], g2.dtype),
            pltpu.SemaphoreType.DMA((n, width, 2)),
            pltpu.SemaphoreType.DMA((n, width, 2)),
            pltpu.SemaphoreType.DMA((n, 2, 2)),
        ],
        compiler_params=pltpu.CompilerParams(collective_id=0, has_side_effects=True),
    )(g1, g2)


def body(axis_order, axis_sizes, crops, first_kernel, second_kernel, out_grad):
    local_samples, channels_in, planes, flat_cells = crops.shape
    whole_input = lax.all_to_all(crops, "space", split_axis=0, concat_axis=2, tiled=True)
    x = whole_input[0].transpose(1, 0, 2)
    c1, c2 = first_kernel.shape[0], second_kernel.shape[0]
    og = out_grad[0]
    ogn = og.reshape(c2, -1)
    ogq = og.transpose(1, 0, 2).reshape(-1, og.shape[2])
    w1 = first_kernel.transpose(0, 2, 3, 4, 1).reshape(c1, -1)
    w2 = second_kernel.transpose(0, 2, 3, 4, 1).reshape(c2, -1)
    w2t = second_kernel.transpose(2, 1, 3, 4, 0).reshape(3, c1, -1)
    t1, sel2, up = selection_tables(WIDTH, HEIGHT // 2, WIDTH // 2)
    feat, fg, sg = per_sample(
        x, ogn, ogq, w1, w2, w2t,
        jnp.asarray(t1, jnp.bfloat16), jnp.asarray(sel2, jnp.bfloat16), jnp.asarray(up, jnp.bfloat16),
    )
    features_out = feat.reshape(out_grad.shape)
    fg, sg = allreduce(fg, sg, axis_order, axis_sizes)
    first_grad = fg.reshape(3, 3, 3, channels_in, c1).transpose(4, 3, 0, 1, 2)
    second_grad = sg.reshape(3, 3, 3, c1, c2).transpose(4, 3, 0, 1, 2)
    return (features_out, first_grad, second_grad)


def solution(mesh):
    placed = (P("sample", None, "space", None), P(), P(), P(("sample", "space"), None, None, None))
    axis_order = tuple(mesh.axis_names)
    axis_sizes = [(a, mesh.shape[a]) for a in ("sample", "space")]
    return jax.shard_map(
        functools.partial(body, axis_order, axis_sizes),
        mesh=mesh,
        in_specs=placed,
        out_specs=(P(("sample", "space"), None, None, None), P(), P()),
        check_vma=False,
    )
```

```python
import functools

import numpy as np

import jax
import jax.numpy as jnp
from jax import lax
from jax.experimental import pallas as pl
from jax.experimental.pallas import tpu as pltpu
from jax.sharding import PartitionSpec as P

HEIGHT = 8
WIDTH = 128

NT = (((1,), (1,)), ((), ()))


def selection_tables(c0_w, c1_h, c1_w):
    t1 = np.zeros((c0_w, 3 * 128), np.float32)
    for c in range(3):
        for pw in range(c0_w // 2):
            w = 2 * pw + c - 1
            if 0 <= w < c0_w:
                t1[w, c * 128 + pw] = 1.0
    q_h, q_w = c1_h // 2, c1_w // 2
    sel2 = np.zeros((c1_h * c1_w, 9 * 128), np.float32)
    up = np.zeros((q_h * q_w, 9 * c1_h * c1_w), np.float32)
    for b in range(3):
        for c in range(3):
            bc = b * 3 + c
            for qh in range(q_h):
                for qw in range(q_w):
                    h2, w2 = 2 * qh + b - 1, 2 * qw + c - 1
                    if 0 <= h2 < c1_h and 0 <= w2 < c1_w:
                        sel2[h2 * c1_w + w2, bc * 128 + qh * q_w + qw] = 1.0
                        up[qh * q_w + qw, bc * c1_h * c1_w + h2 * c1_w + w2] = 1.0
    return t1, sel2, up


def act_kernel(ogq_ref, w2t_ref, up_ref, act_ref, v_ref):
    planes2 = v_ref.shape[0] - 1
    c2 = v_ref.shape[2]
    span = up_ref.shape[1] // 9
    v_ref[planes2] = jnp.zeros(v_ref.shape[1:], v_ref.dtype)
    for bc in range(9):
        u = jnp.dot(ogq_ref[...], up_ref[:, bc * span:(bc + 1) * span], preferred_element_type=jnp.float32)
        v_ref[pl.ds(0, planes2), bc] = u.astype(v_ref.dtype).reshape(planes2, c2, span)

    def plane(q, carry):
        vq = v_ref[q].reshape(9 * c2, span)
        vq1 = v_ref[q + 1].reshape(9 * c2, span)
        even = jnp.dot(w2t_ref[1], vq, preferred_element_type=jnp.float32)
        odd = (jnp.dot(w2t_ref[2], vq, preferred_element_type=jnp.float32)
               + jnp.dot(w2t_ref[0], vq1, preferred_element_type=jnp.float32))
        act_ref[2 * q] = even.astype(act_ref.dtype)
        act_ref[2 * q + 1] = odd.astype(act_ref.dtype)
        return carry

    lax.fori_loop(0, planes2, plane, 0)


def act_grad_of(ogq, w2t, up):
    c2 = w2t.shape[2] // 9
    planes2 = ogq.shape[0] // c2
    c1 = w2t.shape[1]
    span = up.shape[1] // 9
    vmem = pltpu.VMEM
    flops = 2 * ogq.shape[0] * ogq.shape[1] * up.shape[1] + 2 * 3 * 2 * planes2 * c1 * 9 * c2 * span
    return pl.pallas_call(
        act_kernel,
        out_shape=jax.ShapeDtypeStruct((2 * planes2, c1, span), jnp.bfloat16),
        in_specs=[pl.BlockSpec(memory_space=vmem)] * 3,
        out_specs=pl.BlockSpec(memory_space=vmem),
        scratch_shapes=[vmem((planes2 + 1, 9, c2, span), jnp.bfloat16)],
        compiler_params=pltpu.CompilerParams(vmem_limit_bytes=32 * 1024 * 1024),
        cost_estimate=pl.CostEstimate(flops=flops, transcendentals=0,
                                      bytes_accessed=2 * (ogq.size + w2t.size + up.size + 2 * planes2 * c1 * span)),
    )(ogq, w2t, up)


def conv_kernel(x_ref, ogn_ref, act_ref, w1_ref, w2_ref, t1_ref, sel2_ref,
                feat_ref, fg_ref, sg_ref,
                q1_ref, s_ref, fp_ref, a2_ref, q2_ref, s2_ref):
    depth, c0, cells = x_ref.shape
    n_h = cells // 128
    c1 = w1_ref.shape[0]
    c2 = w2_ref.shape[0]
    planes1 = depth // 2
    plane1 = s_ref.shape[2]
    planes2 = planes1 // 2

    q1_ref[0] = jnp.zeros(q1_ref.shape[1:], q1_ref.dtype)
    for h in range(n_h):
        xh = x_ref[:, :, h * 128:(h + 1) * 128].reshape(depth * c0, 128)
        qh = jnp.dot(xh, t1_ref[...], preferred_element_type=jnp.float32)
        q1_ref[pl.ds(1, depth), :, h * 384:(h + 1) * 384] = qh.astype(q1_ref.dtype).reshape(depth, c0, 384)

    a2_ref[0] = jnp.zeros(a2_ref.shape[1:], a2_ref.dtype)

    def build_plane(pd, carry):
        for a in range(3):
            for b in range(3):
                for c in range(3):
                    r0 = ((a * 3 + b) * 3 + c) * c0
                    for m in range(plane1 // 128):
                        h_lo, h_hi = 4 * m + b - 1, 4 * m + b + 1
                        hi = q1_ref[2 * pd + a, :, pl.ds((h_hi * 3 + c) * 128, 128)].astype(jnp.float32)
                        val = pltpu.roll(hi, 64, 1)
                        if h_lo >= 0:
                            val = val + q1_ref[2 * pd + a, :, pl.ds((h_lo * 3 + c) * 128, 128)].astype(jnp.float32)
                        s_ref[pd, pl.ds(r0, c0), pl.ds(m * 128, 128)] = val.astype(s_ref.dtype)
        pre = jnp.dot(w1_ref[...], s_ref[pd], preferred_element_type=jnp.float32)
        sig = 1.0 / (1.0 + jnp.exp(-pre))
        fp_ref[pd] = sig * (1.0 + pre * (1.0 - sig))
        a2_ref[pd + 1] = (pre * sig).astype(a2_ref.dtype)
        return carry

    lax.fori_loop(0, planes1, build_plane, 0)

    a2 = a2_ref[...].reshape((planes1 + 1) * c1, plane1)
    for bc in range(9):
        q2 = jnp.dot(a2, sel2_ref[:, bc * 128:(bc + 1) * 128], preferred_element_type=jnp.float32)
        q2_ref[:, :, bc * 128:(bc + 1) * 128] = q2.reshape(planes1 + 1, c1, 128)

    sg_ref[...] = jnp.zeros(sg_ref.shape, sg_ref.dtype)
    for n in range(planes2 // 2):
        for a in range(3):
            for bc in range(9):
                r0 = (a * 9 + bc) * c1
                lo = q2_ref[4 * n + a, :, bc * 128:(bc + 1) * 128]
                hi = q2_ref[4 * n + a + 2, :, bc * 128:(bc + 1) * 128]
                s2_ref[n, r0:r0 + c1, :] = (lo + pltpu.roll(hi, 64, 1)).astype(s2_ref.dtype)
        feat = jnp.dot(w2_ref[...], s2_ref[n], preferred_element_type=jnp.float32)
        feat_ref[:, n * 128:(n + 1) * 128] = feat.astype(feat_ref.dtype)
        sg_ref[...] += lax.dot_general(ogn_ref[:, n * 128:(n + 1) * 128], s2_ref[n], NT,
                                       preferred_element_type=jnp.float32)

    fg_ref[...] = jnp.zeros(fg_ref.shape, fg_ref.dtype)

    def back_plane(d2, carry):
        slope = fp_ref[d2]
        pg = (act_ref[d2].astype(jnp.float32) * slope).astype(jnp.bfloat16)
        fg_ref[...] += lax.dot_general(pg, s_ref[d2], NT, preferred_element_type=jnp.float32)
        return carry

    lax.fori_loop(0, planes1, back_plane, 0)


def per_sample(x, ogn, act, w1, w2, t1, sel2):
    depth, c0, cells = x.shape
    c1, c2 = w1.shape[0], w2.shape[0]
    planes1, planes2 = depth // 2, depth // 4
    plane1 = (HEIGHT // 2) * (WIDTH // 2)
    plane2 = ogn.shape[1] // planes2
    vmem = pltpu.VMEM
    return pl.pallas_call(
        conv_kernel,
        out_shape=(
            jax.ShapeDtypeStruct((c2, planes2 * plane2), jnp.bfloat16),
            jax.ShapeDtypeStruct((c1, 27 * c0), jnp.float32),
            jax.ShapeDtypeStruct((c2, 27 * c1), jnp.float32),
        ),
        in_specs=[pl.BlockSpec(memory_space=vmem)] * 7,
        out_specs=[pl.BlockSpec(memory_space=vmem)] * 3,
        scratch_shapes=[
            vmem((depth + 1, c0, (cells // 128) * 384), jnp.bfloat16),
            vmem((planes1, 27 * c0, plane1), jnp.bfloat16),
            vmem((planes1, c1, plane1), jnp.float32),
            vmem((planes1 + 1, c1, plane1), jnp.bfloat16),
            vmem((planes1 + 1, c1, 9 * 128), jnp.float32),
            vmem((planes2 // 2, 27 * c1, 128), jnp.bfloat16),
        ],
        compiler_params=pltpu.CompilerParams(vmem_limit_bytes=60 * 1024 * 1024),
    )(x, ogn, act, w1, w2, t1, sel2)


ROUND_ORDER = ((("sample", 1),), (("space", 4),), (("sample", 2),),
               (("space", 1), ("space", 2), ("sample", 4)), (("space", 8), ("space", 16)))


def exchange_rounds(axis_sizes):
    sizes = dict(axis_sizes)
    rounds = []
    for group in ROUND_ORDER:
        kept = tuple((axis, bit) for axis, bit in group if bit < sizes[axis])
        if kept:
            rounds.append(kept)
    used = {pair for group in rounds for pair in group}
    for axis, size in axis_sizes:
        bit = 1
        while bit < size:
            if (axis, bit) not in used:
                rounds.append(((axis, bit),))
            bit *= 2
    return rounds


def halvings(rows, rounds):
    count = 0
    while (count < len(rounds) and len(rounds[count]) == 1
           and rows % (2 ** (count + 1) * 8) == 0):
        count += 1
    return count


def allreduce_kernel(axis_order, rounds, g1_ref, g2_ref, t1_ref, t2_ref, o1_ref, o2_ref, r1_ref, r2_ref,
                     a1_ref, a2_ref, x1_ref, x2_ref, send_sem, recv_sem, gather_sem):
    me = {axis: lax.axis_index(axis) for axis in axis_order}

    def bit_of(axis, bit):
        return (me[axis] // bit) % 2

    plan_rounds = []
    for group in rounds:
        own = sum(bit_of(axis, bit) * 2 ** idx for idx, (axis, bit) in enumerate(group))
        members = []
        for t in range(1, 2 ** len(group)):
            there = dict(me)
            slot = 0
            for idx, (axis, bit) in enumerate(group):
                flip = (t // 2 ** idx) % 2
                if flip:
                    there[axis] = there[axis] + bit - 2 * bit * bit_of(axis, bit)
                slot = slot + ((bit_of(axis, bit) + flip) % 2) * 2 ** idx
            members.append((t, slot, tuple(there[a] for a in axis_order)))
        plan_rounds.append((group, own, members))

    barrier = pltpu.get_barrier_semaphore()
    count = 0
    for group, own, members in plan_rounds:
        for t, slot, device in members:
            pl.semaphore_signal(barrier, 1, device_id=device, device_id_type=pl.DeviceIdType.MESH)
            count += 1
    pl.semaphore_wait(barrier, count)

    accs = (o1_ref, o2_ref)
    recvs = (r1_ref, r2_ref)
    gathers = (a1_ref, a2_ref)
    groups = (x1_ref, x2_ref)
    o1_ref[...] = g1_ref[...]
    o2_ref[...] = g2_ref[...]
    plans = [{"rows": acc.shape[0], "h": halvings(acc.shape[0], rounds), "off": 0, "kept": []} for acc in accs]

    def remote(src, dst, send, recv, device):
        return pltpu.make_async_remote_copy(
            src_ref=src, dst_ref=dst, send_sem=send, recv_sem=recv,
            device_id=device, device_id_type=pl.DeviceIdType.MESH)

    for r, (group, own, members) in enumerate(plan_rounds):
        sends, recvs_wait, after = [], [], []
        for k, (acc, recv, xbuf, plan) in enumerate(zip(accs, recvs, groups, plans)):
            if r < plan["h"]:
                (axis, bit), = group
                t, slot, device = members[0]
                mine = bit_of(axis, bit)
                half = plan["rows"] // 2
                keep = pl.multiple_of(plan["off"] + mine * half, 8)
                give = pl.multiple_of(plan["off"] + (1 - mine) * half, 8)
                copy = remote(acc.at[pl.ds(give, half)], recv.at[r, pl.ds(0, half)],
                              send_sem.at[r, 0, k], recv_sem.at[r, 0, k], device)
                sends.append(copy)
                recvs_wait.append(copy)
                after.append(("add", acc, recv, r, keep, half))
                plan["kept"].append((r, keep, give, half))
                plan["off"], plan["rows"] = keep, half
            else:
                rows, off = plan["rows"], plan["off"]
                xbuf[r, own] = acc[pl.ds(off, rows)]
                for t, slot, device in members:
                    sends.append(remote(acc.at[pl.ds(off, rows)], xbuf.at[r, own],
                                        send_sem.at[r, t, k], recv_sem.at[r, own, k], device))
                    recvs_wait.append(remote(acc.at[pl.ds(off, rows)], xbuf.at[r, slot],
                                             send_sem.at[r, t, k], recv_sem.at[r, slot, k], device))
                after.append(("sum", acc, xbuf, r, off, rows, 2 ** len(group)))
        for copy in sends:
            copy.start()
        for copy in sends:
            copy.wait_send()
        for copy in recvs_wait:
            copy.wait_recv()
        for item in after:
            if item[0] == "add":
                _, acc, recv, slot_r, off, rows = item
                acc[pl.ds(off, rows)] = acc[pl.ds(off, rows)] + recv[slot_r, pl.ds(0, rows)]
            else:
                _, acc, xbuf, slot_r, off, rows, n_members = item
                total = xbuf[slot_r, 0]
                for q in range(1, n_members):
                    total = total + xbuf[slot_r, q]
                acc[pl.ds(off, rows)] = total

    for r in reversed(range(len(plan_rounds))):
        copies, places = [], []
        group, own, members = plan_rounds[r]
        for k, (acc, gather, plan) in enumerate(zip(accs, gathers, plans)):
            for step, keep, give, half in plan["kept"]:
                if step == r:
                    t, slot, device = members[0]
                    copies.append(remote(acc.at[pl.ds(keep, half)], gather.at[r, pl.ds(0, half)],
                                         gather_sem.at[r, 0, k], gather_sem.at[r, 1, k], device))
                    places.append((acc, gather, give, half))
        for copy in copies:
            copy.start()
        for copy in copies:
            copy.wait()
        for acc, gather, give, half in places:
            acc[pl.ds(give, half)] = gather[r, pl.ds(0, half)]
    t1_ref[...] = o1_ref[...].T
    t2_ref[...] = o2_ref[...].T


def allreduce(g1, g2, axis_order, axis_sizes):
    rounds = exchange_rounds(axis_sizes)
    n = len(rounds)
    width = max(2 ** len(group) for group in rounds)
    vmem = pltpu.VMEM
    chunk = [g.shape[0] // 2 ** halvings(g.shape[0], rounds) for g in (g1, g2)]
    return pl.pallas_call(
        functools.partial(allreduce_kernel, axis_order, rounds),
        out_shape=(jax.ShapeDtypeStruct(g1.shape[::-1], g1.dtype), jax.ShapeDtypeStruct(g2.shape[::-1], g2.dtype)),
        in_specs=[pl.BlockSpec(memory_space=vmem)] * 2,
        out_specs=[pl.BlockSpec(memory_space=vmem)] * 2,
        scratch_shapes=[
            vmem(g1.shape, g1.dtype),
            vmem(g2.shape, g2.dtype),
            vmem((n, g1.shape[0] // 2) + g1.shape[1:], g1.dtype),
            vmem((n, g2.shape[0] // 2) + g2.shape[1:], g2.dtype),
            vmem((n, g1.shape[0] // 2) + g1.shape[1:], g1.dtype),
            vmem((n, g2.shape[0] // 2) + g2.shape[1:], g2.dtype),
            vmem((n, width, chunk[0]) + g1.shape[1:], g1.dtype),
            vmem((n, width, chunk[1]) + g2.shape[1:], g2.dtype),
            pltpu.SemaphoreType.DMA((n, width, 2)),
            pltpu.SemaphoreType.DMA((n, width, 2)),
            pltpu.SemaphoreType.DMA((n, 2, 2)),
        ],
        compiler_params=pltpu.CompilerParams(collective_id=0, has_side_effects=True),
    )(g1, g2)


def body(axis_order, axis_sizes, crops, first_kernel, second_kernel, out_grad):
    local_samples, channels_in, planes, flat_cells = crops.shape
    whole_input = lax.all_to_all(crops, "space", split_axis=0, concat_axis=2, tiled=True)
    x = whole_input[0].transpose(1, 0, 2)
    c1, c2 = first_kernel.shape[0], second_kernel.shape[0]
    og = out_grad[0]
    ogn = og.reshape(c2, -1)
    ogq = og.transpose(1, 0, 2).reshape(-1, og.shape[2])
    w1 = first_kernel.transpose(0, 2, 3, 4, 1).reshape(c1, -1)
    w2 = second_kernel.transpose(0, 2, 3, 4, 1).reshape(c2, -1)
    w2t = second_kernel.transpose(2, 1, 3, 4, 0).reshape(3, c1, -1)
    t1, sel2, up = selection_tables(WIDTH, HEIGHT // 2, WIDTH // 2)
    act = act_grad_of(ogq, w2t, jnp.asarray(up, jnp.bfloat16))
    feat, fg, sg = per_sample(x, ogn, act, w1, w2, jnp.asarray(t1, jnp.bfloat16), jnp.asarray(sel2, jnp.bfloat16))
    features_out = feat.reshape(out_grad.shape)
    fg, sg = allreduce(fg, sg, axis_order, axis_sizes)
    first_grad = fg.reshape(3, 3, 3, channels_in, c1).transpose(4, 3, 0, 1, 2)
    second_grad = sg.reshape(3, 3, 3, c1, c2).transpose(4, 3, 0, 1, 2)
    return (features_out, first_grad, second_grad)


def solution(mesh):
    placed = (P("sample", None, "space", None), P(), P(), P(("sample", "space"), None, None, None))
    axis_order = tuple(mesh.axis_names)
    axis_sizes = [(a, mesh.shape[a]) for a in ("sample", "space")]
    return jax.shard_map(
        functools.partial(body, axis_order, axis_sizes),
        mesh=mesh,
        in_specs=placed,
        out_specs=(P(("sample", "space"), None, None, None), P(), P()),
        check_vma=False,
    )
```

```python
import functools

import numpy as np

import jax
import jax.numpy as jnp
from jax import lax
from jax.experimental import pallas as pl
from jax.experimental.pallas import tpu as pltpu
from jax.sharding import PartitionSpec as P

HEIGHT = 8
WIDTH = 128

NT = (((1,), (1,)), ((), ()))


def selection_tables(c0_w, c1_h, c1_w):
    t1 = np.zeros((c0_w, 3 * 128), np.float32)
    for c in range(3):
        for pw in range(c0_w // 2):
            w = 2 * pw + c - 1
            if 0 <= w < c0_w:
                t1[w, c * 128 + pw] = 1.0
    q_h, q_w = c1_h // 2, c1_w // 2
    sel2 = np.zeros((c1_h * c1_w, 9 * 128), np.float32)
    up = np.zeros((q_h * q_w, 9 * c1_h * c1_w), np.float32)
    for b in range(3):
        for c in range(3):
            bc = b * 3 + c
            for qh in range(q_h):
                for qw in range(q_w):
                    h2, w2 = 2 * qh + b - 1, 2 * qw + c - 1
                    if 0 <= h2 < c1_h and 0 <= w2 < c1_w:
                        sel2[h2 * c1_w + w2, bc * 128 + qh * q_w + qw] = 1.0
                        up[qh * q_w + qw, bc * c1_h * c1_w + h2 * c1_w + w2] = 1.0
    return t1, sel2, up


def act_kernel(ogq_ref, w2t_ref, up_ref, act_ref, v_ref):
    planes2 = v_ref.shape[0] - 1
    c2 = v_ref.shape[2]
    span = up_ref.shape[1] // 9
    v_ref[planes2] = jnp.zeros(v_ref.shape[1:], v_ref.dtype)
    for bc in range(9):
        u = jnp.dot(ogq_ref[...], up_ref[:, bc * span:(bc + 1) * span], preferred_element_type=jnp.float32)
        v_ref[pl.ds(0, planes2), bc] = u.astype(v_ref.dtype).reshape(planes2, c2, span)

    def plane(q, carry):
        vq = v_ref[q].reshape(9 * c2, span)
        vq1 = v_ref[q + 1].reshape(9 * c2, span)
        even = jnp.dot(w2t_ref[1], vq, preferred_element_type=jnp.float32)
        odd = (jnp.dot(w2t_ref[2], vq, preferred_element_type=jnp.float32)
               + jnp.dot(w2t_ref[0], vq1, preferred_element_type=jnp.float32))
        act_ref[2 * q] = even.astype(act_ref.dtype)
        act_ref[2 * q + 1] = odd.astype(act_ref.dtype)
        return carry

    lax.fori_loop(0, planes2, plane, 0)


def act_grad_of(ogq, w2t, up):
    c2 = w2t.shape[2] // 9
    planes2 = ogq.shape[0] // c2
    c1 = w2t.shape[1]
    span = up.shape[1] // 9
    vmem = pltpu.VMEM
    flops = 2 * ogq.shape[0] * ogq.shape[1] * up.shape[1] + 2 * 3 * 2 * planes2 * c1 * 9 * c2 * span
    return pl.pallas_call(
        act_kernel,
        out_shape=jax.ShapeDtypeStruct((2 * planes2, c1, span), jnp.bfloat16),
        in_specs=[pl.BlockSpec(memory_space=vmem)] * 3,
        out_specs=pl.BlockSpec(memory_space=vmem),
        scratch_shapes=[vmem((planes2 + 1, 9, c2, span), jnp.bfloat16)],
        compiler_params=pltpu.CompilerParams(vmem_limit_bytes=32 * 1024 * 1024),
        cost_estimate=pl.CostEstimate(flops=flops, transcendentals=0,
                                      bytes_accessed=2 * (ogq.size + w2t.size + up.size + 2 * planes2 * c1 * span)),
    )(ogq, w2t, up)


def conv_kernel(x_ref, ogn_ref, act_ref, w1_ref, w2_ref, t1_ref, sel2_ref,
                feat_ref, fg_ref, sg_ref,
                q1_ref, s_ref, fp_ref, a2_ref, q2_ref, s2_ref):
    depth, c0, cells = x_ref.shape
    n_h = cells // 128
    c1 = w1_ref.shape[0]
    c2 = w2_ref.shape[0]
    planes1 = depth // 2
    plane1 = s_ref.shape[2]
    planes2 = planes1 // 2

    q1_ref[0] = jnp.zeros(q1_ref.shape[1:], q1_ref.dtype)
    for h in range(n_h):
        xh = x_ref[:, :, h * 128:(h + 1) * 128].reshape(depth * c0, 128)
        qh = jnp.dot(xh, t1_ref[...], preferred_element_type=jnp.float32)
        q1_ref[pl.ds(1, depth), :, h * 384:(h + 1) * 384] = qh.astype(q1_ref.dtype).reshape(depth, c0, 384)

    a2_ref[0] = jnp.zeros(a2_ref.shape[1:], a2_ref.dtype)

    def build_plane(pd, carry):
        for a in range(3):
            for b in range(3):
                for c in range(3):
                    r0 = ((a * 3 + b) * 3 + c) * c0
                    for m in range(plane1 // 128):
                        h_lo, h_hi = 4 * m + b - 1, 4 * m + b + 1
                        hi = q1_ref[2 * pd + a, :, pl.ds((h_hi * 3 + c) * 128, 128)].astype(jnp.float32)
                        val = pltpu.roll(hi, 64, 1)
                        if h_lo >= 0:
                            val = val + q1_ref[2 * pd + a, :, pl.ds((h_lo * 3 + c) * 128, 128)].astype(jnp.float32)
                        s_ref[pd, pl.ds(r0, c0), pl.ds(m * 128, 128)] = val.astype(s_ref.dtype)
        pre = jnp.dot(w1_ref[...], s_ref[pd], preferred_element_type=jnp.float32)
        sig = 1.0 / (1.0 + jnp.exp(-pre))
        fp_ref[pd] = sig * (1.0 + pre * (1.0 - sig))
        a2_ref[pd + 1] = (pre * sig).astype(a2_ref.dtype)
        return carry

    lax.fori_loop(0, planes1, build_plane, 0)

    a2 = a2_ref[...].reshape((planes1 + 1) * c1, plane1)
    for bc in range(9):
        q2 = jnp.dot(a2, sel2_ref[:, bc * 128:(bc + 1) * 128], preferred_element_type=jnp.float32)
        q2_ref[:, :, bc * 128:(bc + 1) * 128] = q2.reshape(planes1 + 1, c1, 128)

    sg_ref[...] = jnp.zeros(sg_ref.shape, sg_ref.dtype)
    for n in range(planes2 // 2):
        for a in range(3):
            for bc in range(9):
                r0 = (a * 9 + bc) * c1
                lo = q2_ref[4 * n + a, :, bc * 128:(bc + 1) * 128]
                hi = q2_ref[4 * n + a + 2, :, bc * 128:(bc + 1) * 128]
                s2_ref[n, r0:r0 + c1, :] = (lo + pltpu.roll(hi, 64, 1)).astype(s2_ref.dtype)
        feat = jnp.dot(w2_ref[...], s2_ref[n], preferred_element_type=jnp.float32)
        feat_ref[:, n * 128:(n + 1) * 128] = feat.astype(feat_ref.dtype)
        sg_ref[...] += lax.dot_general(ogn_ref[:, n * 128:(n + 1) * 128], s2_ref[n], NT,
                                       preferred_element_type=jnp.float32)

    fg_ref[...] = jnp.zeros(fg_ref.shape, fg_ref.dtype)

    def back_plane(d2, carry):
        slope = fp_ref[d2]
        pg = (act_ref[d2].astype(jnp.float32) * slope).astype(jnp.bfloat16)
        fg_ref[...] += lax.dot_general(pg, s_ref[d2], NT, preferred_element_type=jnp.float32)
        return carry

    lax.fori_loop(0, planes1, back_plane, 0)


def per_sample(x, ogn, act, w1, w2, t1, sel2):
    depth, c0, cells = x.shape
    c1, c2 = w1.shape[0], w2.shape[0]
    planes1, planes2 = depth // 2, depth // 4
    plane1 = (HEIGHT // 2) * (WIDTH // 2)
    plane2 = ogn.shape[1] // planes2
    vmem = pltpu.VMEM
    return pl.pallas_call(
        conv_kernel,
        out_shape=(
            jax.ShapeDtypeStruct((c2, planes2 * plane2), jnp.bfloat16),
            jax.ShapeDtypeStruct((c1, 27 * c0), jnp.float32),
            jax.ShapeDtypeStruct((c2, 27 * c1), jnp.float32),
        ),
        in_specs=[pl.BlockSpec(memory_space=vmem)] * 7,
        out_specs=[pl.BlockSpec(memory_space=vmem)] * 3,
        scratch_shapes=[
            vmem((depth + 1, c0, (cells // 128) * 384), jnp.bfloat16),
            vmem((planes1, 27 * c0, plane1), jnp.bfloat16),
            vmem((planes1, c1, plane1), jnp.float32),
            vmem((planes1 + 1, c1, plane1), jnp.bfloat16),
            vmem((planes1 + 1, c1, 9 * 128), jnp.float32),
            vmem((planes2 // 2, 27 * c1, 128), jnp.bfloat16),
        ],
        compiler_params=pltpu.CompilerParams(vmem_limit_bytes=60 * 1024 * 1024),
    )(x, ogn, act, w1, w2, t1, sel2)


ROUND_ORDER = ((("sample", 1),), (("space", 4),), (("sample", 2),),
               (("space", 1), ("space", 2), ("sample", 4)), (("space", 8), ("space", 16)))


def exchange_rounds(axis_sizes):
    sizes = dict(axis_sizes)
    rounds = []
    for group in ROUND_ORDER:
        kept = tuple((axis, bit) for axis, bit in group if bit < sizes[axis])
        if kept:
            rounds.append(kept)
    used = {pair for group in rounds for pair in group}
    for axis, size in axis_sizes:
        bit = 1
        while bit < size:
            if (axis, bit) not in used:
                rounds.append(((axis, bit),))
            bit *= 2
    return rounds


def halvings(rows, rounds):
    count = 0
    while (count < len(rounds) and len(rounds[count]) == 1
           and rows % (2 ** (count + 1) * 8) == 0):
        count += 1
    return count


def allreduce_kernel(axis_order, rounds, g1_ref, g2_ref, t1_ref, t2_ref, o1_ref, o2_ref, r1_ref, r2_ref,
                     a1_ref, a2_ref, x1_ref, x2_ref, send_sem, recv_sem, gather_sem):
    me = {axis: lax.axis_index(axis) for axis in axis_order}

    def bit_of(axis, bit):
        return (me[axis] // bit) % 2

    plan_rounds = []
    for group in rounds:
        own = sum(bit_of(axis, bit) * 2 ** idx for idx, (axis, bit) in enumerate(group))
        members = []
        for t in range(1, 2 ** len(group)):
            there = dict(me)
            slot = 0
            for idx, (axis, bit) in enumerate(group):
                flip = (t // 2 ** idx) % 2
                if flip:
                    there[axis] = there[axis] + bit - 2 * bit * bit_of(axis, bit)
                slot = slot + ((bit_of(axis, bit) + flip) % 2) * 2 ** idx
            members.append((t, slot, tuple(there[a] for a in axis_order)))
        plan_rounds.append((group, own, members))

    def group_members(group):
        own = sum(bit_of(axis, bit) * 2 ** idx for idx, (axis, bit) in enumerate(group))
        members = []
        for t in range(1, 2 ** len(group)):
            there = dict(me)
            slot = 0
            flips = []
            for idx, (axis, bit) in enumerate(group):
                flip = (t // 2 ** idx) % 2
                if flip:
                    there[axis] = there[axis] + bit - 2 * bit * bit_of(axis, bit)
                    flips.append((axis, bit))
                slot = slot + ((bit_of(axis, bit) + flip) % 2) * 2 ** idx
            members.append((t, slot, tuple(there[a] for a in axis_order), frozenset(flips), flips))
        return own, members

    halving_bits = [rounds[r][0] for r in range(max(halvings(acc.shape[0], rounds) for acc in (o1_ref, o2_ref)))]
    seen = {}
    for group, own, members in plan_rounds:
        for t, slot, device in members:
            flips = frozenset((axis, bit) for idx, (axis, bit) in enumerate(group) if (t // 2 ** idx) % 2)
            seen[flips] = device
    for t, slot, device, flips, _ in group_members(halving_bits)[1]:
        seen[flips] = device
    barrier = pltpu.get_barrier_semaphore()
    for device in seen.values():
        pl.semaphore_signal(barrier, 1, device_id=device, device_id_type=pl.DeviceIdType.MESH)
    pl.semaphore_wait(barrier, len(seen))

    accs = (o1_ref, o2_ref)
    recvs = (r1_ref, r2_ref)
    gathers = (a1_ref, a2_ref)
    groups = (x1_ref, x2_ref)
    o1_ref[...] = g1_ref[...]
    o2_ref[...] = g2_ref[...]
    plans = [{"rows": acc.shape[0], "h": halvings(acc.shape[0], rounds), "off": 0, "kept": []} for acc in accs]

    def remote(src, dst, send, recv, device):
        return pltpu.make_async_remote_copy(
            src_ref=src, dst_ref=dst, send_sem=send, recv_sem=recv,
            device_id=device, device_id_type=pl.DeviceIdType.MESH)

    for r, (group, own, members) in enumerate(plan_rounds):
        sends, recvs_wait, after = [], [], []
        for k, (acc, recv, xbuf, plan) in enumerate(zip(accs, recvs, groups, plans)):
            if r < plan["h"]:
                (axis, bit), = group
                t, slot, device = members[0]
                mine = bit_of(axis, bit)
                half = plan["rows"] // 2
                keep = pl.multiple_of(plan["off"] + mine * half, 8)
                give = pl.multiple_of(plan["off"] + (1 - mine) * half, 8)
                copy = remote(acc.at[pl.ds(give, half)], recv.at[r, pl.ds(0, half)],
                              send_sem.at[r, 0, k], recv_sem.at[r, 0, k], device)
                sends.append(copy)
                recvs_wait.append(copy)
                after.append(("add", acc, recv, r, keep, half))
                plan["kept"].append((r, keep, give, half))
                plan["off"], plan["rows"] = keep, half
            else:
                rows, off = plan["rows"], plan["off"]
                xbuf[r, own] = acc[pl.ds(off, rows)]
                for t, slot, device in members:
                    sends.append(remote(acc.at[pl.ds(off, rows)], xbuf.at[r, own],
                                        send_sem.at[r, t, k], recv_sem.at[r, own, k], device))
                    recvs_wait.append(remote(acc.at[pl.ds(off, rows)], xbuf.at[r, slot],
                                             send_sem.at[r, t, k], recv_sem.at[r, slot, k], device))
                after.append(("sum", acc, xbuf, r, off, rows, 2 ** len(group)))
        for copy in sends:
            copy.start()
        for copy in sends:
            copy.wait_send()
        for copy in recvs_wait:
            copy.wait_recv()
        for item in after:
            if item[0] == "add":
                _, acc, recv, slot_r, off, rows = item
                acc[pl.ds(off, rows)] = acc[pl.ds(off, rows)] + recv[slot_r, pl.ds(0, rows)]
            else:
                _, acc, xbuf, slot_r, off, rows, n_members = item
                total = xbuf[slot_r, 0]
                for q in range(1, n_members):
                    total = total + xbuf[slot_r, q]
                acc[pl.ds(off, rows)] = total

    copies, places = [], []
    for k, (acc, gather, plan) in enumerate(zip(accs, gathers, plans)):
        if plan["h"] == 0:
            continue
        bits = [rounds[r][0] for r in range(plan["h"])]
        halves = [half for step, keep, give, half in plan["kept"]]
        own, members = group_members(bits)
        rows, off = plan["rows"], plan["off"]
        for t, slot, device, flips, flip_list in members:
            copies.append((
                remote(acc.at[pl.ds(off, rows)], gather.at[own], gather_sem.at[t, 0, k], gather_sem.at[own, 1, k], device),
                remote(acc.at[pl.ds(off, rows)], gather.at[slot], gather_sem.at[t, 0, k], gather_sem.at[slot, 1, k], device)))
            where = 0
            for idx, (axis, bit) in enumerate(bits):
                flip = 1 if (axis, bit) in flips else 0
                where = where + ((bit_of(axis, bit) + flip) % 2) * halves[idx]
            places.append((acc, gather, slot, pl.multiple_of(where, 8), rows))
    for send, recv in copies:
        send.start()
    for send, recv in copies:
        send.wait_send()
    for send, recv in copies:
        recv.wait_recv()
    for acc, gather, slot, where, rows in places:
        acc[pl.ds(where, rows)] = gather[slot]
    t1_ref[...] = o1_ref[...].T
    t2_ref[...] = o2_ref[...].T


def allreduce(g1, g2, axis_order, axis_sizes):
    rounds = exchange_rounds(axis_sizes)
    n = len(rounds)
    width = max(2 ** len(group) for group in rounds)
    vmem = pltpu.VMEM
    chunk = [g.shape[0] // 2 ** halvings(g.shape[0], rounds) for g in (g1, g2)]
    gwidth = max(2 ** halvings(g.shape[0], rounds) for g in (g1, g2))
    return pl.pallas_call(
        functools.partial(allreduce_kernel, axis_order, rounds),
        out_shape=(jax.ShapeDtypeStruct(g1.shape[::-1], g1.dtype), jax.ShapeDtypeStruct(g2.shape[::-1], g2.dtype)),
        in_specs=[pl.BlockSpec(memory_space=vmem)] * 2,
        out_specs=[pl.BlockSpec(memory_space=vmem)] * 2,
        scratch_shapes=[
            vmem(g1.shape, g1.dtype),
            vmem(g2.shape, g2.dtype),
            vmem((n, g1.shape[0] // 2) + g1.shape[1:], g1.dtype),
            vmem((n, g2.shape[0] // 2) + g2.shape[1:], g2.dtype),
            vmem((gwidth, chunk[0]) + g1.shape[1:], g1.dtype),
            vmem((gwidth, chunk[1]) + g2.shape[1:], g2.dtype),
            vmem((n, width, chunk[0]) + g1.shape[1:], g1.dtype),
            vmem((n, width, chunk[1]) + g2.shape[1:], g2.dtype),
            pltpu.SemaphoreType.DMA((n, width, 2)),
            pltpu.SemaphoreType.DMA((n, width, 2)),
            pltpu.SemaphoreType.DMA((gwidth, 2, 2)),
        ],
        compiler_params=pltpu.CompilerParams(collective_id=0, has_side_effects=True),
    )(g1, g2)


def body(axis_order, axis_sizes, crops, first_kernel, second_kernel, out_grad):
    local_samples, channels_in, planes, flat_cells = crops.shape
    whole_input = lax.all_to_all(crops, "space", split_axis=0, concat_axis=2, tiled=True)
    x = whole_input[0].transpose(1, 0, 2)
    c1, c2 = first_kernel.shape[0], second_kernel.shape[0]
    og = out_grad[0]
    ogn = og.reshape(c2, -1)
    ogq = og.transpose(1, 0, 2).reshape(-1, og.shape[2])
    w1 = first_kernel.transpose(0, 2, 3, 4, 1).reshape(c1, -1)
    w2 = second_kernel.transpose(0, 2, 3, 4, 1).reshape(c2, -1)
    w2t = second_kernel.transpose(2, 1, 3, 4, 0).reshape(3, c1, -1)
    t1, sel2, up = selection_tables(WIDTH, HEIGHT // 2, WIDTH // 2)
    act = act_grad_of(ogq, w2t, jnp.asarray(up, jnp.bfloat16))
    feat, fg, sg = per_sample(x, ogn, act, w1, w2, jnp.asarray(t1, jnp.bfloat16), jnp.asarray(sel2, jnp.bfloat16))
    features_out = feat.reshape(out_grad.shape)
    fg, sg = allreduce(fg, sg, axis_order, axis_sizes)
    first_grad = fg.reshape(3, 3, 3, channels_in, c1).transpose(4, 3, 0, 1, 2)
    second_grad = sg.reshape(3, 3, 3, c1, c2).transpose(4, 3, 0, 1, 2)
    return (features_out, first_grad, second_grad)


def solution(mesh):
    placed = (P("sample", None, "space", None), P(), P(), P(("sample", "space"), None, None, None))
    axis_order = tuple(mesh.axis_names)
    axis_sizes = [(a, mesh.shape[a]) for a in ("sample", "space")]
    return jax.shard_map(
        functools.partial(body, axis_order, axis_sizes),
        mesh=mesh,
        in_specs=placed,
        out_specs=(P(("sample", "space"), None, None, None), P(), P()),
        check_vma=False,
    )
```

```python
import functools

import numpy as np

import jax
import jax.numpy as jnp
from jax import lax
from jax.experimental import pallas as pl
from jax.experimental.pallas import tpu as pltpu
from jax.sharding import PartitionSpec as P

HEIGHT = 8
WIDTH = 128

NT = (((1,), (1,)), ((), ()))


def selection_tables(c0_w, c1_h, c1_w):
    t1 = np.zeros((c0_w, 3 * 128), np.float32)
    for c in range(3):
        for pw in range(c0_w // 2):
            w = 2 * pw + c - 1
            if 0 <= w < c0_w:
                t1[w, c * 128 + pw] = 1.0
    q_h, q_w = c1_h // 2, c1_w // 2
    sel2 = np.zeros((c1_h * c1_w, 9 * 128), np.float32)
    up = np.zeros((q_h * q_w, 9 * c1_h * c1_w), np.float32)
    for b in range(3):
        for c in range(3):
            bc = b * 3 + c
            for qh in range(q_h):
                for qw in range(q_w):
                    h2, w2 = 2 * qh + b - 1, 2 * qw + c - 1
                    if 0 <= h2 < c1_h and 0 <= w2 < c1_w:
                        sel2[h2 * c1_w + w2, bc * 128 + qh * q_w + qw] = 1.0
                        up[qh * q_w + qw, bc * c1_h * c1_w + h2 * c1_w + w2] = 1.0
    return t1, sel2, up


def act_kernel(ogq_ref, w2t_ref, up_ref, act_ref, v_ref):
    planes2 = v_ref.shape[0] - 1
    c2 = v_ref.shape[2]
    span = up_ref.shape[1] // 9
    v_ref[planes2] = jnp.zeros(v_ref.shape[1:], v_ref.dtype)
    for bc in range(9):
        u = jnp.dot(ogq_ref[...], up_ref[:, bc * span:(bc + 1) * span], preferred_element_type=jnp.float32)
        v_ref[pl.ds(0, planes2), bc] = u.astype(v_ref.dtype).reshape(planes2, c2, span)

    def plane(q, carry):
        vq = v_ref[q].reshape(9 * c2, span)
        vq1 = v_ref[q + 1].reshape(9 * c2, span)
        even = jnp.dot(w2t_ref[1], vq, preferred_element_type=jnp.float32)
        odd = (jnp.dot(w2t_ref[2], vq, preferred_element_type=jnp.float32)
               + jnp.dot(w2t_ref[0], vq1, preferred_element_type=jnp.float32))
        act_ref[2 * q] = even.astype(act_ref.dtype)
        act_ref[2 * q + 1] = odd.astype(act_ref.dtype)
        return carry

    lax.fori_loop(0, planes2, plane, 0)


def act_grad_of(ogq, w2t, up):
    c2 = w2t.shape[2] // 9
    planes2 = ogq.shape[0] // c2
    c1 = w2t.shape[1]
    span = up.shape[1] // 9
    vmem = pltpu.VMEM
    flops = 2 * ogq.shape[0] * ogq.shape[1] * up.shape[1] + 2 * 3 * 2 * planes2 * c1 * 9 * c2 * span
    return pl.pallas_call(
        act_kernel,
        out_shape=jax.ShapeDtypeStruct((2 * planes2, c1, span), jnp.bfloat16),
        in_specs=[pl.BlockSpec(memory_space=vmem)] * 3,
        out_specs=pl.BlockSpec(memory_space=vmem),
        scratch_shapes=[vmem((planes2 + 1, 9, c2, span), jnp.bfloat16)],
        compiler_params=pltpu.CompilerParams(vmem_limit_bytes=32 * 1024 * 1024),
        cost_estimate=pl.CostEstimate(flops=flops, transcendentals=0,
                                      bytes_accessed=2 * (ogq.size + w2t.size + up.size + 2 * planes2 * c1 * span)),
    )(ogq, w2t, up)


def conv_kernel(x_ref, ogn_ref, act_ref, w1_ref, w2_ref, t1_ref, sel2_ref,
                feat_ref, fg_ref, sg_ref,
                q1_ref, s_ref, fp_ref, a2_ref, q2_ref, s2_ref):
    depth, c0, cells = x_ref.shape
    n_h = cells // 128
    c1 = w1_ref.shape[0]
    c2 = w2_ref.shape[0]
    planes1 = depth // 2
    plane1 = s_ref.shape[2]
    planes2 = planes1 // 2

    q1_ref[0] = jnp.zeros(q1_ref.shape[1:], q1_ref.dtype)
    for h in range(n_h):
        xh = x_ref[:, :, h * 128:(h + 1) * 128].reshape(depth * c0, 128)
        qh = jnp.dot(xh, t1_ref[...], preferred_element_type=jnp.float32)
        q1_ref[pl.ds(1, depth), :, h * 384:(h + 1) * 384] = qh.astype(q1_ref.dtype).reshape(depth, c0, 384)

    a2_ref[0] = jnp.zeros(a2_ref.shape[1:], a2_ref.dtype)

    def build_plane(pd, carry):
        for a in range(3):
            for b in range(3):
                for c in range(3):
                    r0 = ((a * 3 + b) * 3 + c) * c0
                    for m in range(plane1 // 128):
                        h_lo, h_hi = 4 * m + b - 1, 4 * m + b + 1
                        hi = q1_ref[2 * pd + a, :, pl.ds((h_hi * 3 + c) * 128, 128)].astype(jnp.float32)
                        val = pltpu.roll(hi, 64, 1)
                        if h_lo >= 0:
                            val = val + q1_ref[2 * pd + a, :, pl.ds((h_lo * 3 + c) * 128, 128)].astype(jnp.float32)
                        s_ref[pd, pl.ds(r0, c0), pl.ds(m * 128, 128)] = val.astype(s_ref.dtype)
        pre = jnp.dot(w1_ref[...], s_ref[pd], preferred_element_type=jnp.float32)
        sig = 1.0 / (1.0 + jnp.exp(-pre))
        fp_ref[pd] = sig * (1.0 + pre * (1.0 - sig))
        a2_ref[pd + 1] = (pre * sig).astype(a2_ref.dtype)
        return carry

    lax.fori_loop(0, planes1, build_plane, 0)

    a2 = a2_ref[...].reshape((planes1 + 1) * c1, plane1)
    for bc in range(9):
        q2 = jnp.dot(a2, sel2_ref[:, bc * 128:(bc + 1) * 128], preferred_element_type=jnp.float32)
        q2_ref[:, :, bc * 128:(bc + 1) * 128] = q2.reshape(planes1 + 1, c1, 128)

    sg_ref[...] = jnp.zeros(sg_ref.shape, sg_ref.dtype)
    for n in range(planes2 // 2):
        for a in range(3):
            for bc in range(9):
                r0 = (a * 9 + bc) * c1
                lo = q2_ref[4 * n + a, :, bc * 128:(bc + 1) * 128]
                hi = q2_ref[4 * n + a + 2, :, bc * 128:(bc + 1) * 128]
                s2_ref[n, r0:r0 + c1, :] = (lo + pltpu.roll(hi, 64, 1)).astype(s2_ref.dtype)
        feat = jnp.dot(w2_ref[...], s2_ref[n], preferred_element_type=jnp.float32)
        half = feat_ref.shape[2]
        feat_ref[:, 2 * n, :] = feat[:, :half].astype(feat_ref.dtype)
        feat_ref[:, 2 * n + 1, :] = feat[:, half:].astype(feat_ref.dtype)
        sg_ref[...] += lax.dot_general(ogn_ref[:, n * 128:(n + 1) * 128], s2_ref[n], NT,
                                       preferred_element_type=jnp.float32)

    fg_ref[...] = jnp.zeros(fg_ref.shape, fg_ref.dtype)

    def back_plane(d2, carry):
        slope = fp_ref[d2]
        pg = (act_ref[d2].astype(jnp.float32) * slope).astype(jnp.bfloat16)
        fg_ref[...] += lax.dot_general(pg, s_ref[d2], NT, preferred_element_type=jnp.float32)
        return carry

    lax.fori_loop(0, planes1, back_plane, 0)


def per_sample(x, ogn, act, w1, w2, t1, sel2):
    depth, c0, cells = x.shape
    c1, c2 = w1.shape[0], w2.shape[0]
    planes1, planes2 = depth // 2, depth // 4
    plane1 = (HEIGHT // 2) * (WIDTH // 2)
    plane2 = ogn.shape[1] // planes2
    vmem = pltpu.VMEM
    return pl.pallas_call(
        conv_kernel,
        out_shape=(
            jax.ShapeDtypeStruct((c2, planes2, plane2), jnp.bfloat16),
            jax.ShapeDtypeStruct((c1, 27 * c0), jnp.float32),
            jax.ShapeDtypeStruct((c2, 27 * c1), jnp.float32),
        ),
        in_specs=[pl.BlockSpec(memory_space=vmem)] * 7,
        out_specs=[pl.BlockSpec(memory_space=vmem)] * 3,
        scratch_shapes=[
            vmem((depth + 1, c0, (cells // 128) * 384), jnp.bfloat16),
            vmem((planes1, 27 * c0, plane1), jnp.bfloat16),
            vmem((planes1, c1, plane1), jnp.float32),
            vmem((planes1 + 1, c1, plane1), jnp.bfloat16),
            vmem((planes1 + 1, c1, 9 * 128), jnp.float32),
            vmem((planes2 // 2, 27 * c1, 128), jnp.bfloat16),
        ],
        compiler_params=pltpu.CompilerParams(vmem_limit_bytes=60 * 1024 * 1024),
    )(x, ogn, act, w1, w2, t1, sel2)


ROUND_ORDER = ((("sample", 1),), (("space", 4),), (("sample", 2),),
               (("space", 1), ("space", 2), ("sample", 4)), (("space", 8), ("space", 16)))


def exchange_rounds(axis_sizes):
    sizes = dict(axis_sizes)
    rounds = []
    for group in ROUND_ORDER:
        kept = tuple((axis, bit) for axis, bit in group if bit < sizes[axis])
        if kept:
            rounds.append(kept)
    used = {pair for group in rounds for pair in group}
    for axis, size in axis_sizes:
        bit = 1
        while bit < size:
            if (axis, bit) not in used:
                rounds.append(((axis, bit),))
            bit *= 2
    return rounds


def halvings(rows, rounds):
    count = 0
    while (count < len(rounds) and len(rounds[count]) == 1
           and rows % (2 ** (count + 1) * 8) == 0):
        count += 1
    return count


def allreduce_kernel(axis_order, rounds, g1_ref, g2_ref, t1_ref, t2_ref, o1_ref, o2_ref, r1_ref, r2_ref,
                     a1_ref, a2_ref, x1_ref, x2_ref, send_sem, recv_sem, gather_sem):
    me = {axis: lax.axis_index(axis) for axis in axis_order}

    def bit_of(axis, bit):
        return (me[axis] // bit) % 2

    plan_rounds = []
    for group in rounds:
        own = sum(bit_of(axis, bit) * 2 ** idx for idx, (axis, bit) in enumerate(group))
        members = []
        for t in range(1, 2 ** len(group)):
            there = dict(me)
            slot = 0
            for idx, (axis, bit) in enumerate(group):
                flip = (t // 2 ** idx) % 2
                if flip:
                    there[axis] = there[axis] + bit - 2 * bit * bit_of(axis, bit)
                slot = slot + ((bit_of(axis, bit) + flip) % 2) * 2 ** idx
            members.append((t, slot, tuple(there[a] for a in axis_order)))
        plan_rounds.append((group, own, members))

    def group_members(group):
        own = sum(bit_of(axis, bit) * 2 ** idx for idx, (axis, bit) in enumerate(group))
        members = []
        for t in range(1, 2 ** len(group)):
            there = dict(me)
            slot = 0
            flips = []
            for idx, (axis, bit) in enumerate(group):
                flip = (t // 2 ** idx) % 2
                if flip:
                    there[axis] = there[axis] + bit - 2 * bit * bit_of(axis, bit)
                    flips.append((axis, bit))
                slot = slot + ((bit_of(axis, bit) + flip) % 2) * 2 ** idx
            members.append((t, slot, tuple(there[a] for a in axis_order), frozenset(flips), flips))
        return own, members

    halving_bits = [rounds[r][0] for r in range(max(halvings(acc.shape[0], rounds) for acc in (o1_ref, o2_ref)))]
    seen = {}
    for group, own, members in plan_rounds:
        for t, slot, device in members:
            flips = frozenset((axis, bit) for idx, (axis, bit) in enumerate(group) if (t // 2 ** idx) % 2)
            seen[flips] = device
    for t, slot, device, flips, _ in group_members(halving_bits)[1]:
        seen[flips] = device
    barrier = pltpu.get_barrier_semaphore()
    for device in seen.values():
        pl.semaphore_signal(barrier, 1, device_id=device, device_id_type=pl.DeviceIdType.MESH)
    pl.semaphore_wait(barrier, len(seen))

    accs = (o1_ref, o2_ref)
    recvs = (r1_ref, r2_ref)
    gathers = (a1_ref, a2_ref)
    groups = (x1_ref, x2_ref)
    o1_ref[...] = g1_ref[...]
    o2_ref[...] = g2_ref[...]
    plans = [{"rows": acc.shape[0], "h": halvings(acc.shape[0], rounds), "off": 0, "kept": []} for acc in accs]

    def remote(src, dst, send, recv, device):
        return pltpu.make_async_remote_copy(
            src_ref=src, dst_ref=dst, send_sem=send, recv_sem=recv,
            device_id=device, device_id_type=pl.DeviceIdType.MESH)

    for r, (group, own, members) in enumerate(plan_rounds):
        sends, recvs_wait, after = [], [], []
        for k, (acc, recv, xbuf, plan) in enumerate(zip(accs, recvs, groups, plans)):
            if r < plan["h"]:
                (axis, bit), = group
                t, slot, device = members[0]
                mine = bit_of(axis, bit)
                half = plan["rows"] // 2
                keep = pl.multiple_of(plan["off"] + mine * half, 8)
                give = pl.multiple_of(plan["off"] + (1 - mine) * half, 8)
                copy = remote(acc.at[pl.ds(give, half)], recv.at[r, pl.ds(0, half)],
                              send_sem.at[r, 0, k], recv_sem.at[r, 0, k], device)
                sends.append(copy)
                recvs_wait.append(copy)
                after.append(("add", acc, recv, r, keep, half))
                plan["kept"].append((r, keep, give, half))
                plan["off"], plan["rows"] = keep, half
            else:
                rows, off = plan["rows"], plan["off"]
                xbuf[r, own] = acc[pl.ds(off, rows)]
                for t, slot, device in members:
                    sends.append(remote(acc.at[pl.ds(off, rows)], xbuf.at[r, own],
                                        send_sem.at[r, t, k], recv_sem.at[r, own, k], device))
                    recvs_wait.append(remote(acc.at[pl.ds(off, rows)], xbuf.at[r, slot],
                                             send_sem.at[r, t, k], recv_sem.at[r, slot, k], device))
                after.append(("sum", acc, xbuf, r, off, rows, 2 ** len(group)))
        for copy in sends:
            copy.start()
        for copy in sends:
            copy.wait_send()
        for copy in recvs_wait:
            copy.wait_recv()
        for item in after:
            if item[0] == "add":
                _, acc, recv, slot_r, off, rows = item
                acc[pl.ds(off, rows)] = acc[pl.ds(off, rows)] + recv[slot_r, pl.ds(0, rows)]
            else:
                _, acc, xbuf, slot_r, off, rows, n_members = item
                total = xbuf[slot_r, 0]
                for q in range(1, n_members):
                    total = total + xbuf[slot_r, q]
                acc[pl.ds(off, rows)] = total

    copies, places = [], []
    for k, (acc, gather, plan) in enumerate(zip(accs, gathers, plans)):
        if plan["h"] == 0:
            continue
        bits = [rounds[r][0] for r in range(plan["h"])]
        halves = [half for step, keep, give, half in plan["kept"]]
        own, members = group_members(bits)
        rows, off = plan["rows"], plan["off"]
        for t, slot, device, flips, flip_list in members:
            copies.append((
                remote(acc.at[pl.ds(off, rows)], gather.at[own], gather_sem.at[t, 0, k], gather_sem.at[own, 1, k], device),
                remote(acc.at[pl.ds(off, rows)], gather.at[slot], gather_sem.at[t, 0, k], gather_sem.at[slot, 1, k], device)))
            where = 0
            for idx, (axis, bit) in enumerate(bits):
                flip = 1 if (axis, bit) in flips else 0
                where = where + ((bit_of(axis, bit) + flip) % 2) * halves[idx]
            places.append((acc, gather, slot, pl.multiple_of(where, 8), rows))
    for send, recv in copies:
        send.start()
    for send, recv in copies:
        send.wait_send()
    for send, recv in copies:
        recv.wait_recv()
    for acc, gather, slot, where, rows in places:
        acc[pl.ds(where, rows)] = gather[slot]
    t1_ref[...] = o1_ref[...].T
    t2_ref[...] = o2_ref[...].T


def allreduce(g1, g2, axis_order, axis_sizes):
    rounds = exchange_rounds(axis_sizes)
    n = len(rounds)
    width = max(2 ** len(group) for group in rounds)
    vmem = pltpu.VMEM
    chunk = [g.shape[0] // 2 ** halvings(g.shape[0], rounds) for g in (g1, g2)]
    gwidth = max(2 ** halvings(g.shape[0], rounds) for g in (g1, g2))
    return pl.pallas_call(
        functools.partial(allreduce_kernel, axis_order, rounds),
        out_shape=(jax.ShapeDtypeStruct(g1.shape[::-1], g1.dtype), jax.ShapeDtypeStruct(g2.shape[::-1], g2.dtype)),
        in_specs=[pl.BlockSpec(memory_space=vmem)] * 2,
        out_specs=[pl.BlockSpec(memory_space=vmem)] * 2,
        scratch_shapes=[
            vmem(g1.shape, g1.dtype),
            vmem(g2.shape, g2.dtype),
            vmem((n, g1.shape[0] // 2) + g1.shape[1:], g1.dtype),
            vmem((n, g2.shape[0] // 2) + g2.shape[1:], g2.dtype),
            vmem((gwidth, chunk[0]) + g1.shape[1:], g1.dtype),
            vmem((gwidth, chunk[1]) + g2.shape[1:], g2.dtype),
            vmem((n, width, chunk[0]) + g1.shape[1:], g1.dtype),
            vmem((n, width, chunk[1]) + g2.shape[1:], g2.dtype),
            pltpu.SemaphoreType.DMA((n, width, 2)),
            pltpu.SemaphoreType.DMA((n, width, 2)),
            pltpu.SemaphoreType.DMA((gwidth, 2, 2)),
        ],
        compiler_params=pltpu.CompilerParams(collective_id=0, has_side_effects=True),
    )(g1, g2)


def body(axis_order, axis_sizes, crops, first_kernel, second_kernel, out_grad):
    local_samples, channels_in, planes, flat_cells = crops.shape
    whole_input = lax.all_to_all(crops, "space", split_axis=0, concat_axis=2, tiled=True)
    x = whole_input[0].transpose(1, 0, 2)
    c1, c2 = first_kernel.shape[0], second_kernel.shape[0]
    og = out_grad[0]
    ogn = og.reshape(c2, -1)
    ogq = og.transpose(1, 0, 2).reshape(-1, og.shape[2])
    w1 = first_kernel.transpose(0, 2, 3, 4, 1).reshape(c1, -1)
    w2 = second_kernel.transpose(0, 2, 3, 4, 1).reshape(c2, -1)
    w2t = second_kernel.transpose(2, 1, 3, 4, 0).reshape(3, c1, -1)
    t1, sel2, up = selection_tables(WIDTH, HEIGHT // 2, WIDTH // 2)
    act = act_grad_of(ogq, w2t, jnp.asarray(up, jnp.bfloat16))
    feat, fg, sg = per_sample(x, ogn, act, w1, w2, jnp.asarray(t1, jnp.bfloat16), jnp.asarray(sel2, jnp.bfloat16))
    features_out = feat.reshape(out_grad.shape)
    fg, sg = allreduce(fg, sg, axis_order, axis_sizes)
    first_grad = fg.reshape(3, 3, 3, channels_in, c1).transpose(4, 3, 0, 1, 2)
    second_grad = sg.reshape(3, 3, 3, c1, c2).transpose(4, 3, 0, 1, 2)
    return (features_out, first_grad, second_grad)


def solution(mesh):
    placed = (P("sample", None, "space", None), P(), P(), P(("sample", "space"), None, None, None))
    axis_order = tuple(mesh.axis_names)
    axis_sizes = [(a, mesh.shape[a]) for a in ("sample", "space")]
    return jax.shard_map(
        functools.partial(body, axis_order, axis_sizes),
        mesh=mesh,
        in_specs=placed,
        out_specs=(P(("sample", "space"), None, None, None), P(), P()),
        check_vma=False,
    )
```

```python
import functools

import numpy as np

import jax
import jax.numpy as jnp
from jax import lax
from jax.experimental import pallas as pl
from jax.experimental.pallas import tpu as pltpu
from jax.sharding import PartitionSpec as P

HEIGHT = 8
WIDTH = 128

NT = (((1,), (1,)), ((), ()))


def selection_tables(c0_w, c1_h, c1_w):
    t1 = np.zeros((c0_w, 3 * 128), np.float32)
    for c in range(3):
        for pw in range(c0_w // 2):
            w = 2 * pw + c - 1
            if 0 <= w < c0_w:
                t1[w, c * 128 + pw] = 1.0
    q_h, q_w = c1_h // 2, c1_w // 2
    sel2 = np.zeros((c1_h * c1_w, 9 * 128), np.float32)
    up = np.zeros((q_h * q_w, 9 * c1_h * c1_w), np.float32)
    for b in range(3):
        for c in range(3):
            bc = b * 3 + c
            for qh in range(q_h):
                for qw in range(q_w):
                    h2, w2 = 2 * qh + b - 1, 2 * qw + c - 1
                    if 0 <= h2 < c1_h and 0 <= w2 < c1_w:
                        sel2[h2 * c1_w + w2, bc * 128 + qh * q_w + qw] = 1.0
                        up[qh * q_w + qw, bc * c1_h * c1_w + h2 * c1_w + w2] = 1.0
    return t1, sel2, up


def act_kernel(ogq_ref, w2t_ref, up_ref, act_ref, v_ref):
    planes2 = v_ref.shape[0] - 1
    c2 = v_ref.shape[2]
    span = up_ref.shape[1] // 9
    v_ref[planes2] = jnp.zeros(v_ref.shape[1:], v_ref.dtype)
    for bc in range(9):
        u = jnp.dot(ogq_ref[...], up_ref[:, bc * span:(bc + 1) * span], preferred_element_type=jnp.float32)
        v_ref[pl.ds(0, planes2), bc] = u.astype(v_ref.dtype).reshape(planes2, c2, span)

    def plane(q, carry):
        vq = v_ref[q].reshape(9 * c2, span)
        vq1 = v_ref[q + 1].reshape(9 * c2, span)
        even = jnp.dot(w2t_ref[1], vq, preferred_element_type=jnp.float32)
        odd = (jnp.dot(w2t_ref[2], vq, preferred_element_type=jnp.float32)
               + jnp.dot(w2t_ref[0], vq1, preferred_element_type=jnp.float32))
        act_ref[2 * q] = even.astype(act_ref.dtype)
        act_ref[2 * q + 1] = odd.astype(act_ref.dtype)
        return carry

    lax.fori_loop(0, planes2, plane, 0)


def act_grad_of(ogq, w2t, up):
    c2 = w2t.shape[2] // 9
    planes2 = ogq.shape[0] // c2
    c1 = w2t.shape[1]
    span = up.shape[1] // 9
    vmem = pltpu.VMEM
    flops = 2 * ogq.shape[0] * ogq.shape[1] * up.shape[1] + 2 * 3 * 2 * planes2 * c1 * 9 * c2 * span
    return pl.pallas_call(
        act_kernel,
        out_shape=jax.ShapeDtypeStruct((2 * planes2, c1, span), jnp.bfloat16),
        in_specs=[pl.BlockSpec(memory_space=vmem)] * 3,
        out_specs=pl.BlockSpec(memory_space=vmem),
        scratch_shapes=[vmem((planes2 + 1, 9, c2, span), jnp.bfloat16)],
        compiler_params=pltpu.CompilerParams(vmem_limit_bytes=32 * 1024 * 1024),
        cost_estimate=pl.CostEstimate(flops=flops, transcendentals=0,
                                      bytes_accessed=2 * (ogq.size + w2t.size + up.size + 2 * planes2 * c1 * span)),
    )(ogq, w2t, up)


def conv_kernel(x_ref, ogn_ref, act_ref, w1_ref, w2_ref, t1_ref, sel2_ref,
                feat_ref, fg_ref, sg_ref,
                q1_ref, s_ref, fp_ref, a2_ref, q2_ref, s2_ref):
    depth, c0, cells = x_ref.shape
    n_h = cells // 128
    c1 = w1_ref.shape[0]
    c2 = w2_ref.shape[0]
    planes1 = depth // 2
    plane1 = s_ref.shape[2]
    planes2 = planes1 // 2

    q1_ref[0] = jnp.zeros(q1_ref.shape[1:], q1_ref.dtype)
    for h in range(n_h):
        xh = x_ref[:, :, h * 128:(h + 1) * 128].reshape(depth * c0, 128)
        qh = jnp.dot(xh, t1_ref[...], preferred_element_type=jnp.float32)
        q1_ref[pl.ds(1, depth), :, h * 384:(h + 1) * 384] = qh.astype(q1_ref.dtype).reshape(depth, c0, 384)

    a2_ref[0] = jnp.zeros(a2_ref.shape[1:], a2_ref.dtype)

    def build_plane(pd, carry):
        for a in range(3):
            for b in range(3):
                for c in range(3):
                    r0 = ((a * 3 + b) * 3 + c) * c0
                    for m in range(plane1 // 128):
                        h_lo, h_hi = 4 * m + b - 1, 4 * m + b + 1
                        hi = q1_ref[2 * pd + a, :, pl.ds((h_hi * 3 + c) * 128, 128)].astype(jnp.float32)
                        val = pltpu.roll(hi, 64, 1)
                        if h_lo >= 0:
                            val = val + q1_ref[2 * pd + a, :, pl.ds((h_lo * 3 + c) * 128, 128)].astype(jnp.float32)
                        s_ref[pd, pl.ds(r0, c0), pl.ds(m * 128, 128)] = val.astype(s_ref.dtype)
        pre = jnp.dot(w1_ref[...], s_ref[pd], preferred_element_type=jnp.float32)
        sig = 1.0 / (1.0 + jnp.exp(-pre))
        fp_ref[pd] = sig * (1.0 + pre * (1.0 - sig))
        a2_ref[pd + 1] = (pre * sig).astype(a2_ref.dtype)
        return carry

    lax.fori_loop(0, planes1, build_plane, 0, unroll=4)

    a2 = a2_ref[...].reshape((planes1 + 1) * c1, plane1)
    for bc in range(9):
        q2 = jnp.dot(a2, sel2_ref[:, bc * 128:(bc + 1) * 128], preferred_element_type=jnp.float32)
        q2_ref[:, :, bc * 128:(bc + 1) * 128] = q2.reshape(planes1 + 1, c1, 128)

    sg_ref[...] = jnp.zeros(sg_ref.shape, sg_ref.dtype)
    for n in range(planes2 // 2):
        for a in range(3):
            for bc in range(9):
                r0 = (a * 9 + bc) * c1
                lo = q2_ref[4 * n + a, :, bc * 128:(bc + 1) * 128]
                hi = q2_ref[4 * n + a + 2, :, bc * 128:(bc + 1) * 128]
                s2_ref[n, r0:r0 + c1, :] = (lo + pltpu.roll(hi, 64, 1)).astype(s2_ref.dtype)
        feat = jnp.dot(w2_ref[...], s2_ref[n], preferred_element_type=jnp.float32)
        half = feat_ref.shape[2]
        feat_ref[:, 2 * n, :] = feat[:, :half].astype(feat_ref.dtype)
        feat_ref[:, 2 * n + 1, :] = feat[:, half:].astype(feat_ref.dtype)
        sg_ref[...] += lax.dot_general(ogn_ref[:, n * 128:(n + 1) * 128], s2_ref[n], NT,
                                       preferred_element_type=jnp.float32)

    fg_ref[...] = jnp.zeros(fg_ref.shape, fg_ref.dtype)

    def back_plane(d2, carry):
        slope = fp_ref[d2]
        pg = (act_ref[d2].astype(jnp.float32) * slope).astype(jnp.bfloat16)
        fg_ref[...] += lax.dot_general(pg, s_ref[d2], NT, preferred_element_type=jnp.float32)
        return carry

    lax.fori_loop(0, planes1, back_plane, 0, unroll=8)


def per_sample(x, ogn, act, w1, w2, t1, sel2):
    depth, c0, cells = x.shape
    c1, c2 = w1.shape[0], w2.shape[0]
    planes1, planes2 = depth // 2, depth // 4
    plane1 = (HEIGHT // 2) * (WIDTH // 2)
    plane2 = ogn.shape[1] // planes2
    vmem = pltpu.VMEM
    return pl.pallas_call(
        conv_kernel,
        out_shape=(
            jax.ShapeDtypeStruct((c2, planes2, plane2), jnp.bfloat16),
            jax.ShapeDtypeStruct((c1, 27 * c0), jnp.float32),
            jax.ShapeDtypeStruct((c2, 27 * c1), jnp.float32),
        ),
        in_specs=[pl.BlockSpec(memory_space=vmem)] * 7,
        out_specs=[pl.BlockSpec(memory_space=vmem)] * 3,
        scratch_shapes=[
            vmem((depth + 1, c0, (cells // 128) * 384), jnp.bfloat16),
            vmem((planes1, 27 * c0, plane1), jnp.bfloat16),
            vmem((planes1, c1, plane1), jnp.float32),
            vmem((planes1 + 1, c1, plane1), jnp.bfloat16),
            vmem((planes1 + 1, c1, 9 * 128), jnp.float32),
            vmem((planes2 // 2, 27 * c1, 128), jnp.bfloat16),
        ],
        compiler_params=pltpu.CompilerParams(vmem_limit_bytes=60 * 1024 * 1024),
    )(x, ogn, act, w1, w2, t1, sel2)


ROUND_ORDER = ((("sample", 1),), (("space", 4),), (("sample", 2),),
               (("space", 1), ("space", 2), ("sample", 4)), (("space", 8), ("space", 16)))


def exchange_rounds(axis_sizes):
    sizes = dict(axis_sizes)
    rounds = []
    for group in ROUND_ORDER:
        kept = tuple((axis, bit) for axis, bit in group if bit < sizes[axis])
        if kept:
            rounds.append(kept)
    used = {pair for group in rounds for pair in group}
    for axis, size in axis_sizes:
        bit = 1
        while bit < size:
            if (axis, bit) not in used:
                rounds.append(((axis, bit),))
            bit *= 2
    return rounds


def halvings(rows, rounds):
    count = 0
    while (count < len(rounds) and len(rounds[count]) == 1
           and rows % (2 ** (count + 1) * 8) == 0):
        count += 1
    return count


def allreduce_kernel(axis_order, rounds, g1_ref, g2_ref, t1_ref, t2_ref, o1_ref, o2_ref, r1_ref, r2_ref,
                     a1_ref, a2_ref, x1_ref, x2_ref, send_sem, recv_sem, gather_sem):
    me = {axis: lax.axis_index(axis) for axis in axis_order}

    def bit_of(axis, bit):
        return (me[axis] // bit) % 2

    plan_rounds = []
    for group in rounds:
        own = sum(bit_of(axis, bit) * 2 ** idx for idx, (axis, bit) in enumerate(group))
        members = []
        for t in range(1, 2 ** len(group)):
            there = dict(me)
            slot = 0
            for idx, (axis, bit) in enumerate(group):
                flip = (t // 2 ** idx) % 2
                if flip:
                    there[axis] = there[axis] + bit - 2 * bit * bit_of(axis, bit)
                slot = slot + ((bit_of(axis, bit) + flip) % 2) * 2 ** idx
            members.append((t, slot, tuple(there[a] for a in axis_order)))
        plan_rounds.append((group, own, members))

    def group_members(group):
        own = sum(bit_of(axis, bit) * 2 ** idx for idx, (axis, bit) in enumerate(group))
        members = []
        for t in range(1, 2 ** len(group)):
            there = dict(me)
            slot = 0
            flips = []
            for idx, (axis, bit) in enumerate(group):
                flip = (t // 2 ** idx) % 2
                if flip:
                    there[axis] = there[axis] + bit - 2 * bit * bit_of(axis, bit)
                    flips.append((axis, bit))
                slot = slot + ((bit_of(axis, bit) + flip) % 2) * 2 ** idx
            members.append((t, slot, tuple(there[a] for a in axis_order), frozenset(flips), flips))
        return own, members

    halving_bits = [rounds[r][0] for r in range(max(halvings(acc.shape[0], rounds) for acc in (o1_ref, o2_ref)))]
    seen = {}
    for group, own, members in plan_rounds:
        for t, slot, device in members:
            flips = frozenset((axis, bit) for idx, (axis, bit) in enumerate(group) if (t // 2 ** idx) % 2)
            seen[flips] = device
    for t, slot, device, flips, _ in group_members(halving_bits)[1]:
        seen[flips] = device
    barrier = pltpu.get_barrier_semaphore()
    for device in seen.values():
        pl.semaphore_signal(barrier, 1, device_id=device, device_id_type=pl.DeviceIdType.MESH)
    pl.semaphore_wait(barrier, len(seen))

    accs = (o1_ref, o2_ref)
    recvs = (r1_ref, r2_ref)
    gathers = (a1_ref, a2_ref)
    groups = (x1_ref, x2_ref)
    o1_ref[...] = g1_ref[...]
    o2_ref[...] = g2_ref[...]
    plans = [{"rows": acc.shape[0], "h": halvings(acc.shape[0], rounds), "off": 0, "kept": []} for acc in accs]

    def remote(src, dst, send, recv, device):
        return pltpu.make_async_remote_copy(
            src_ref=src, dst_ref=dst, send_sem=send, recv_sem=recv,
            device_id=device, device_id_type=pl.DeviceIdType.MESH)

    for r, (group, own, members) in enumerate(plan_rounds):
        sends, recvs_wait, after = [], [], []
        for k, (acc, recv, xbuf, plan) in enumerate(zip(accs, recvs, groups, plans)):
            if r < plan["h"]:
                (axis, bit), = group
                t, slot, device = members[0]
                mine = bit_of(axis, bit)
                half = plan["rows"] // 2
                keep = pl.multiple_of(plan["off"] + mine * half, 8)
                give = pl.multiple_of(plan["off"] + (1 - mine) * half, 8)
                copy = remote(acc.at[pl.ds(give, half)], recv.at[r, pl.ds(0, half)],
                              send_sem.at[r, 0, k], recv_sem.at[r, 0, k], device)
                sends.append(copy)
                recvs_wait.append(copy)
                after.append(("add", acc, recv, r, keep, half))
                plan["kept"].append((r, keep, give, half))
                plan["off"], plan["rows"] = keep, half
            else:
                rows, off = plan["rows"], plan["off"]
                xbuf[r, own] = acc[pl.ds(off, rows)]
                for t, slot, device in members:
                    sends.append(remote(acc.at[pl.ds(off, rows)], xbuf.at[r, own],
                                        send_sem.at[r, t, k], recv_sem.at[r, own, k], device))
                    recvs_wait.append(remote(acc.at[pl.ds(off, rows)], xbuf.at[r, slot],
                                             send_sem.at[r, t, k], recv_sem.at[r, slot, k], device))
                after.append(("sum", acc, xbuf, r, off, rows, 2 ** len(group)))
        for copy in sends:
            copy.start()
        for copy in sends:
            copy.wait_send()
        for copy in recvs_wait:
            copy.wait_recv()
        for item in after:
            if item[0] == "add":
                _, acc, recv, slot_r, off, rows = item
                acc[pl.ds(off, rows)] = acc[pl.ds(off, rows)] + recv[slot_r, pl.ds(0, rows)]
            else:
                _, acc, xbuf, slot_r, off, rows, n_members = item
                total = xbuf[slot_r, 0]
                for q in range(1, n_members):
                    total = total + xbuf[slot_r, q]
                acc[pl.ds(off, rows)] = total

    copies, places = [], []
    for k, (acc, gather, plan) in enumerate(zip(accs, gathers, plans)):
        if plan["h"] == 0:
            continue
        bits = [rounds[r][0] for r in range(plan["h"])]
        halves = [half for step, keep, give, half in plan["kept"]]
        own, members = group_members(bits)
        rows, off = plan["rows"], plan["off"]
        for t, slot, device, flips, flip_list in members:
            copies.append((
                remote(acc.at[pl.ds(off, rows)], gather.at[own], gather_sem.at[t, 0, k], gather_sem.at[own, 1, k], device),
                remote(acc.at[pl.ds(off, rows)], gather.at[slot], gather_sem.at[t, 0, k], gather_sem.at[slot, 1, k], device)))
            where = 0
            for idx, (axis, bit) in enumerate(bits):
                flip = 1 if (axis, bit) in flips else 0
                where = where + ((bit_of(axis, bit) + flip) % 2) * halves[idx]
            places.append((acc, gather, slot, pl.multiple_of(where, 8), rows))
    for send, recv in copies:
        send.start()
    for send, recv in copies:
        send.wait_send()
    for send, recv in copies:
        recv.wait_recv()
    for acc, gather, slot, where, rows in places:
        acc[pl.ds(where, rows)] = gather[slot]
    t1_ref[...] = o1_ref[...].T
    t2_ref[...] = o2_ref[...].T


def allreduce(g1, g2, axis_order, axis_sizes):
    rounds = exchange_rounds(axis_sizes)
    n = len(rounds)
    width = max(2 ** len(group) for group in rounds)
    vmem = pltpu.VMEM
    chunk = [g.shape[0] // 2 ** halvings(g.shape[0], rounds) for g in (g1, g2)]
    gwidth = max(2 ** halvings(g.shape[0], rounds) for g in (g1, g2))
    return pl.pallas_call(
        functools.partial(allreduce_kernel, axis_order, rounds),
        out_shape=(jax.ShapeDtypeStruct(g1.shape[::-1], g1.dtype), jax.ShapeDtypeStruct(g2.shape[::-1], g2.dtype)),
        in_specs=[pl.BlockSpec(memory_space=vmem)] * 2,
        out_specs=[pl.BlockSpec(memory_space=vmem)] * 2,
        scratch_shapes=[
            vmem(g1.shape, g1.dtype),
            vmem(g2.shape, g2.dtype),
            vmem((n, g1.shape[0] // 2) + g1.shape[1:], g1.dtype),
            vmem((n, g2.shape[0] // 2) + g2.shape[1:], g2.dtype),
            vmem((gwidth, chunk[0]) + g1.shape[1:], g1.dtype),
            vmem((gwidth, chunk[1]) + g2.shape[1:], g2.dtype),
            vmem((n, width, chunk[0]) + g1.shape[1:], g1.dtype),
            vmem((n, width, chunk[1]) + g2.shape[1:], g2.dtype),
            pltpu.SemaphoreType.DMA((n, width, 2)),
            pltpu.SemaphoreType.DMA((n, width, 2)),
            pltpu.SemaphoreType.DMA((gwidth, 2, 2)),
        ],
        compiler_params=pltpu.CompilerParams(collective_id=0, has_side_effects=True),
    )(g1, g2)


def body(axis_order, axis_sizes, crops, first_kernel, second_kernel, out_grad):
    local_samples, channels_in, planes, flat_cells = crops.shape
    whole_input = lax.all_to_all(crops, "space", split_axis=0, concat_axis=2, tiled=True)
    x = whole_input[0].transpose(1, 0, 2)
    c1, c2 = first_kernel.shape[0], second_kernel.shape[0]
    og = out_grad[0]
    ogn = og.reshape(c2, -1)
    ogq = og.transpose(1, 0, 2).reshape(-1, og.shape[2])
    w1 = first_kernel.transpose(0, 2, 3, 4, 1).reshape(c1, -1)
    w2 = second_kernel.transpose(0, 2, 3, 4, 1).reshape(c2, -1)
    w2t = second_kernel.transpose(2, 1, 3, 4, 0).reshape(3, c1, -1)
    t1, sel2, up = selection_tables(WIDTH, HEIGHT // 2, WIDTH // 2)
    act = act_grad_of(ogq, w2t, jnp.asarray(up, jnp.bfloat16))
    feat, fg, sg = per_sample(x, ogn, act, w1, w2, jnp.asarray(t1, jnp.bfloat16), jnp.asarray(sel2, jnp.bfloat16))
    features_out = feat.reshape(out_grad.shape)
    fg, sg = allreduce(fg, sg, axis_order, axis_sizes)
    first_grad = fg.reshape(3, 3, 3, channels_in, c1).transpose(4, 3, 0, 1, 2)
    second_grad = sg.reshape(3, 3, 3, c1, c2).transpose(4, 3, 0, 1, 2)
    return (features_out, first_grad, second_grad)


def solution(mesh):
    placed = (P("sample", None, "space", None), P(), P(), P(("sample", "space"), None, None, None))
    axis_order = tuple(mesh.axis_names)
    axis_sizes = [(a, mesh.shape[a]) for a in ("sample", "space")]
    return jax.shard_map(
        functools.partial(body, axis_order, axis_sizes),
        mesh=mesh,
        in_specs=placed,
        out_specs=(P(("sample", "space"), None, None, None), P(), P()),
        check_vma=False,
    )
```

```python
import functools

import numpy as np

import jax
import jax.numpy as jnp
from jax import lax
from jax.experimental import pallas as pl
from jax.experimental.pallas import tpu as pltpu
from jax.sharding import PartitionSpec as P

HEIGHT = 8
WIDTH = 128

NT = (((1,), (1,)), ((), ()))


def selection_tables(c0_w, c1_h, c1_w):
    t1 = np.zeros((c0_w, 3 * 128), np.float32)
    for c in range(3):
        for pw in range(c0_w // 2):
            w = 2 * pw + c - 1
            if 0 <= w < c0_w:
                t1[w, c * 128 + pw] = 1.0
    q_h, q_w = c1_h // 2, c1_w // 2
    sel2 = np.zeros((c1_h * c1_w, 9 * 128), np.float32)
    up = np.zeros((q_h * q_w, 9 * c1_h * c1_w), np.float32)
    for b in range(3):
        for c in range(3):
            bc = b * 3 + c
            for qh in range(q_h):
                for qw in range(q_w):
                    h2, w2 = 2 * qh + b - 1, 2 * qw + c - 1
                    if 0 <= h2 < c1_h and 0 <= w2 < c1_w:
                        sel2[h2 * c1_w + w2, bc * 128 + qh * q_w + qw] = 1.0
                        up[qh * q_w + qw, bc * c1_h * c1_w + h2 * c1_w + w2] = 1.0
    return t1, sel2, up


def act_kernel(ogq_ref, w2t_ref, up_ref, act_ref, v_ref):
    planes2 = v_ref.shape[0] - 1
    c2 = v_ref.shape[2]
    span = up_ref.shape[1] // 9
    v_ref[planes2] = jnp.zeros(v_ref.shape[1:], v_ref.dtype)
    for bc in range(9):
        u = jnp.dot(ogq_ref[...], up_ref[:, bc * span:(bc + 1) * span], preferred_element_type=jnp.float32)
        v_ref[pl.ds(0, planes2), bc] = u.astype(v_ref.dtype).reshape(planes2, c2, span)

    def plane(q, carry):
        vq = v_ref[q].reshape(9 * c2, span)
        vq1 = v_ref[q + 1].reshape(9 * c2, span)
        even = jnp.dot(w2t_ref[1], vq, preferred_element_type=jnp.float32)
        odd = (jnp.dot(w2t_ref[2], vq, preferred_element_type=jnp.float32)
               + jnp.dot(w2t_ref[0], vq1, preferred_element_type=jnp.float32))
        act_ref[2 * q] = even.astype(act_ref.dtype)
        act_ref[2 * q + 1] = odd.astype(act_ref.dtype)
        return carry

    lax.fori_loop(0, planes2, plane, 0)


def act_grad_of(ogq, w2t, up):
    c2 = w2t.shape[2] // 9
    planes2 = ogq.shape[0] // c2
    c1 = w2t.shape[1]
    span = up.shape[1] // 9
    vmem = pltpu.VMEM
    flops = 2 * ogq.shape[0] * ogq.shape[1] * up.shape[1] + 2 * 3 * 2 * planes2 * c1 * 9 * c2 * span
    return pl.pallas_call(
        act_kernel,
        out_shape=jax.ShapeDtypeStruct((2 * planes2, c1, span), jnp.bfloat16),
        in_specs=[pl.BlockSpec(memory_space=vmem)] * 3,
        out_specs=pl.BlockSpec(memory_space=vmem),
        scratch_shapes=[vmem((planes2 + 1, 9, c2, span), jnp.bfloat16)],
        compiler_params=pltpu.CompilerParams(vmem_limit_bytes=32 * 1024 * 1024),
        cost_estimate=pl.CostEstimate(flops=flops, transcendentals=0,
                                      bytes_accessed=2 * (ogq.size + w2t.size + up.size + 2 * planes2 * c1 * span)),
    )(ogq, w2t, up)


def conv_kernel(x_ref, ogn_ref, act_ref, w1_ref, w2_ref, t1_ref, sel2_ref,
                feat_ref, fg_ref, sg_ref,
                q1_ref, s_ref, fp_ref, a2_ref, q2_ref, s2_ref):
    depth, c0, cells = x_ref.shape
    n_h = cells // 128
    c1 = w1_ref.shape[0]
    c2 = w2_ref.shape[0]
    planes1 = depth // 2
    plane1 = s_ref.shape[2]
    planes2 = planes1 // 2

    q1_ref[0] = jnp.zeros(q1_ref.shape[1:], q1_ref.dtype)
    for h in range(n_h):
        xh = x_ref[:, :, h * 128:(h + 1) * 128].reshape(depth * c0, 128)
        qh = jnp.dot(xh, t1_ref[...], preferred_element_type=jnp.float32)
        q1_ref[pl.ds(1, depth), :, h * 384:(h + 1) * 384] = qh.astype(q1_ref.dtype).reshape(depth, c0, 384)

    a2_ref[0] = jnp.zeros(a2_ref.shape[1:], a2_ref.dtype)

    def build_plane(pd, carry):
        for a in range(3):
            for b in range(3):
                for c in range(3):
                    r0 = ((a * 3 + b) * 3 + c) * c0
                    for m in range(plane1 // 128):
                        h_lo, h_hi = 4 * m + b - 1, 4 * m + b + 1
                        hi = q1_ref[2 * pd + a, :, pl.ds((h_hi * 3 + c) * 128, 128)].astype(jnp.float32)
                        val = pltpu.roll(hi, 64, 1)
                        if h_lo >= 0:
                            val = val + q1_ref[2 * pd + a, :, pl.ds((h_lo * 3 + c) * 128, 128)].astype(jnp.float32)
                        s_ref[pd, pl.ds(r0, c0), pl.ds(m * 128, 128)] = val.astype(s_ref.dtype)
        pre = jnp.dot(w1_ref[...], s_ref[pd], preferred_element_type=jnp.float32)
        sig = 1.0 / (1.0 + jnp.exp(-pre))
        fp_ref[pd] = sig * (1.0 + pre * (1.0 - sig))
        a2_ref[pd + 1] = (pre * sig).astype(a2_ref.dtype)
        return carry

    lax.fori_loop(0, planes1, build_plane, 0, unroll=8)

    a2 = a2_ref[...].reshape((planes1 + 1) * c1, plane1)
    for bc in range(9):
        q2 = jnp.dot(a2, sel2_ref[:, bc * 128:(bc + 1) * 128], preferred_element_type=jnp.float32)
        q2_ref[:, :, bc * 128:(bc + 1) * 128] = q2.reshape(planes1 + 1, c1, 128)

    sg_ref[...] = jnp.zeros(sg_ref.shape, sg_ref.dtype)
    for n in range(planes2 // 2):
        for a in range(3):
            for bc in range(9):
                r0 = (a * 9 + bc) * c1
                lo = q2_ref[4 * n + a, :, bc * 128:(bc + 1) * 128]
                hi = q2_ref[4 * n + a + 2, :, bc * 128:(bc + 1) * 128]
                s2_ref[n, r0:r0 + c1, :] = (lo + pltpu.roll(hi, 64, 1)).astype(s2_ref.dtype)
        feat = jnp.dot(w2_ref[...], s2_ref[n], preferred_element_type=jnp.float32)
        half = feat_ref.shape[2]
        feat_ref[:, 2 * n, :] = feat[:, :half].astype(feat_ref.dtype)
        feat_ref[:, 2 * n + 1, :] = feat[:, half:].astype(feat_ref.dtype)
        sg_ref[...] += lax.dot_general(ogn_ref[:, n * 128:(n + 1) * 128], s2_ref[n], NT,
                                       preferred_element_type=jnp.float32)

    fg_ref[...] = jnp.zeros(fg_ref.shape, fg_ref.dtype)

    def back_plane(d2, carry):
        slope = fp_ref[d2]
        pg = (act_ref[d2].astype(jnp.float32) * slope).astype(jnp.bfloat16)
        fg_ref[...] += lax.dot_general(pg, s_ref[d2], NT, preferred_element_type=jnp.float32)
        return carry

    lax.fori_loop(0, planes1, back_plane, 0, unroll=16)


def per_sample(x, ogn, act, w1, w2, t1, sel2):
    depth, c0, cells = x.shape
    c1, c2 = w1.shape[0], w2.shape[0]
    planes1, planes2 = depth // 2, depth // 4
    plane1 = (HEIGHT // 2) * (WIDTH // 2)
    plane2 = ogn.shape[1] // planes2
    vmem = pltpu.VMEM
    return pl.pallas_call(
        conv_kernel,
        out_shape=(
            jax.ShapeDtypeStruct((c2, planes2, plane2), jnp.bfloat16),
            jax.ShapeDtypeStruct((c1, 27 * c0), jnp.float32),
            jax.ShapeDtypeStruct((c2, 27 * c1), jnp.float32),
        ),
        in_specs=[pl.BlockSpec(memory_space=vmem)] * 7,
        out_specs=[pl.BlockSpec(memory_space=vmem)] * 3,
        scratch_shapes=[
            vmem((depth + 1, c0, (cells // 128) * 384), jnp.bfloat16),
            vmem((planes1, 27 * c0, plane1), jnp.bfloat16),
            vmem((planes1, c1, plane1), jnp.float32),
            vmem((planes1 + 1, c1, plane1), jnp.bfloat16),
            vmem((planes1 + 1, c1, 9 * 128), jnp.float32),
            vmem((planes2 // 2, 27 * c1, 128), jnp.bfloat16),
        ],
        compiler_params=pltpu.CompilerParams(vmem_limit_bytes=60 * 1024 * 1024),
    )(x, ogn, act, w1, w2, t1, sel2)


ROUND_ORDER = ((("sample", 1),), (("space", 4),), (("sample", 2),),
               (("space", 1), ("space", 2), ("sample", 4)), (("space", 8), ("space", 16)))


def exchange_rounds(axis_sizes):
    sizes = dict(axis_sizes)
    rounds = []
    for group in ROUND_ORDER:
        kept = tuple((axis, bit) for axis, bit in group if bit < sizes[axis])
        if kept:
            rounds.append(kept)
    used = {pair for group in rounds for pair in group}
    for axis, size in axis_sizes:
        bit = 1
        while bit < size:
            if (axis, bit) not in used:
                rounds.append(((axis, bit),))
            bit *= 2
    return rounds


def halvings(rows, rounds):
    count = 0
    while (count < len(rounds) and len(rounds[count]) == 1
           and rows % (2 ** (count + 1) * 8) == 0):
        count += 1
    return count


def allreduce_kernel(axis_order, rounds, g1_ref, g2_ref, t1_ref, t2_ref, o1_ref, o2_ref, r1_ref, r2_ref,
                     a1_ref, a2_ref, x1_ref, x2_ref, send_sem, recv_sem, gather_sem):
    me = {axis: lax.axis_index(axis) for axis in axis_order}

    def bit_of(axis, bit):
        return (me[axis] // bit) % 2

    plan_rounds = []
    for group in rounds:
        own = sum(bit_of(axis, bit) * 2 ** idx for idx, (axis, bit) in enumerate(group))
        members = []
        for t in range(1, 2 ** len(group)):
            there = dict(me)
            slot = 0
            for idx, (axis, bit) in enumerate(group):
                flip = (t // 2 ** idx) % 2
                if flip:
                    there[axis] = there[axis] + bit - 2 * bit * bit_of(axis, bit)
                slot = slot + ((bit_of(axis, bit) + flip) % 2) * 2 ** idx
            members.append((t, slot, tuple(there[a] for a in axis_order)))
        plan_rounds.append((group, own, members))

    def group_members(group):
        own = sum(bit_of(axis, bit) * 2 ** idx for idx, (axis, bit) in enumerate(group))
        members = []
        for t in range(1, 2 ** len(group)):
            there = dict(me)
            slot = 0
            flips = []
            for idx, (axis, bit) in enumerate(group):
                flip = (t // 2 ** idx) % 2
                if flip:
                    there[axis] = there[axis] + bit - 2 * bit * bit_of(axis, bit)
                    flips.append((axis, bit))
                slot = slot + ((bit_of(axis, bit) + flip) % 2) * 2 ** idx
            members.append((t, slot, tuple(there[a] for a in axis_order), frozenset(flips), flips))
        return own, members

    halving_bits = [rounds[r][0] for r in range(max(halvings(acc.shape[0], rounds) for acc in (o1_ref, o2_ref)))]
    seen = {}
    for group, own, members in plan_rounds:
        for t, slot, device in members:
            flips = frozenset((axis, bit) for idx, (axis, bit) in enumerate(group) if (t // 2 ** idx) % 2)
            seen[flips] = device
    for t, slot, device, flips, _ in group_members(halving_bits)[1]:
        seen[flips] = device
    barrier = pltpu.get_barrier_semaphore()
    for device in seen.values():
        pl.semaphore_signal(barrier, 1, device_id=device, device_id_type=pl.DeviceIdType.MESH)
    pl.semaphore_wait(barrier, len(seen))

    accs = (o1_ref, o2_ref)
    recvs = (r1_ref, r2_ref)
    gathers = (a1_ref, a2_ref)
    groups = (x1_ref, x2_ref)
    o1_ref[...] = g1_ref[...]
    o2_ref[...] = g2_ref[...]
    plans = [{"rows": acc.shape[0], "h": halvings(acc.shape[0], rounds), "off": 0, "kept": []} for acc in accs]

    def remote(src, dst, send, recv, device):
        return pltpu.make_async_remote_copy(
            src_ref=src, dst_ref=dst, send_sem=send, recv_sem=recv,
            device_id=device, device_id_type=pl.DeviceIdType.MESH)

    for r, (group, own, members) in enumerate(plan_rounds):
        sends, recvs_wait, after = [], [], []
        for k, (acc, recv, xbuf, plan) in enumerate(zip(accs, recvs, groups, plans)):
            if r < plan["h"]:
                (axis, bit), = group
                t, slot, device = members[0]
                mine = bit_of(axis, bit)
                half = plan["rows"] // 2
                keep = pl.multiple_of(plan["off"] + mine * half, 8)
                give = pl.multiple_of(plan["off"] + (1 - mine) * half, 8)
                copy = remote(acc.at[pl.ds(give, half)], recv.at[r, pl.ds(0, half)],
                              send_sem.at[r, 0, k], recv_sem.at[r, 0, k], device)
                sends.append(copy)
                recvs_wait.append(copy)
                after.append(("add", acc, recv, r, keep, half))
                plan["kept"].append((r, keep, give, half))
                plan["off"], plan["rows"] = keep, half
            else:
                rows, off = plan["rows"], plan["off"]
                xbuf[r, own] = acc[pl.ds(off, rows)]
                for t, slot, device in members:
                    sends.append(remote(acc.at[pl.ds(off, rows)], xbuf.at[r, own],
                                        send_sem.at[r, t, k], recv_sem.at[r, own, k], device))
                    recvs_wait.append(remote(acc.at[pl.ds(off, rows)], xbuf.at[r, slot],
                                             send_sem.at[r, t, k], recv_sem.at[r, slot, k], device))
                after.append(("sum", acc, xbuf, r, off, rows, 2 ** len(group)))
        for copy in sends:
            copy.start()
        for copy in sends:
            copy.wait_send()
        for copy in recvs_wait:
            copy.wait_recv()
        for item in after:
            if item[0] == "add":
                _, acc, recv, slot_r, off, rows = item
                acc[pl.ds(off, rows)] = acc[pl.ds(off, rows)] + recv[slot_r, pl.ds(0, rows)]
            else:
                _, acc, xbuf, slot_r, off, rows, n_members = item
                total = xbuf[slot_r, 0]
                for q in range(1, n_members):
                    total = total + xbuf[slot_r, q]
                acc[pl.ds(off, rows)] = total

    copies, places = [], []
    for k, (acc, gather, plan) in enumerate(zip(accs, gathers, plans)):
        if plan["h"] == 0:
            continue
        bits = [rounds[r][0] for r in range(plan["h"])]
        halves = [half for step, keep, give, half in plan["kept"]]
        own, members = group_members(bits)
        rows, off = plan["rows"], plan["off"]
        for t, slot, device, flips, flip_list in members:
            copies.append((
                remote(acc.at[pl.ds(off, rows)], gather.at[own], gather_sem.at[t, 0, k], gather_sem.at[own, 1, k], device),
                remote(acc.at[pl.ds(off, rows)], gather.at[slot], gather_sem.at[t, 0, k], gather_sem.at[slot, 1, k], device)))
            where = 0
            for idx, (axis, bit) in enumerate(bits):
                flip = 1 if (axis, bit) in flips else 0
                where = where + ((bit_of(axis, bit) + flip) % 2) * halves[idx]
            places.append((acc, gather, slot, pl.multiple_of(where, 8), rows))
    for send, recv in copies:
        send.start()
    for send, recv in copies:
        send.wait_send()
    for send, recv in copies:
        recv.wait_recv()
    for acc, gather, slot, where, rows in places:
        acc[pl.ds(where, rows)] = gather[slot]
    t1_ref[...] = o1_ref[...].T
    t2_ref[...] = o2_ref[...].T


def allreduce(g1, g2, axis_order, axis_sizes):
    rounds = exchange_rounds(axis_sizes)
    n = len(rounds)
    width = max(2 ** len(group) for group in rounds)
    vmem = pltpu.VMEM
    chunk = [g.shape[0] // 2 ** halvings(g.shape[0], rounds) for g in (g1, g2)]
    gwidth = max(2 ** halvings(g.shape[0], rounds) for g in (g1, g2))
    return pl.pallas_call(
        functools.partial(allreduce_kernel, axis_order, rounds),
        out_shape=(jax.ShapeDtypeStruct(g1.shape[::-1], g1.dtype), jax.ShapeDtypeStruct(g2.shape[::-1], g2.dtype)),
        in_specs=[pl.BlockSpec(memory_space=vmem)] * 2,
        out_specs=[pl.BlockSpec(memory_space=vmem)] * 2,
        scratch_shapes=[
            vmem(g1.shape, g1.dtype),
            vmem(g2.shape, g2.dtype),
            vmem((n, g1.shape[0] // 2) + g1.shape[1:], g1.dtype),
            vmem((n, g2.shape[0] // 2) + g2.shape[1:], g2.dtype),
            vmem((gwidth, chunk[0]) + g1.shape[1:], g1.dtype),
            vmem((gwidth, chunk[1]) + g2.shape[1:], g2.dtype),
            vmem((n, width, chunk[0]) + g1.shape[1:], g1.dtype),
            vmem((n, width, chunk[1]) + g2.shape[1:], g2.dtype),
            pltpu.SemaphoreType.DMA((n, width, 2)),
            pltpu.SemaphoreType.DMA((n, width, 2)),
            pltpu.SemaphoreType.DMA((gwidth, 2, 2)),
        ],
        compiler_params=pltpu.CompilerParams(collective_id=0, has_side_effects=True),
    )(g1, g2)


def body(axis_order, axis_sizes, crops, first_kernel, second_kernel, out_grad):
    local_samples, channels_in, planes, flat_cells = crops.shape
    whole_input = lax.all_to_all(crops, "space", split_axis=0, concat_axis=2, tiled=True)
    x = whole_input[0].transpose(1, 0, 2)
    c1, c2 = first_kernel.shape[0], second_kernel.shape[0]
    og = out_grad[0]
    ogn = og.reshape(c2, -1)
    ogq = og.transpose(1, 0, 2).reshape(-1, og.shape[2])
    w1 = first_kernel.transpose(0, 2, 3, 4, 1).reshape(c1, -1)
    w2 = second_kernel.transpose(0, 2, 3, 4, 1).reshape(c2, -1)
    w2t = second_kernel.transpose(2, 1, 3, 4, 0).reshape(3, c1, -1)
    t1, sel2, up = selection_tables(WIDTH, HEIGHT // 2, WIDTH // 2)
    act = act_grad_of(ogq, w2t, jnp.asarray(up, jnp.bfloat16))
    feat, fg, sg = per_sample(x, ogn, act, w1, w2, jnp.asarray(t1, jnp.bfloat16), jnp.asarray(sel2, jnp.bfloat16))
    features_out = feat.reshape(out_grad.shape)
    fg, sg = allreduce(fg, sg, axis_order, axis_sizes)
    first_grad = fg.reshape(3, 3, 3, channels_in, c1).transpose(4, 3, 0, 1, 2)
    second_grad = sg.reshape(3, 3, 3, c1, c2).transpose(4, 3, 0, 1, 2)
    return (features_out, first_grad, second_grad)


def solution(mesh):
    placed = (P("sample", None, "space", None), P(), P(), P(("sample", "space"), None, None, None))
    axis_order = tuple(mesh.axis_names)
    axis_sizes = [(a, mesh.shape[a]) for a in ("sample", "space")]
    return jax.shard_map(
        functools.partial(body, axis_order, axis_sizes),
        mesh=mesh,
        in_specs=placed,
        out_specs=(P(("sample", "space"), None, None, None), P(), P()),
        check_vma=False,
    )
```

```python
import functools

import numpy as np

import jax
import jax.numpy as jnp
from jax import lax
from jax.experimental import pallas as pl
from jax.experimental.pallas import tpu as pltpu
from jax.sharding import PartitionSpec as P

HEIGHT = 8
WIDTH = 128

NT = (((1,), (1,)), ((), ()))


def selection_tables(c0_w, c1_h, c1_w):
    t1 = np.zeros((c0_w, 3 * 128), np.float32)
    for c in range(3):
        for pw in range(c0_w // 2):
            w = 2 * pw + c - 1
            if 0 <= w < c0_w:
                t1[w, c * 128 + pw] = 1.0
    q_h, q_w = c1_h // 2, c1_w // 2
    sel2 = np.zeros((c1_h * c1_w, 9 * 128), np.float32)
    up = np.zeros((q_h * q_w, 9 * c1_h * c1_w), np.float32)
    for b in range(3):
        for c in range(3):
            bc = b * 3 + c
            for qh in range(q_h):
                for qw in range(q_w):
                    h2, w2 = 2 * qh + b - 1, 2 * qw + c - 1
                    if 0 <= h2 < c1_h and 0 <= w2 < c1_w:
                        sel2[h2 * c1_w + w2, bc * 128 + qh * q_w + qw] = 1.0
                        up[qh * q_w + qw, bc * c1_h * c1_w + h2 * c1_w + w2] = 1.0
    return t1, sel2, up


def act_kernel(ogq_ref, w2t_ref, up_ref, act_ref, v_ref):
    planes2 = v_ref.shape[0] - 1
    c2 = v_ref.shape[2]
    span = up_ref.shape[1] // 9
    v_ref[planes2] = jnp.zeros(v_ref.shape[1:], v_ref.dtype)
    for bc in range(9):
        u = jnp.dot(ogq_ref[...], up_ref[:, bc * span:(bc + 1) * span], preferred_element_type=jnp.float32)
        v_ref[pl.ds(0, planes2), bc] = u.astype(v_ref.dtype).reshape(planes2, c2, span)

    def plane(q, carry):
        vq = v_ref[q].reshape(9 * c2, span)
        vq1 = v_ref[q + 1].reshape(9 * c2, span)
        even = jnp.dot(w2t_ref[1], vq, preferred_element_type=jnp.float32)
        odd = (jnp.dot(w2t_ref[2], vq, preferred_element_type=jnp.float32)
               + jnp.dot(w2t_ref[0], vq1, preferred_element_type=jnp.float32))
        act_ref[2 * q] = even.astype(act_ref.dtype)
        act_ref[2 * q + 1] = odd.astype(act_ref.dtype)
        return carry

    lax.fori_loop(0, planes2, plane, 0)


def act_grad_of(ogq, w2t, up):
    c2 = w2t.shape[2] // 9
    planes2 = ogq.shape[0] // c2
    c1 = w2t.shape[1]
    span = up.shape[1] // 9
    vmem = pltpu.VMEM
    flops = 2 * ogq.shape[0] * ogq.shape[1] * up.shape[1] + 2 * 3 * 2 * planes2 * c1 * 9 * c2 * span
    return pl.pallas_call(
        act_kernel,
        out_shape=jax.ShapeDtypeStruct((2 * planes2, c1, span), jnp.bfloat16),
        in_specs=[pl.BlockSpec(memory_space=vmem)] * 3,
        out_specs=pl.BlockSpec(memory_space=vmem),
        scratch_shapes=[vmem((planes2 + 1, 9, c2, span), jnp.bfloat16)],
        compiler_params=pltpu.CompilerParams(vmem_limit_bytes=32 * 1024 * 1024),
        cost_estimate=pl.CostEstimate(flops=flops, transcendentals=0,
                                      bytes_accessed=2 * (ogq.size + w2t.size + up.size + 2 * planes2 * c1 * span)),
    )(ogq, w2t, up)


def conv_kernel(x_ref, ogn_ref, act_ref, w1_ref, w2_ref, t1_ref, sel2_ref,
                feat_ref, fg_ref, sg_ref,
                q1_ref, s_ref, fp_ref, a2_ref, q2_ref, s2_ref):
    depth, c0, cells = x_ref.shape
    n_h = cells // 128
    c1 = w1_ref.shape[0]
    c2 = w2_ref.shape[0]
    planes1 = depth // 2
    plane1 = s_ref.shape[2]
    planes2 = planes1 // 2

    q1_ref[0] = jnp.zeros(q1_ref.shape[1:], q1_ref.dtype)
    for h in range(n_h):
        xh = x_ref[:, :, h * 128:(h + 1) * 128].reshape(depth * c0, 128)
        qh = jnp.dot(xh, t1_ref[...], preferred_element_type=jnp.float32)
        q1_ref[pl.ds(1, depth), :, h * 384:(h + 1) * 384] = qh.astype(q1_ref.dtype).reshape(depth, c0, 384)

    a2_ref[0] = jnp.zeros(a2_ref.shape[1:], a2_ref.dtype)

    def build_plane(pd, carry):
        for a in range(3):
            for b in range(3):
                for c in range(3):
                    r0 = ((a * 3 + b) * 3 + c) * c0
                    for m in range(plane1 // 128):
                        h_lo, h_hi = 4 * m + b - 1, 4 * m + b + 1
                        hi = q1_ref[2 * pd + a, :, pl.ds((h_hi * 3 + c) * 128, 128)].astype(jnp.float32)
                        val = pltpu.roll(hi, 64, 1)
                        if h_lo >= 0:
                            val = val + q1_ref[2 * pd + a, :, pl.ds((h_lo * 3 + c) * 128, 128)].astype(jnp.float32)
                        s_ref[pd, pl.ds(r0, c0), pl.ds(m * 128, 128)] = val.astype(s_ref.dtype)
        pre = jnp.dot(w1_ref[...], s_ref[pd], preferred_element_type=jnp.float32)
        sig = 1.0 / (1.0 + jnp.exp(-pre))
        fp_ref[pd] = sig * (1.0 + pre * (1.0 - sig))
        a2_ref[pd + 1] = (pre * sig).astype(a2_ref.dtype)
        return carry

    lax.fori_loop(0, planes1, build_plane, 0, unroll=8)

    a2 = a2_ref[...].reshape((planes1 + 1) * c1, plane1)
    q2 = jnp.dot(a2, sel2_ref[...], preferred_element_type=jnp.float32)
    q2_ref[...] = q2.reshape(planes1 + 1, c1, 9 * 128)

    sg_ref[...] = jnp.zeros(sg_ref.shape, sg_ref.dtype)
    for n in range(planes2 // 2):
        for a in range(3):
            for bc in range(9):
                r0 = (a * 9 + bc) * c1
                lo = q2_ref[4 * n + a, :, bc * 128:(bc + 1) * 128]
                hi = q2_ref[4 * n + a + 2, :, bc * 128:(bc + 1) * 128]
                s2_ref[n, r0:r0 + c1, :] = (lo + pltpu.roll(hi, 64, 1)).astype(s2_ref.dtype)
        feat = jnp.dot(w2_ref[...], s2_ref[n], preferred_element_type=jnp.float32)
        half = feat_ref.shape[2]
        feat_ref[:, 2 * n, :] = feat[:, :half].astype(feat_ref.dtype)
        feat_ref[:, 2 * n + 1, :] = feat[:, half:].astype(feat_ref.dtype)
        sg_ref[...] += lax.dot_general(ogn_ref[:, n * 128:(n + 1) * 128], s2_ref[n], NT,
                                       preferred_element_type=jnp.float32)

    fg_ref[...] = jnp.zeros(fg_ref.shape, fg_ref.dtype)

    def back_plane(d2, carry):
        slope = fp_ref[d2]
        pg = (act_ref[d2].astype(jnp.float32) * slope).astype(jnp.bfloat16)
        fg_ref[...] += lax.dot_general(pg, s_ref[d2], NT, preferred_element_type=jnp.float32)
        return carry

    lax.fori_loop(0, planes1, back_plane, 0, unroll=16)


def per_sample(x, ogn, act, w1, w2, t1, sel2):
    depth, c0, cells = x.shape
    c1, c2 = w1.shape[0], w2.shape[0]
    planes1, planes2 = depth // 2, depth // 4
    plane1 = (HEIGHT // 2) * (WIDTH // 2)
    plane2 = ogn.shape[1] // planes2
    vmem = pltpu.VMEM
    return pl.pallas_call(
        conv_kernel,
        out_shape=(
            jax.ShapeDtypeStruct((c2, planes2, plane2), jnp.bfloat16),
            jax.ShapeDtypeStruct((c1, 27 * c0), jnp.float32),
            jax.ShapeDtypeStruct((c2, 27 * c1), jnp.float32),
        ),
        in_specs=[pl.BlockSpec(memory_space=vmem)] * 7,
        out_specs=[pl.BlockSpec(memory_space=vmem)] * 3,
        scratch_shapes=[
            vmem((depth + 1, c0, (cells // 128) * 384), jnp.bfloat16),
            vmem((planes1, 27 * c0, plane1), jnp.bfloat16),
            vmem((planes1, c1, plane1), jnp.float32),
            vmem((planes1 + 1, c1, plane1), jnp.bfloat16),
            vmem((planes1 + 1, c1, 9 * 128), jnp.float32),
            vmem((planes2 // 2, 27 * c1, 128), jnp.bfloat16),
        ],
        compiler_params=pltpu.CompilerParams(vmem_limit_bytes=60 * 1024 * 1024),
    )(x, ogn, act, w1, w2, t1, sel2)


ROUND_ORDER = ((("sample", 1),), (("space", 4),), (("sample", 2),),
               (("space", 1), ("space", 2), ("sample", 4)), (("space", 8), ("space", 16)))


def exchange_rounds(axis_sizes):
    sizes = dict(axis_sizes)
    rounds = []
    for group in ROUND_ORDER:
        kept = tuple((axis, bit) for axis, bit in group if bit < sizes[axis])
        if kept:
            rounds.append(kept)
    used = {pair for group in rounds for pair in group}
    for axis, size in axis_sizes:
        bit = 1
        while bit < size:
            if (axis, bit) not in used:
                rounds.append(((axis, bit),))
            bit *= 2
    return rounds


def halvings(rows, rounds):
    count = 0
    while (count < len(rounds) and len(rounds[count]) == 1
           and rows % (2 ** (count + 1) * 8) == 0):
        count += 1
    return count


def allreduce_kernel(axis_order, rounds, g1_ref, g2_ref, t1_ref, t2_ref, o1_ref, o2_ref, r1_ref, r2_ref,
                     a1_ref, a2_ref, x1_ref, x2_ref, send_sem, recv_sem, gather_sem):
    me = {axis: lax.axis_index(axis) for axis in axis_order}

    def bit_of(axis, bit):
        return (me[axis] // bit) % 2

    plan_rounds = []
    for group in rounds:
        own = sum(bit_of(axis, bit) * 2 ** idx for idx, (axis, bit) in enumerate(group))
        members = []
        for t in range(1, 2 ** len(group)):
            there = dict(me)
            slot = 0
            for idx, (axis, bit) in enumerate(group):
                flip = (t // 2 ** idx) % 2
                if flip:
                    there[axis] = there[axis] + bit - 2 * bit * bit_of(axis, bit)
                slot = slot + ((bit_of(axis, bit) + flip) % 2) * 2 ** idx
            members.append((t, slot, tuple(there[a] for a in axis_order)))
        plan_rounds.append((group, own, members))

    def group_members(group):
        own = sum(bit_of(axis, bit) * 2 ** idx for idx, (axis, bit) in enumerate(group))
        members = []
        for t in range(1, 2 ** len(group)):
            there = dict(me)
            slot = 0
            flips = []
            for idx, (axis, bit) in enumerate(group):
                flip = (t // 2 ** idx) % 2
                if flip:
                    there[axis] = there[axis] + bit - 2 * bit * bit_of(axis, bit)
                    flips.append((axis, bit))
                slot = slot + ((bit_of(axis, bit) + flip) % 2) * 2 ** idx
            members.append((t, slot, tuple(there[a] for a in axis_order), frozenset(flips), flips))
        return own, members

    halving_bits = [rounds[r][0] for r in range(max(halvings(acc.shape[0], rounds) for acc in (o1_ref, o2_ref)))]
    seen = {}
    for group, own, members in plan_rounds:
        for t, slot, device in members:
            flips = frozenset((axis, bit) for idx, (axis, bit) in enumerate(group) if (t // 2 ** idx) % 2)
            seen[flips] = device
    for t, slot, device, flips, _ in group_members(halving_bits)[1]:
        seen[flips] = device
    barrier = pltpu.get_barrier_semaphore()
    for device in seen.values():
        pl.semaphore_signal(barrier, 1, device_id=device, device_id_type=pl.DeviceIdType.MESH)
    pl.semaphore_wait(barrier, len(seen))

    accs = (o1_ref, o2_ref)
    recvs = (r1_ref, r2_ref)
    gathers = (a1_ref, a2_ref)
    groups = (x1_ref, x2_ref)
    o1_ref[...] = g1_ref[...]
    o2_ref[...] = g2_ref[...]
    plans = [{"rows": acc.shape[0], "h": halvings(acc.shape[0], rounds), "off": 0, "kept": []} for acc in accs]

    def remote(src, dst, send, recv, device):
        return pltpu.make_async_remote_copy(
            src_ref=src, dst_ref=dst, send_sem=send, recv_sem=recv,
            device_id=device, device_id_type=pl.DeviceIdType.MESH)

    for r, (group, own, members) in enumerate(plan_rounds):
        sends, recvs_wait, after = [], [], []
        for k, (acc, recv, xbuf, plan) in enumerate(zip(accs, recvs, groups, plans)):
            if r < plan["h"]:
                (axis, bit), = group
                t, slot, device = members[0]
                mine = bit_of(axis, bit)
                half = plan["rows"] // 2
                keep = pl.multiple_of(plan["off"] + mine * half, 8)
                give = pl.multiple_of(plan["off"] + (1 - mine) * half, 8)
                copy = remote(acc.at[pl.ds(give, half)], recv.at[r, pl.ds(0, half)],
                              send_sem.at[r, 0, k], recv_sem.at[r, 0, k], device)
                sends.append(copy)
                recvs_wait.append(copy)
                after.append(("add", acc, recv, r, keep, half))
                plan["kept"].append((r, keep, give, half))
                plan["off"], plan["rows"] = keep, half
            else:
                rows, off = plan["rows"], plan["off"]
                xbuf[r, own] = acc[pl.ds(off, rows)]
                for t, slot, device in members:
                    sends.append(remote(acc.at[pl.ds(off, rows)], xbuf.at[r, own],
                                        send_sem.at[r, t, k], recv_sem.at[r, own, k], device))
                    recvs_wait.append(remote(acc.at[pl.ds(off, rows)], xbuf.at[r, slot],
                                             send_sem.at[r, t, k], recv_sem.at[r, slot, k], device))
                after.append(("sum", acc, xbuf, r, off, rows, 2 ** len(group)))
        for copy in sends:
            copy.start()
        for copy in sends:
            copy.wait_send()
        for copy in recvs_wait:
            copy.wait_recv()
        for item in after:
            if item[0] == "add":
                _, acc, recv, slot_r, off, rows = item
                acc[pl.ds(off, rows)] = acc[pl.ds(off, rows)] + recv[slot_r, pl.ds(0, rows)]
            else:
                _, acc, xbuf, slot_r, off, rows, n_members = item
                total = xbuf[slot_r, 0]
                for q in range(1, n_members):
                    total = total + xbuf[slot_r, q]
                acc[pl.ds(off, rows)] = total

    copies, places = [], []
    for k, (acc, gather, plan) in enumerate(zip(accs, gathers, plans)):
        if plan["h"] == 0:
            continue
        bits = [rounds[r][0] for r in range(plan["h"])]
        halves = [half for step, keep, give, half in plan["kept"]]
        own, members = group_members(bits)
        rows, off = plan["rows"], plan["off"]
        for t, slot, device, flips, flip_list in members:
            copies.append((
                remote(acc.at[pl.ds(off, rows)], gather.at[own], gather_sem.at[t, 0, k], gather_sem.at[own, 1, k], device),
                remote(acc.at[pl.ds(off, rows)], gather.at[slot], gather_sem.at[t, 0, k], gather_sem.at[slot, 1, k], device)))
            where = 0
            for idx, (axis, bit) in enumerate(bits):
                flip = 1 if (axis, bit) in flips else 0
                where = where + ((bit_of(axis, bit) + flip) % 2) * halves[idx]
            places.append((acc, gather, slot, pl.multiple_of(where, 8), rows))
    for send, recv in copies:
        send.start()
    for send, recv in copies:
        send.wait_send()
    for send, recv in copies:
        recv.wait_recv()
    for acc, gather, slot, where, rows in places:
        acc[pl.ds(where, rows)] = gather[slot]
    t1_ref[...] = o1_ref[...].T
    t2_ref[...] = o2_ref[...].T


def allreduce(g1, g2, axis_order, axis_sizes):
    rounds = exchange_rounds(axis_sizes)
    n = len(rounds)
    width = max(2 ** len(group) for group in rounds)
    vmem = pltpu.VMEM
    chunk = [g.shape[0] // 2 ** halvings(g.shape[0], rounds) for g in (g1, g2)]
    gwidth = max(2 ** halvings(g.shape[0], rounds) for g in (g1, g2))
    return pl.pallas_call(
        functools.partial(allreduce_kernel, axis_order, rounds),
        out_shape=(jax.ShapeDtypeStruct(g1.shape[::-1], g1.dtype), jax.ShapeDtypeStruct(g2.shape[::-1], g2.dtype)),
        in_specs=[pl.BlockSpec(memory_space=vmem)] * 2,
        out_specs=[pl.BlockSpec(memory_space=vmem)] * 2,
        scratch_shapes=[
            vmem(g1.shape, g1.dtype),
            vmem(g2.shape, g2.dtype),
            vmem((n, g1.shape[0] // 2) + g1.shape[1:], g1.dtype),
            vmem((n, g2.shape[0] // 2) + g2.shape[1:], g2.dtype),
            vmem((gwidth, chunk[0]) + g1.shape[1:], g1.dtype),
            vmem((gwidth, chunk[1]) + g2.shape[1:], g2.dtype),
            vmem((n, width, chunk[0]) + g1.shape[1:], g1.dtype),
            vmem((n, width, chunk[1]) + g2.shape[1:], g2.dtype),
            pltpu.SemaphoreType.DMA((n, width, 2)),
            pltpu.SemaphoreType.DMA((n, width, 2)),
            pltpu.SemaphoreType.DMA((gwidth, 2, 2)),
        ],
        compiler_params=pltpu.CompilerParams(collective_id=0, has_side_effects=True),
    )(g1, g2)


def body(axis_order, axis_sizes, crops, first_kernel, second_kernel, out_grad):
    local_samples, channels_in, planes, flat_cells = crops.shape
    whole_input = lax.all_to_all(crops, "space", split_axis=0, concat_axis=2, tiled=True)
    x = whole_input[0].transpose(1, 0, 2)
    c1, c2 = first_kernel.shape[0], second_kernel.shape[0]
    og = out_grad[0]
    ogn = og.reshape(c2, -1)
    ogq = og.transpose(1, 0, 2).reshape(-1, og.shape[2])
    w1 = first_kernel.transpose(0, 2, 3, 4, 1).reshape(c1, -1)
    w2 = second_kernel.transpose(0, 2, 3, 4, 1).reshape(c2, -1)
    w2t = second_kernel.transpose(2, 1, 3, 4, 0).reshape(3, c1, -1)
    t1, sel2, up = selection_tables(WIDTH, HEIGHT // 2, WIDTH // 2)
    act = act_grad_of(ogq, w2t, jnp.asarray(up, jnp.bfloat16))
    feat, fg, sg = per_sample(x, ogn, act, w1, w2, jnp.asarray(t1, jnp.bfloat16), jnp.asarray(sel2, jnp.bfloat16))
    features_out = feat.reshape(out_grad.shape)
    fg, sg = allreduce(fg, sg, axis_order, axis_sizes)
    first_grad = fg.reshape(3, 3, 3, channels_in, c1).transpose(4, 3, 0, 1, 2)
    second_grad = sg.reshape(3, 3, 3, c1, c2).transpose(4, 3, 0, 1, 2)
    return (features_out, first_grad, second_grad)


def solution(mesh):
    placed = (P("sample", None, "space", None), P(), P(), P(("sample", "space"), None, None, None))
    axis_order = tuple(mesh.axis_names)
    axis_sizes = [(a, mesh.shape[a]) for a in ("sample", "space")]
    return jax.shard_map(
        functools.partial(body, axis_order, axis_sizes),
        mesh=mesh,
        in_specs=placed,
        out_specs=(P(("sample", "space"), None, None, None), P(), P()),
        check_vma=False,
    )
```

```python
import functools

import numpy as np

import jax
import jax.numpy as jnp
from jax import lax
from jax.experimental import pallas as pl
from jax.experimental.pallas import tpu as pltpu
from jax.sharding import PartitionSpec as P

HEIGHT = 8
WIDTH = 128

NT = (((1,), (1,)), ((), ()))


def selection_tables(c0_w, c1_h, c1_w):
    t1 = np.zeros((c0_w, 3 * 128), np.float32)
    for c in range(3):
        for pw in range(c0_w // 2):
            w = 2 * pw + c - 1
            if 0 <= w < c0_w:
                t1[w, c * 128 + pw] = 1.0
    q_h, q_w = c1_h // 2, c1_w // 2
    sel2 = np.zeros((c1_h * c1_w, 9 * 128), np.float32)
    up = np.zeros((q_h * q_w, 9 * c1_h * c1_w), np.float32)
    for b in range(3):
        for c in range(3):
            bc = b * 3 + c
            for qh in range(q_h):
                for qw in range(q_w):
                    h2, w2 = 2 * qh + b - 1, 2 * qw + c - 1
                    if 0 <= h2 < c1_h and 0 <= w2 < c1_w:
                        sel2[h2 * c1_w + w2, bc * 128 + qh * q_w + qw] = 1.0
                        up[qh * q_w + qw, bc * c1_h * c1_w + h2 * c1_w + w2] = 1.0
    return t1, sel2, up


def act_kernel(ogq_ref, w2t_ref, up_ref, act_ref, v_ref):
    planes2 = v_ref.shape[0] - 1
    c2 = v_ref.shape[2]
    span = up_ref.shape[1] // 9
    v_ref[planes2] = jnp.zeros(v_ref.shape[1:], v_ref.dtype)
    for bc in range(9):
        u = jnp.dot(ogq_ref[...], up_ref[:, bc * span:(bc + 1) * span], preferred_element_type=jnp.float32)
        v_ref[pl.ds(0, planes2), bc] = u.astype(v_ref.dtype).reshape(planes2, c2, span)

    def plane(q, carry):
        vq = v_ref[q].reshape(9 * c2, span)
        vq1 = v_ref[q + 1].reshape(9 * c2, span)
        even = jnp.dot(w2t_ref[1], vq, preferred_element_type=jnp.float32)
        odd = (jnp.dot(w2t_ref[2], vq, preferred_element_type=jnp.float32)
               + jnp.dot(w2t_ref[0], vq1, preferred_element_type=jnp.float32))
        act_ref[2 * q] = even.astype(act_ref.dtype)
        act_ref[2 * q + 1] = odd.astype(act_ref.dtype)
        return carry

    lax.fori_loop(0, planes2, plane, 0)


def act_grad_of(ogq, w2t, up):
    c2 = w2t.shape[2] // 9
    planes2 = ogq.shape[0] // c2
    c1 = w2t.shape[1]
    span = up.shape[1] // 9
    vmem = pltpu.VMEM
    flops = 2 * ogq.shape[0] * ogq.shape[1] * up.shape[1] + 2 * 3 * 2 * planes2 * c1 * 9 * c2 * span
    return pl.pallas_call(
        act_kernel,
        out_shape=jax.ShapeDtypeStruct((2 * planes2, c1, span), jnp.bfloat16),
        in_specs=[pl.BlockSpec(memory_space=vmem)] * 3,
        out_specs=pl.BlockSpec(memory_space=vmem),
        scratch_shapes=[vmem((planes2 + 1, 9, c2, span), jnp.bfloat16)],
        compiler_params=pltpu.CompilerParams(vmem_limit_bytes=32 * 1024 * 1024),
        cost_estimate=pl.CostEstimate(flops=flops, transcendentals=0,
                                      bytes_accessed=2 * (ogq.size + w2t.size + up.size + 2 * planes2 * c1 * span)),
    )(ogq, w2t, up)


def conv_kernel(x_ref, ogn_ref, act_ref, w1_ref, w2_ref, t1_ref, sel2_ref,
                feat_ref, fg_ref, sg_ref,
                q1_ref, s_ref, fp_ref, a2_ref, q2_ref, s2_ref):
    depth, c0, cells = x_ref.shape
    n_h = cells // 128
    c1 = w1_ref.shape[0]
    c2 = w2_ref.shape[0]
    planes1 = depth // 2
    plane1 = s_ref.shape[2]
    planes2 = planes1 // 2

    q1_ref[0] = jnp.zeros(q1_ref.shape[1:], q1_ref.dtype)
    for h in range(n_h):
        xh = x_ref[:, :, h * 128:(h + 1) * 128].reshape(depth * c0, 128)
        qh = jnp.dot(xh, t1_ref[...], preferred_element_type=jnp.float32)
        q1_ref[pl.ds(1, depth), :, h * 384:(h + 1) * 384] = qh.astype(q1_ref.dtype).reshape(depth, c0, 384)

    a2_ref[0] = jnp.zeros(a2_ref.shape[1:], a2_ref.dtype)

    def build_plane(pd, carry):
        for a in range(3):
            for b in range(3):
                for c in range(3):
                    r0 = ((a * 3 + b) * 3 + c) * c0
                    for m in range(plane1 // 128):
                        h_lo, h_hi = 4 * m + b - 1, 4 * m + b + 1
                        hi = q1_ref[2 * pd + a, :, pl.ds((h_hi * 3 + c) * 128, 128)].astype(jnp.float32)
                        val = pltpu.roll(hi, 64, 1)
                        if h_lo >= 0:
                            val = val + q1_ref[2 * pd + a, :, pl.ds((h_lo * 3 + c) * 128, 128)].astype(jnp.float32)
                        s_ref[pd, pl.ds(r0, c0), pl.ds(m * 128, 128)] = val.astype(s_ref.dtype)
        pre = jnp.dot(w1_ref[...], s_ref[pd], preferred_element_type=jnp.float32)
        sig = 1.0 / (1.0 + jnp.exp(-pre))
        fp_ref[pd] = sig * (1.0 + pre * (1.0 - sig))
        a2_ref[pd + 1] = (pre * sig).astype(a2_ref.dtype)
        return carry

    lax.fori_loop(0, planes1, build_plane, 0, unroll=32)

    a2 = a2_ref[...].reshape((planes1 + 1) * c1, plane1)
    q2 = jnp.dot(a2, sel2_ref[...], preferred_element_type=jnp.float32)
    q2_ref[...] = q2.reshape(planes1 + 1, c1, 9 * 128)

    sg_ref[...] = jnp.zeros(sg_ref.shape, sg_ref.dtype)
    for n in range(planes2 // 2):
        for a in range(3):
            for bc in range(9):
                r0 = (a * 9 + bc) * c1
                lo = q2_ref[4 * n + a, :, bc * 128:(bc + 1) * 128]
                hi = q2_ref[4 * n + a + 2, :, bc * 128:(bc + 1) * 128]
                s2_ref[n, r0:r0 + c1, :] = (lo + pltpu.roll(hi, 64, 1)).astype(s2_ref.dtype)
        feat = jnp.dot(w2_ref[...], s2_ref[n], preferred_element_type=jnp.float32)
        half = feat_ref.shape[2]
        feat_ref[:, 2 * n, :] = feat[:, :half].astype(feat_ref.dtype)
        feat_ref[:, 2 * n + 1, :] = feat[:, half:].astype(feat_ref.dtype)
        sg_ref[...] += lax.dot_general(ogn_ref[:, n * 128:(n + 1) * 128], s2_ref[n], NT,
                                       preferred_element_type=jnp.float32)

    fg_ref[...] = jnp.zeros(fg_ref.shape, fg_ref.dtype)

    def back_plane(d2, carry):
        slope = fp_ref[d2]
        pg = (act_ref[d2].astype(jnp.float32) * slope).astype(jnp.bfloat16)
        fg_ref[...] += lax.dot_general(pg, s_ref[d2], NT, preferred_element_type=jnp.float32)
        return carry

    lax.fori_loop(0, planes1, back_plane, 0, unroll=32)


def per_sample(x, ogn, act, w1, w2, t1, sel2):
    depth, c0, cells = x.shape
    c1, c2 = w1.shape[0], w2.shape[0]
    planes1, planes2 = depth // 2, depth // 4
    plane1 = (HEIGHT // 2) * (WIDTH // 2)
    plane2 = ogn.shape[1] // planes2
    vmem = pltpu.VMEM
    return pl.pallas_call(
        conv_kernel,
        out_shape=(
            jax.ShapeDtypeStruct((c2, planes2, plane2), jnp.bfloat16),
            jax.ShapeDtypeStruct((c1, 27 * c0), jnp.float32),
            jax.ShapeDtypeStruct((c2, 27 * c1), jnp.float32),
        ),
        in_specs=[pl.BlockSpec(memory_space=vmem)] * 7,
        out_specs=[pl.BlockSpec(memory_space=vmem)] * 3,
        scratch_shapes=[
            vmem((depth + 1, c0, (cells // 128) * 384), jnp.bfloat16),
            vmem((planes1, 27 * c0, plane1), jnp.bfloat16),
            vmem((planes1, c1, plane1), jnp.float32),
            vmem((planes1 + 1, c1, plane1), jnp.bfloat16),
            vmem((planes1 + 1, c1, 9 * 128), jnp.float32),
            vmem((planes2 // 2, 27 * c1, 128), jnp.bfloat16),
        ],
        compiler_params=pltpu.CompilerParams(vmem_limit_bytes=60 * 1024 * 1024),
    )(x, ogn, act, w1, w2, t1, sel2)


ROUND_ORDER = ((("sample", 1),), (("space", 4),), (("sample", 2),),
               (("space", 1), ("space", 2), ("sample", 4)), (("space", 8), ("space", 16)))


def exchange_rounds(axis_sizes):
    sizes = dict(axis_sizes)
    rounds = []
    for group in ROUND_ORDER:
        kept = tuple((axis, bit) for axis, bit in group if bit < sizes[axis])
        if kept:
            rounds.append(kept)
    used = {pair for group in rounds for pair in group}
    for axis, size in axis_sizes:
        bit = 1
        while bit < size:
            if (axis, bit) not in used:
                rounds.append(((axis, bit),))
            bit *= 2
    return rounds


def halvings(rows, rounds):
    count = 0
    while (count < len(rounds) and len(rounds[count]) == 1
           and rows % (2 ** (count + 1) * 8) == 0):
        count += 1
    return count


def allreduce_kernel(axis_order, rounds, g1_ref, g2_ref, t1_ref, t2_ref, o1_ref, o2_ref, r1_ref, r2_ref,
                     a1_ref, a2_ref, x1_ref, x2_ref, send_sem, recv_sem, gather_sem):
    me = {axis: lax.axis_index(axis) for axis in axis_order}

    def bit_of(axis, bit):
        return (me[axis] // bit) % 2

    plan_rounds = []
    for group in rounds:
        own = sum(bit_of(axis, bit) * 2 ** idx for idx, (axis, bit) in enumerate(group))
        members = []
        for t in range(1, 2 ** len(group)):
            there = dict(me)
            slot = 0
            for idx, (axis, bit) in enumerate(group):
                flip = (t // 2 ** idx) % 2
                if flip:
                    there[axis] = there[axis] + bit - 2 * bit * bit_of(axis, bit)
                slot = slot + ((bit_of(axis, bit) + flip) % 2) * 2 ** idx
            members.append((t, slot, tuple(there[a] for a in axis_order)))
        plan_rounds.append((group, own, members))

    def group_members(group):
        own = sum(bit_of(axis, bit) * 2 ** idx for idx, (axis, bit) in enumerate(group))
        members = []
        for t in range(1, 2 ** len(group)):
            there = dict(me)
            slot = 0
            flips = []
            for idx, (axis, bit) in enumerate(group):
                flip = (t // 2 ** idx) % 2
                if flip:
                    there[axis] = there[axis] + bit - 2 * bit * bit_of(axis, bit)
                    flips.append((axis, bit))
                slot = slot + ((bit_of(axis, bit) + flip) % 2) * 2 ** idx
            members.append((t, slot, tuple(there[a] for a in axis_order), frozenset(flips), flips))
        return own, members

    halving_bits = [rounds[r][0] for r in range(max(halvings(acc.shape[0], rounds) for acc in (o1_ref, o2_ref)))]
    seen = {}
    for group, own, members in plan_rounds:
        for t, slot, device in members:
            flips = frozenset((axis, bit) for idx, (axis, bit) in enumerate(group) if (t // 2 ** idx) % 2)
            seen[flips] = device
    for t, slot, device, flips, _ in group_members(halving_bits)[1]:
        seen[flips] = device
    barrier = pltpu.get_barrier_semaphore()
    for device in seen.values():
        pl.semaphore_signal(barrier, 1, device_id=device, device_id_type=pl.DeviceIdType.MESH)
    pl.semaphore_wait(barrier, len(seen))

    accs = (o1_ref, o2_ref)
    recvs = (r1_ref, r2_ref)
    gathers = (a1_ref, a2_ref)
    groups = (x1_ref, x2_ref)
    o1_ref[...] = g1_ref[...]
    o2_ref[...] = g2_ref[...]
    plans = [{"rows": acc.shape[0], "h": halvings(acc.shape[0], rounds), "off": 0, "kept": []} for acc in accs]

    def remote(src, dst, send, recv, device):
        return pltpu.make_async_remote_copy(
            src_ref=src, dst_ref=dst, send_sem=send, recv_sem=recv,
            device_id=device, device_id_type=pl.DeviceIdType.MESH)

    for r, (group, own, members) in enumerate(plan_rounds):
        sends, recvs_wait, after = [], [], []
        for k, (acc, recv, xbuf, plan) in enumerate(zip(accs, recvs, groups, plans)):
            if r < plan["h"]:
                (axis, bit), = group
                t, slot, device = members[0]
                mine = bit_of(axis, bit)
                half = plan["rows"] // 2
                keep = pl.multiple_of(plan["off"] + mine * half, 8)
                give = pl.multiple_of(plan["off"] + (1 - mine) * half, 8)
                copy = remote(acc.at[pl.ds(give, half)], recv.at[r, pl.ds(0, half)],
                              send_sem.at[r, 0, k], recv_sem.at[r, 0, k], device)
                sends.append(copy)
                recvs_wait.append(copy)
                after.append(("add", acc, recv, r, keep, half))
                plan["kept"].append((r, keep, give, half))
                plan["off"], plan["rows"] = keep, half
            else:
                rows, off = plan["rows"], plan["off"]
                xbuf[r, own] = acc[pl.ds(off, rows)]
                for t, slot, device in members:
                    sends.append(remote(acc.at[pl.ds(off, rows)], xbuf.at[r, own],
                                        send_sem.at[r, t, k], recv_sem.at[r, own, k], device))
                    recvs_wait.append(remote(acc.at[pl.ds(off, rows)], xbuf.at[r, slot],
                                             send_sem.at[r, t, k], recv_sem.at[r, slot, k], device))
                after.append(("sum", acc, xbuf, r, off, rows, 2 ** len(group)))
        for copy in sends:
            copy.start()
        for copy in sends:
            copy.wait_send()
        for copy in recvs_wait:
            copy.wait_recv()
        for item in after:
            if item[0] == "add":
                _, acc, recv, slot_r, off, rows = item
                acc[pl.ds(off, rows)] = acc[pl.ds(off, rows)] + recv[slot_r, pl.ds(0, rows)]
            else:
                _, acc, xbuf, slot_r, off, rows, n_members = item
                total = xbuf[slot_r, 0]
                for q in range(1, n_members):
                    total = total + xbuf[slot_r, q]
                acc[pl.ds(off, rows)] = total

    copies, places = [], []
    for k, (acc, gather, plan) in enumerate(zip(accs, gathers, plans)):
        if plan["h"] == 0:
            continue
        bits = [rounds[r][0] for r in range(plan["h"])]
        halves = [half for step, keep, give, half in plan["kept"]]
        own, members = group_members(bits)
        rows, off = plan["rows"], plan["off"]
        for t, slot, device, flips, flip_list in members:
            copies.append((
                remote(acc.at[pl.ds(off, rows)], gather.at[own], gather_sem.at[t, 0, k], gather_sem.at[own, 1, k], device),
                remote(acc.at[pl.ds(off, rows)], gather.at[slot], gather_sem.at[t, 0, k], gather_sem.at[slot, 1, k], device)))
            where = 0
            for idx, (axis, bit) in enumerate(bits):
                flip = 1 if (axis, bit) in flips else 0
                where = where + ((bit_of(axis, bit) + flip) % 2) * halves[idx]
            places.append((acc, gather, slot, pl.multiple_of(where, 8), rows))
    for send, recv in copies:
        send.start()
    for send, recv in copies:
        send.wait_send()
    for send, recv in copies:
        recv.wait_recv()
    for acc, gather, slot, where, rows in places:
        acc[pl.ds(where, rows)] = gather[slot]
    t1_ref[...] = o1_ref[...].T
    t2_ref[...] = o2_ref[...].T


def allreduce(g1, g2, axis_order, axis_sizes):
    rounds = exchange_rounds(axis_sizes)
    n = len(rounds)
    width = max(2 ** len(group) for group in rounds)
    vmem = pltpu.VMEM
    chunk = [g.shape[0] // 2 ** halvings(g.shape[0], rounds) for g in (g1, g2)]
    gwidth = max(2 ** halvings(g.shape[0], rounds) for g in (g1, g2))
    return pl.pallas_call(
        functools.partial(allreduce_kernel, axis_order, rounds),
        out_shape=(jax.ShapeDtypeStruct(g1.shape[::-1], g1.dtype), jax.ShapeDtypeStruct(g2.shape[::-1], g2.dtype)),
        in_specs=[pl.BlockSpec(memory_space=vmem)] * 2,
        out_specs=[pl.BlockSpec(memory_space=vmem)] * 2,
        scratch_shapes=[
            vmem(g1.shape, g1.dtype),
            vmem(g2.shape, g2.dtype),
            vmem((n, g1.shape[0] // 2) + g1.shape[1:], g1.dtype),
            vmem((n, g2.shape[0] // 2) + g2.shape[1:], g2.dtype),
            vmem((gwidth, chunk[0]) + g1.shape[1:], g1.dtype),
            vmem((gwidth, chunk[1]) + g2.shape[1:], g2.dtype),
            vmem((n, width, chunk[0]) + g1.shape[1:], g1.dtype),
            vmem((n, width, chunk[1]) + g2.shape[1:], g2.dtype),
            pltpu.SemaphoreType.DMA((n, width, 2)),
            pltpu.SemaphoreType.DMA((n, width, 2)),
            pltpu.SemaphoreType.DMA((gwidth, 2, 2)),
        ],
        compiler_params=pltpu.CompilerParams(collective_id=0, has_side_effects=True),
    )(g1, g2)


def body(axis_order, axis_sizes, crops, first_kernel, second_kernel, out_grad):
    local_samples, channels_in, planes, flat_cells = crops.shape
    whole_input = lax.all_to_all(crops, "space", split_axis=0, concat_axis=2, tiled=True)
    x = whole_input[0].transpose(1, 0, 2)
    c1, c2 = first_kernel.shape[0], second_kernel.shape[0]
    og = out_grad[0]
    ogn = og.reshape(c2, -1)
    ogq = og.transpose(1, 0, 2).reshape(-1, og.shape[2])
    w1 = first_kernel.transpose(0, 2, 3, 4, 1).reshape(c1, -1)
    w2 = second_kernel.transpose(0, 2, 3, 4, 1).reshape(c2, -1)
    w2t = second_kernel.transpose(2, 1, 3, 4, 0).reshape(3, c1, -1)
    t1, sel2, up = selection_tables(WIDTH, HEIGHT // 2, WIDTH // 2)
    act = act_grad_of(ogq, w2t, jnp.asarray(up, jnp.bfloat16))
    feat, fg, sg = per_sample(x, ogn, act, w1, w2, jnp.asarray(t1, jnp.bfloat16), jnp.asarray(sel2, jnp.bfloat16))
    features_out = feat.reshape(out_grad.shape)
    fg, sg = allreduce(fg, sg, axis_order, axis_sizes)
    first_grad = fg.reshape(3, 3, 3, channels_in, c1).transpose(4, 3, 0, 1, 2)
    second_grad = sg.reshape(3, 3, 3, c1, c2).transpose(4, 3, 0, 1, 2)
    return (features_out, first_grad, second_grad)


def solution(mesh):
    placed = (P("sample", None, "space", None), P(), P(), P(("sample", "space"), None, None, None))
    axis_order = tuple(mesh.axis_names)
    axis_sizes = [(a, mesh.shape[a]) for a in ("sample", "space")]
    return jax.shard_map(
        functools.partial(body, axis_order, axis_sizes),
        mesh=mesh,
        in_specs=placed,
        out_specs=(P(("sample", "space"), None, None, None), P(), P()),
        check_vma=False,
    )
```
